128 devices in a mesh: band: 8 (over z_hi, y), lon: 16 (over z_lo, x, core).
Axes of the slice: x: 4, y: 4, z: 4 (z_hi: 2, z_lo: 2; z = z_hi * 2 + z_lo), core: 2. Of those that a mesh axis runs over, the one named last changes fastest.
Arguments:
- latent: bfloat16 [256, 2048, 256], P('band', 'lon'), may hold values from -6 to 6
- row_index: int32 [8, 16, 32], P('band', 'lon'), may hold values from 0 to 31
- interp_weights: bfloat16 [4096, 128, 128], P(('band', 'lon')), may hold values from -0.5 to 0.5
- observation_slot_index: int32 [4096, 128], P(('band', 'lon')), may hold values from 0 to 6
- counts: int32 [4096], P(('band', 'lon')), may hold values from 32 to 128
- targets: bfloat16 [4096, 128, 128], P(('band', 'lon')), may hold values from -6 to 6
- gain: float32 [256], replicated, may hold values from 0.5 to 1.5
- w_in: bfloat16 [256, 512], replicated, may hold values from -0.375 to 0.375
- w_out: bfloat16 [512, 256], replicated, may hold values from -0.25 to 0.25
- head: bfloat16 [256, 128], replicated, may hold values from -0.375 to 0.375
Outputs:
- grad_latent: float32 [256, 2048, 256], P('band', 'lon')
- grad_w_in: float32 [256, 512], replicated
- grad_w_out: float32 [512, 256], replicated
- grad_gain: float32 [256], replicated
- grad_head: float32 [256, 128], replicated
The draws below stay inside these ranges and needn't reach their ends.
All inputs are finite; a program needn't handle non-finite values.
Results may differ from the reference program's by a relative error of at most 0.007.
Values may be sent and summed in bfloat16 or wider, within the bound.
No kernel may reach another device: no remote copies, remote signals or barrier semaphores. Data moves between devices by JAX's collectives and lax.ppermute only.
A program may use at most 128 MiB of HBM per device.

```python
import math
import jax
import jax.numpy as jnp
from jax import lax

C = 256
HID = 512
NV = 128
LAT_DEV = 32
LON_DEV = 128
BLOCK_OBS_SLOTS = 128
BPP = 2
WINDOW_SLOTS = 7
LAT = 256
LONS = 2048
NB = 32
TOTAL_OBS_BLOCKS = 4096
N_BAND = 8
N_LON = 16
DEVICES = 128


def touch_ends(drawn, rng, least, largest):
    place = [jax.random.randint(jax.random.fold_in(rng, axis), (), 0, length) for axis, length in enumerate(drawn.shape)]
    widest = drawn.shape.index(max(drawn.shape))
    beside = place[:widest] + [(place[widest] + 1) % drawn.shape[widest]] + place[widest + 1:]
    return drawn.at[tuple(place)].set(least).at[tuple(beside)].set(largest)


def shard_levels(stream_key, extent, cuts, low, largest):
    def one(position, shards_of):
        draws = jax.random.uniform(jax.random.fold_in(jax.random.fold_in(stream_key, 6), position), (shards_of,), jnp.float32, low / len(cuts), largest / len(cuts))
        return jnp.repeat(jnp.exp(draws), extent[position] // shards_of).reshape((-1,) + (1,) * (len(extent) - position - 1))

    loudness = one(*cuts[0])
    for cut in cuts[1:]:
        loudness = loudness * one(*cut)
    return loudness


def gaussian(rng, dims, spread, most, cuts=(), kind=jnp.bfloat16):
    array = jax.random.normal(rng, dims, jnp.float32) * spread
    if len(cuts) > 0:
        array = shard_levels(rng, dims, cuts, -0.22, 0.18) * array
    return jnp.clip(array, min=-most, max=most).astype(kind)


def setup_inputs(seed: int = 0) -> dict:
    keys = jax.random.split(jax.random.key(seed), 11)
    return {
        "latent": gaussian(keys[0], (LAT, LONS, C), 1.0, 6.0, ((0, 8), (1, 16))),
        "row_index": touch_ends(jax.random.randint(keys[1], (N_BAND, N_LON, NB), 0, LAT_DEV), jax.random.fold_in(keys[1], 1), 0, LAT_DEV - 1).astype(jnp.int32),
        "interp_weights": gaussian(keys[2], (TOTAL_OBS_BLOCKS, BLOCK_OBS_SLOTS, LON_DEV), LON_DEV ** -0.5, 0.5, ((0, 128),)),
        "observation_slot_index": touch_ends(jax.random.randint(keys[3], (TOTAL_OBS_BLOCKS, BLOCK_OBS_SLOTS), 0, WINDOW_SLOTS), jax.random.fold_in(keys[3], 1), 0, WINDOW_SLOTS - 1).astype(jnp.int32),
        "counts": touch_ends(jax.random.randint(keys[4], (TOTAL_OBS_BLOCKS,), BLOCK_OBS_SLOTS // 4, BLOCK_OBS_SLOTS + 1), jax.random.fold_in(keys[4], 1), BLOCK_OBS_SLOTS // 4, BLOCK_OBS_SLOTS).astype(jnp.int32),
        "targets": gaussian(keys[5], (TOTAL_OBS_BLOCKS, BLOCK_OBS_SLOTS, NV), 1.0, 6.0, ((0, 128),)),
        "gain": jnp.clip(1.0 + 0.1 * jax.random.normal(keys[6], (C,), jnp.float32), 0.5, 1.5),
        "w_in": gaussian(keys[7], (C, HID), C ** -0.5, 0.375),
        "w_out": gaussian(keys[8], (HID, C), HID ** -0.5, 0.25),
        "head": gaussian(keys[9], (C, NV), C ** -0.5, 0.375),
    }


norm_eps = 1e-05

def rounded_slots(values):
    return lax.optimization_barrier(values.astype(jnp.bfloat16))

def cycle_mix(layer_in):
    return layer_in + 0.5 * (jnp.roll(layer_in, 1, axis=-2) + jnp.roll(layer_in, -1, axis=-2))

def silu_slope(pre_act):
    sigmoid_a = jax.nn.sigmoid(pre_act)
    return sigmoid_a * (1.0 + pre_act * (1.0 - sigmoid_a))

def processor_row(lat_row, gain, w_in, w_out):
    summed = cycle_mix(lat_row.astype(jnp.float32))
    inv_rms = lax.rsqrt(lax.optimization_barrier(jnp.mean(summed * summed, axis=-1, keepdims=True)) + norm_eps)
    normed = (summed * inv_rms * gain).astype(jnp.bfloat16)
    pre_act = jnp.dot(normed, w_in, preferred_element_type=jnp.float32)
    activated = jax.nn.silu(pre_act).astype(jnp.bfloat16)
    advanced = (lat_row.astype(jnp.float32) + jnp.dot(activated, w_out, preferred_element_type=jnp.float32)).astype(jnp.bfloat16)
    return (summed, inv_rms, normed, pre_act, activated, advanced)

def per_device(values):
    return values.reshape((DEVICES, NB) + values.shape[1:])

def reference(latent, row_index, interp_weights, observation_slot_index, counts, targets, gain, w_in, w_out, head):
    channels = latent.shape[-1]

    def forward_row(lat_row):
        return processor_row(lat_row, gain, w_in, w_out)[5]
    advanced = lax.map(forward_row, latent)
    stacked = jnp.concatenate([latent, advanced], axis=-1).reshape(LAT, N_LON, LON_DEV, 2 * channels)
    loss_scale = 1.0 / math.sqrt(BLOCK_OBS_SLOTS)
    block_ids = jnp.arange(NB, dtype=jnp.int32)
    owner_ids = block_ids // BPP
    slot_ids = block_ids % BPP
    live_base = jnp.arange(BLOCK_OBS_SLOTS, dtype=jnp.int32)
    device_ids = jnp.arange(DEVICES, dtype=jnp.int32)

    def obs_device(carry, inputs):
        grid_grad, head_grad = carry
        device, weights_dev, device_slot_count, counts_dev, targets_dev = inputs
        band = device // N_LON
        sender = device % N_LON
        row_ids = row_index[band, owner_ids, sender * BPP + slot_ids].astype(jnp.int32)
        glob_rows = band * LAT_DEV + row_ids
        tile_pairs = stacked[glob_rows, owner_ids].astype(jnp.float32)
        temporal_weight = rounded_slots(device_slot_count.astype(jnp.float32) / (WINDOW_SLOTS - 1)).astype(jnp.float32)[..., None]
        weights_f = weights_dev.astype(jnp.float32)
        proj_old = jnp.einsum('bol,blc->boc', weights_f, tile_pairs[..., :channels])
        proj_new = jnp.einsum('bol,blc->boc', weights_f, tile_pairs[..., channels:])
        obs_latent = ((1.0 - temporal_weight) * proj_old + temporal_weight * proj_new).astype(jnp.bfloat16).reshape(-1, channels)
        predicted = jnp.dot(obs_latent, head, preferred_element_type=jnp.float32)
        live_rows = (live_base[None, :] < counts_dev[:, None]).reshape(-1, 1)
        residual = jnp.where(live_rows, predicted - targets_dev.reshape(-1, predicted.shape[-1]).astype(jnp.float32), 0.0)
        pred_grad = (residual * loss_scale).astype(jnp.bfloat16)
        head_grad = head_grad + jnp.dot(obs_latent.T, pred_grad, preferred_element_type=jnp.float32)
        obs_grad = jnp.dot(pred_grad, head.T, preferred_element_type=jnp.float32)
        obs_grad = rounded_slots(obs_grad).astype(jnp.float32).reshape(NB, BLOCK_OBS_SLOTS, channels)
        back_old = rounded_slots((1.0 - temporal_weight) * obs_grad).astype(jnp.float32)
        back_new = rounded_slots(temporal_weight * obs_grad).astype(jnp.float32)
        tile_old = jnp.einsum('bol,boc->blc', weights_f, back_old)
        tile_new = jnp.einsum('bol,boc->blc', weights_f, back_new)
        tile_grads = rounded_slots(jnp.concatenate([tile_old, tile_new], axis=-1)).astype(jnp.float32)
        grid_grad = grid_grad.at[glob_rows, owner_ids].add(tile_grads)
        return ((grid_grad, head_grad), None)
    start = (jnp.zeros((LAT, N_LON, LON_DEV, 2 * channels), jnp.float32), jnp.zeros(head.shape, jnp.float32))
    (grid_grad, head_grad), _ = lax.scan(obs_device, start, (device_ids, per_device(interp_weights), per_device(observation_slot_index), per_device(counts), per_device(targets)))
    grid_grad = grid_grad.reshape(LAT, LONS, 2 * channels)

    def backward_row(carry, inputs):
        grad_in, grad_out, grad_gain = carry
        lat_row, row_grad = inputs
        summed, inv_rms, normed, pre_act, activated, advanced = processor_row(lat_row, gain, w_in, w_out)
        grad_adv = row_grad[:, channels:].astype(jnp.bfloat16)
        grad_out = grad_out + jnp.dot(activated.T, grad_adv, preferred_element_type=jnp.float32)
        act_grad = jnp.dot(grad_adv, w_out.T, preferred_element_type=jnp.float32)
        pre_grad = (act_grad * silu_slope(pre_act)).astype(jnp.bfloat16)
        grad_in = grad_in + jnp.dot(normed.T, pre_grad, preferred_element_type=jnp.float32)
        normed_grad = jnp.dot(pre_grad, w_in.T, preferred_element_type=jnp.float32)
        grad_gain = grad_gain + lax.optimization_barrier(jnp.sum(normed_grad * summed * inv_rms, axis=0))
        gained = normed_grad * gain
        summed_grad = inv_rms * (gained - summed * inv_rms * inv_rms * lax.optimization_barrier(jnp.mean(gained * summed, axis=-1, keepdims=True)))
        latent_grad = row_grad[:, :channels] + row_grad[:, channels:] + cycle_mix(summed_grad)
        return ((grad_in, grad_out, grad_gain), latent_grad)
    start_back = (jnp.zeros(w_in.shape, jnp.float32), jnp.zeros(w_out.shape, jnp.float32), jnp.zeros(gain.shape, jnp.float32))
    (grad_in, grad_out, grad_gain), grad_latent = lax.scan(backward_row, start_back, (latent, grid_grad))
    return (grad_latent, grad_in / DEVICES, grad_out / DEVICES, grad_gain / DEVICES, head_grad / DEVICES)
```

```python
import functools
import math

import jax
import jax.numpy as jnp
from jax import lax
from jax.experimental import pallas as pl
from jax.experimental.pallas import tpu as pltpu
from jax.sharding import PartitionSpec as P

WINDOW_SLOTS = 7
NORM_EPS = 1e-05
ROWS_STEP = 4
BLOCKS_STEP = 4
META = 8
VMEM_LIMIT = 48 * 2**20

f32 = jnp.float32
bf16 = jnp.bfloat16


def dot(a, b):
    return jnp.dot(a, b, preferred_element_type=f32)


def dot_t(a, b):
    return lax.dot_general(a, b, (((0,), (0,)), ((), ())), preferred_element_type=f32)


def params(**kw):
    return pltpu.CompilerParams(vmem_limit_bytes=VMEM_LIMIT, **kw)


def cost(flops, nbytes, trans=0):
    return pl.CostEstimate(flops=flops, bytes_accessed=nbytes, transcendentals=trans)


def pack_kernel(counts, slot_ref, w_hbm, t_hbm, out_hbm, meta, sems):
    blocks, obs = slot_ref.shape
    nv = t_hbm.shape[1]
    copies = [
        pltpu.make_async_copy(w_hbm, out_hbm.at[:, pl.ds(0, obs), :], sems.at[0]),
        pltpu.make_async_copy(t_hbm, out_hbm.at[:, pl.ds(obs, nv), :], sems.at[1]),
    ]
    for c in copies:
        c.start()
    coef = slot_ref[...].astype(f32) / (WINDOW_SLOTS - 1)
    lane = lax.broadcasted_iota(jnp.int32, (META, obs), 1)
    row = lax.broadcasted_iota(jnp.int32, (META, obs), 0)
    for b in range(blocks):
        live = jnp.where(lane < counts[b], 1.0, 0.0)
        meta[b] = jnp.where(row == 0, coef[b : b + 1, :], live).astype(bf16)
    last = pltpu.make_async_copy(meta, out_hbm.at[:, pl.ds(obs + nv, META), :], sems.at[2])
    last.start()
    for c in copies:
        c.wait()
    last.wait()


def pack(weights, targets, slots, counts):
    blocks, obs, cells = weights.shape
    return pl.pallas_call(
        pack_kernel,
        out_shape=jax.ShapeDtypeStruct((blocks, 2 * obs + META, cells), bf16),
        in_specs=[
            pl.BlockSpec(memory_space=pltpu.SMEM),
            pl.BlockSpec(memory_space=pltpu.VMEM),
            pl.BlockSpec(memory_space=pl.ANY),
            pl.BlockSpec(memory_space=pl.ANY),
        ],
        out_specs=pl.BlockSpec(memory_space=pl.ANY),
        scratch_shapes=[pltpu.VMEM((blocks, META, obs), bf16), pltpu.SemaphoreType.DMA((3,))],
        compiler_params=params(),
        cost_estimate=cost(1, 4 * 2**20),
        name="pack",
    )(counts, slots, weights, targets)


def mixed(x, left, right):
    cells = x.shape[1]
    place = lax.broadcasted_iota(jnp.int32, x.shape, 1)
    from_left = jnp.where(place == 0, left, pltpu.roll(x, 1, 1))
    from_right = jnp.where(place == cells - 1, right, pltpu.roll(x, cells - 1, 1))
    return x + 0.5 * (from_left + from_right)


def normalized(lat, left, right):
    summed = mixed(lat, left, right)
    inv = lax.rsqrt(jnp.mean(summed * summed, axis=-1, keepdims=True) + NORM_EPS)
    return summed * inv, inv


def forward_kernel(lat_ref, left_ref, right_ref, gain_ref, w_in_ref, w_out_ref, stk_ref, slope_ref, act_t_ref, xhat_t_ref):
    rows, cells, ch = lat_ref.shape
    lat_b = lat_ref[...]
    lat = lat_b.astype(f32)
    xhat, _ = normalized(lat, left_ref[...], right_ref[...])
    xhat = xhat.reshape(rows * cells, ch)
    pre = dot((xhat * gain_ref[...]).astype(bf16), w_in_ref[...])
    sig = jax.nn.sigmoid(pre)
    act = pre * sig
    act_b = act.astype(bf16)
    slope_ref[...] = (sig * (1.0 + pre * (1.0 - sig))).astype(bf16)
    new = lat.reshape(rows * cells, ch) + dot(act_b, w_out_ref[...])
    stk_ref[:, 0:cells, :] = lat_b
    stk_ref[:, cells : 2 * cells, :] = new.astype(bf16).reshape(rows, cells, ch)
    act_t_ref[...] = act_b.T
    xhat_t_ref[...] = xhat.astype(bf16).T


def forward(latent, left, right, gain, w_in, w_out):
    rows, cells, ch = latent.shape
    hid = w_in.shape[1]
    n = rows * cells
    step = ROWS_STEP * cells
    return pl.pallas_call(
        forward_kernel,
        grid=(rows // ROWS_STEP,),
        out_shape=(
            jax.ShapeDtypeStruct((rows, 2 * cells, ch), bf16),
            jax.ShapeDtypeStruct((n, hid), bf16),
            jax.ShapeDtypeStruct((hid, n), bf16),
            jax.ShapeDtypeStruct((ch, n), bf16),
        ),
        in_specs=[
            pl.BlockSpec((ROWS_STEP, cells, ch), lambda i: (i, 0, 0)),
            pl.BlockSpec((ROWS_STEP, 1, ch), lambda i: (i, 0, 0)),
            pl.BlockSpec((ROWS_STEP, 1, ch), lambda i: (i, 0, 0)),
            pl.BlockSpec((1, ch), lambda i: (0, 0)),
            pl.BlockSpec((ch, hid), lambda i: (0, 0)),
            pl.BlockSpec((hid, ch), lambda i: (0, 0)),
        ],
        out_specs=(
            pl.BlockSpec((ROWS_STEP, 2 * cells, ch), lambda i: (i, 0, 0)),
            pl.BlockSpec((step, hid), lambda i: (i, 0)),
            pl.BlockSpec((hid, step), lambda i: (0, i)),
            pl.BlockSpec((ch, step), lambda i: (0, i)),
        ),
        compiler_params=params(),
        cost_estimate=cost(4 * n * ch * hid, 16 * 2**20, 2 * n * hid),
        name="forward",
    )(latent, left, right, gain, w_in, w_out)


def decode_kernel(
    rows_ref, got_ref, stk_ref, head_ref, head_t_ref, w_out_t_ref, slope_ref, act_t_ref, xhat_t_ref,
    pre_grad_ref, both_ref, sums_ref,
    acc_both, acc_new, acc_head, acc_in, acc_out,
    *, obs_steps, row_steps,
):
    i = pl.program_id(0)
    nb = got_ref.shape[0]
    ch, nv = head_ref.shape
    obs = (got_ref.shape[1] - META) // 2
    cells = got_ref.shape[2]
    scale = 1.0 / math.sqrt(obs)

    @pl.when(i == 0)
    def _():
        acc_both[...] = jnp.zeros_like(acc_both)
        acc_new[...] = jnp.zeros_like(acc_new)
        acc_head[...] = jnp.zeros_like(acc_head)
        acc_in[...] = jnp.zeros_like(acc_in)
        acc_out[...] = jnp.zeros_like(acc_out)

    @pl.when(i < obs_steps)
    def _():
        places = [rows_ref[0, 0, i * nb + j] for j in range(nb)]
        latents, coefs, lives = [], [], []
        for j in range(nb):
            meta = got_ref[j, 2 * obs : 2 * obs + META, :].astype(f32).T
            t, live = meta[:, 0:1], meta[:, 1:2]
            w = got_ref[j, 0:obs, :].astype(f32)
            pair = jnp.concatenate([(w * (1.0 - t)).astype(bf16), (w * t).astype(bf16)], axis=1)
            latents.append(dot(pair, stk_ref[places[j]]).astype(bf16))
            coefs.append(t)
            lives.append(live)
        obs_latent = jnp.concatenate(latents, axis=0)
        pred = dot(obs_latent, head_ref[...])
        goals = jnp.concatenate([got_ref[j, obs : 2 * obs, :] for j in range(nb)], axis=0)
        live = jnp.concatenate(lives, axis=0)
        residual = jnp.where(live > 0.5, pred - goals.astype(f32), 0.0)
        pred_grad = (residual * scale).astype(bf16)
        acc_head[...] += dot_t(pred_grad, obs_latent)
        grad = dot(pred_grad, head_t_ref[...])
        for j in range(nb):
            g = grad[j * obs : (j + 1) * obs, :]
            w = got_ref[j, 0:obs, :]
            pulled = dot_t(w, jnp.concatenate([g.astype(bf16), (g * coefs[j]).astype(bf16)], axis=1))
            acc_both[places[j]] += pulled[:, :ch]
            acc_new[places[j]] += pulled[:, ch:]

    @pl.when(i >= obs_steps)
    def _():
        k = i - obs_steps
        nr = both_ref.shape[0]
        both_ref[...] = acc_both[pl.ds(k * nr, nr)]
        adv = acc_new[pl.ds(k * nr, nr)].reshape(nr * cells, ch).astype(bf16)
        pre_grad = (dot(adv, w_out_t_ref[...]) * slope_ref[...].astype(f32)).astype(bf16)
        pre_grad_ref[...] = pre_grad
        acc_in[...] += dot(xhat_t_ref[...], pre_grad)
        acc_out[...] += dot(act_t_ref[...], adv)

    @pl.when(i == obs_steps + row_steps - 1)
    def _():
        put_chunks(sums_ref, 0, acc_in)
        put_chunks(sums_ref, 1, acc_out)
        put_chunks(sums_ref, 2, acc_head)
        left = acc_head.shape[0] * acc_head.shape[1] // (8 * 128)
        sums_ref[left:, 16:24, :] = jnp.zeros((sums_ref.shape[0] - left, 8, 128), bf16)


def put_chunks(sums_ref, part, acc):
    down = acc.shape[0] // 8
    for j in range(acc.shape[1] // 128):
        tiles = acc[:, 128 * j : 128 * (j + 1)].reshape(down, 8, 128)
        sums_ref[down * j : down * (j + 1), 8 * part : 8 * part + 8, :] = tiles.astype(bf16)


def take_chunks(got_ref, part, shape):
    down = shape[0] // 8
    return jnp.concatenate(
        [
            got_ref[down * j : down * (j + 1), 8 * part : 8 * part + 8, :].astype(f32).reshape(shape[0], 128)
            for j in range(shape[1] // 128)
        ],
        axis=1,
    )


def decode(rows, got, stk, head, head_t, w_out_t, slope, act_t, xhat_t, chunks):
    nrow, two_cells, ch = stk.shape
    cells = two_cells // 2
    blocks = got.shape[0]
    nv = head.shape[1]
    hid = w_out_t.shape[1]
    n = nrow * cells
    obs_steps, row_steps = blocks // BLOCKS_STEP, nrow // ROWS_STEP
    step = ROWS_STEP * cells

    def at(i):
        return jnp.maximum(i - obs_steps, 0)

    once = pl.Buffered(1)
    return pl.pallas_call(
        functools.partial(decode_kernel, obs_steps=obs_steps, row_steps=row_steps),
        grid=(obs_steps + row_steps,),
        out_shape=(
            jax.ShapeDtypeStruct((n, hid), bf16),
            jax.ShapeDtypeStruct((nrow, cells, ch), f32),
            jax.ShapeDtypeStruct((chunks, 24, 128), bf16),
        ),
        in_specs=[
            pl.BlockSpec(memory_space=pltpu.SMEM),
            pl.BlockSpec((BLOCKS_STEP,) + got.shape[1:], lambda i: (jnp.minimum(i, obs_steps - 1), 0, 0)),
            pl.BlockSpec(stk.shape, lambda i: (0, 0, 0), pipeline_mode=once),
            pl.BlockSpec((ch, nv), lambda i: (0, 0)),
            pl.BlockSpec((nv, ch), lambda i: (0, 0)),
            pl.BlockSpec((ch, hid), lambda i: (0, 0)),
            pl.BlockSpec((step, hid), lambda i: (at(i), 0)),
            pl.BlockSpec((hid, step), lambda i: (0, at(i))),
            pl.BlockSpec((ch, step), lambda i: (0, at(i))),
        ],
        out_specs=(
            pl.BlockSpec((step, hid), lambda i: (at(i), 0)),
            pl.BlockSpec((ROWS_STEP, cells, ch), lambda i: (at(i), 0, 0)),
            pl.BlockSpec((chunks, 24, 128), lambda i: (0, 0, 0)),
        ),
        scratch_shapes=[
            pltpu.VMEM((nrow, cells, ch), f32),
            pltpu.VMEM((nrow, cells, ch), f32),
            pltpu.VMEM((nv, ch), f32),
            pltpu.VMEM((ch, hid), f32),
            pltpu.VMEM((hid, ch), f32),
        ],
        compiler_params=params(),
        cost_estimate=cost(10 * n * ch * hid, 24 * 2**20),
        name="decode",
    )(rows, got, stk, head, head_t, w_out_t, slope, act_t, xhat_t)


def backward_kernel(lat_ref, left_ref, right_ref, gain_ref, w_in_t_ref, pre_grad_ref, both_ref, out_ref, first_ref, last_ref):
    rows, cells, ch = lat_ref.shape
    xhat, inv = normalized(lat_ref[...].astype(f32), left_ref[...], right_ref[...])
    gained = dot(pre_grad_ref[...], w_in_t_ref[...]) * gain_ref[...]
    gained = gained.reshape(rows, cells, ch)
    summed_grad = inv * (gained - xhat * jnp.mean(gained * xhat, axis=-1, keepdims=True))
    out_ref[...] = both_ref[...] + mixed(summed_grad, jnp.zeros((), f32), jnp.zeros((), f32))
    first_ref[...] = summed_grad[:, 0:1, :]
    last_ref[...] = summed_grad[:, cells - 1 : cells, :]


def backward(latent, left, right, gain, w_in_t, pre_grad, both):
    rows, cells, ch = latent.shape
    hid = w_in_t.shape[0]
    step = ROWS_STEP * cells
    edge = pl.BlockSpec((ROWS_STEP, 1, ch), lambda i: (i, 0, 0))
    whole = pl.BlockSpec((ROWS_STEP, cells, ch), lambda i: (i, 0, 0))
    return pl.pallas_call(
        backward_kernel,
        grid=(rows // ROWS_STEP,),
        out_shape=(
            jax.ShapeDtypeStruct((rows, cells, ch), f32),
            jax.ShapeDtypeStruct((rows, 1, ch), f32),
            jax.ShapeDtypeStruct((rows, 1, ch), f32),
        ),
        in_specs=[
            whole,
            edge,
            edge,
            pl.BlockSpec((1, ch), lambda i: (0, 0)),
            pl.BlockSpec((hid, ch), lambda i: (0, 0)),
            pl.BlockSpec((step, hid), lambda i: (i, 0)),
            whole,
        ],
        out_specs=(whole, edge, edge),
        compiler_params=params(),
        cost_estimate=cost(2 * rows * cells * ch * hid, 16 * 2**20),
        name="backward",
    )(latent, left, right, gain, w_in_t, pre_grad, both)


def edges_kernel(left_ref, right_ref, grad_ref, out_ref):
    block = grad_ref[...]
    place = lax.broadcasted_iota(jnp.int32, block.shape, 1)
    at_start = pl.program_id(0) == 0
    add = 0.5 * jnp.where(at_start, left_ref[...], right_ref[...])
    hit = place == jnp.where(at_start, 0, block.shape[1] - 1)
    out_ref[...] = block + jnp.where(hit, add, 0.0)


def add_edges(grad, left, right):
    rows, cells, ch = grad.shape
    ends = pl.BlockSpec((rows, 8, ch), lambda i: (0, i * (cells // 8 - 1), 0))
    edge = pl.BlockSpec((rows, 1, ch), lambda i: (0, 0, 0))
    return pl.pallas_call(
        edges_kernel,
        grid=(2,),
        out_shape=jax.ShapeDtypeStruct(grad.shape, f32),
        in_specs=[edge, edge, ends],
        out_specs=ends,
        input_output_aliases={2: 0},
        compiler_params=params(),
        cost_estimate=cost(rows * 16 * ch, 2**20),
        name="edges",
    )(left, right, grad)


def total_kernel(got_ref, out_ref):
    total = jnp.sum(got_ref[...].astype(f32), axis=0, keepdims=True).astype(bf16)
    out_ref[...] = jnp.broadcast_to(total, out_ref.shape)


def total(got):
    return pl.pallas_call(
        total_kernel,
        out_shape=jax.ShapeDtypeStruct(got.shape, bf16),
        compiler_params=params(),
        cost_estimate=cost(got.size, 2 * got.size * 2),
        name="total",
    )(got)


def finish_kernel(got_ref, gain_ref, w_in_ref, in_ref, out_ref, gain_grad_ref, head_ref, *, devices):
    share = 1.0 / devices
    x = take_chunks(got_ref, 0, in_ref.shape) * share
    in_ref[...] = x * gain_ref[...]
    per_channel = jnp.sum(x * w_in_ref[...].astype(f32), axis=1, keepdims=True)
    gain_grad_ref[...] = jnp.broadcast_to(per_channel, (x.shape[0], 128)).T[0:1, :]
    out_ref[...] = take_chunks(got_ref, 1, out_ref.shape) * share
    head_ref[...] = (take_chunks(got_ref, 2, head_ref.shape[::-1]) * share).T


def finish(got, gain, w_in, head, devices):
    ch, hid = w_in.shape
    return pl.pallas_call(
        functools.partial(finish_kernel, devices=devices),
        out_shape=(
            jax.ShapeDtypeStruct((ch, hid), f32),
            jax.ShapeDtypeStruct((hid, ch), f32),
            jax.ShapeDtypeStruct((1, ch), f32),
            jax.ShapeDtypeStruct(head.shape, f32),
        ),
        compiler_params=params(),
        cost_estimate=cost(4 * ch * hid, 3 * 2**20),
        name="finish",
    )(got, gain.reshape(ch, 1), w_in)


def from_sides(first, last):
    count = lax.axis_size("lon")
    left = lax.ppermute(last, "lon", [(i, (i + 1) % count) for i in range(count)])
    right = lax.ppermute(first, "lon", [((i + 1) % count, i) for i in range(count)])
    return left, right


def body(latent, row_index, weights, slots, counts, targets, gain, w_in, w_out, head):
    both_axes = ("band", "lon")
    devices = lax.axis_size("band") * lax.axis_size("lon")
    cells = latent.shape[1]
    got = lax.all_to_all(pack(weights, targets, slots, counts), "lon", 0, 0, tiled=True)
    left, right = from_sides(latent[:, 0:1, :], latent[:, cells - 1 : cells, :])
    left, right = left.astype(f32), right.astype(f32)
    gain_row = gain.reshape(1, -1)
    stk, slope, act_t, xhat_t = forward(latent, left, right, gain_row, w_in, w_out)
    pre_grad, both, sums = decode(row_index, got, stk, head, head.T, w_out.T, slope, act_t, xhat_t, devices)
    parts = lax.all_to_all(sums, both_axes, 0, 0, tiled=True)
    grad, first, last = backward(latent, left, right, gain_row, w_in.T, pre_grad, both)
    grad_left, grad_right = from_sides(first.astype(bf16), last.astype(bf16))
    grad = add_edges(grad, grad_left.astype(f32), grad_right.astype(f32))
    chunks = lax.all_to_all(total(parts), both_axes, 0, 0, tiled=True)
    grad_in, grad_out, grad_gain, grad_head = finish(chunks, gain, w_in, head, devices)
    return grad, grad_in, grad_out, grad_gain.reshape(-1), grad_head


def solution(mesh):
    return jax.shard_map(
        body,
        mesh=mesh,
        in_specs=(
            P("band", "lon", None),
            P("band", "lon", None),
            P(("band", "lon"), None, None),
            P(("band", "lon"), None),
            P(("band", "lon")),
            P(("band", "lon"), None, None),
            P(),
            P(),
            P(),
            P(),
        ),
        out_specs=(P("band", "lon", None), P(), P(), P(), P()),
        check_vma=False,
    )
```

```python
import functools
import math

import jax
import jax.numpy as jnp
from jax import lax
from jax.experimental import pallas as pl
from jax.experimental.pallas import tpu as pltpu
from jax.sharding import PartitionSpec as P

WINDOW_SLOTS = 7
NORM_EPS = 1e-05
ROWS_STEP = 4
BLOCKS_STEP = 8
PULL_ROWS = 16
META = 8

f32 = jnp.float32
bf16 = jnp.bfloat16
INSIDE = pl.BlockSpec(memory_space=pltpu.VMEM)
OUTSIDE = pl.BlockSpec(memory_space=pltpu.HBM)


def dot(a, b):
    return jnp.dot(a, b, preferred_element_type=f32)


def dot_t(a, b):
    return lax.dot_general(a, b, (((0,), (0,)), ((), ())), preferred_element_type=f32)


def params(mib=48):
    return pltpu.CompilerParams(vmem_limit_bytes=mib * 2**20)


def in_hbm(*arrays):
    return [pltpu.with_memory_space_constraint(x, pltpu.HBM) for x in arrays]


def cost(flops, nbytes, trans=0):
    return pl.CostEstimate(flops=flops, bytes_accessed=nbytes, transcendentals=trans)


def pack_kernel(w_hbm, t_hbm, slot_hbm, count_hbm, out_hbm, slots, counts, meta, sems):
    blocks, obs = slots.shape
    nv = t_hbm.shape[1]
    small = [
        pltpu.make_async_copy(slot_hbm, slots, sems.at[0]),
        pltpu.make_async_copy(count_hbm, counts, sems.at[1]),
    ]
    large = [
        pltpu.make_async_copy(w_hbm, out_hbm.at[:, pl.ds(0, obs), :], sems.at[2]),
        pltpu.make_async_copy(t_hbm, out_hbm.at[:, pl.ds(obs, nv), :], sems.at[3]),
    ]
    for c in small + large:
        c.start()
    for c in small:
        c.wait()
    coef = slots[...].astype(f32) / (WINDOW_SLOTS - 1)
    lane = lax.broadcasted_iota(jnp.int32, (META, obs), 1)
    row = lax.broadcasted_iota(jnp.int32, (META, obs), 0)
    for b in range(blocks):
        live = jnp.where(lane < counts[b], 1.0, 0.0)
        meta[b] = jnp.where(row == 0, coef[b : b + 1, :], live).astype(bf16)
    last = pltpu.make_async_copy(meta, out_hbm.at[:, pl.ds(obs + nv, META), :], sems.at[4])
    last.start()
    for c in large:
        c.wait()
    last.wait()


def pack(weights, targets, slots, counts):
    blocks, obs, cells = weights.shape
    return pl.pallas_call(
        pack_kernel,
        out_shape=pltpu.HBM((blocks, 2 * obs + META, cells), bf16),
        in_specs=[OUTSIDE] * 4,
        out_specs=OUTSIDE,
        scratch_shapes=[
            pltpu.VMEM(slots.shape, jnp.int32),
            pltpu.SMEM(counts.shape, jnp.int32),
            pltpu.VMEM((blocks, META, obs), bf16),
            pltpu.SemaphoreType.DMA((5,)),
        ],
        compiler_params=params(),
        cost_estimate=cost(1, 4 * 2**20),
        name="pack",
    )(*in_hbm(weights, targets, slots, counts))


def mixed(x, left, right):
    cells = x.shape[1]
    place = lax.broadcasted_iota(jnp.int32, x.shape, 1)
    from_left = jnp.where(place == 0, left, pltpu.roll(x, 1, 1))
    from_right = jnp.where(place == cells - 1, right, pltpu.roll(x, cells - 1, 1))
    return x + 0.5 * (from_left + from_right)


def normalized(lat, left, right):
    summed = mixed(lat, left, right)
    inv = lax.rsqrt(jnp.mean(summed * summed, axis=-1, keepdims=True) + NORM_EPS)
    return summed * inv, inv


def forward_kernel(lat_ref, left_ref, right_ref, gain_ref, w_in_ref, w_out_ref, stk_ref, slope_ref, act_t_ref, xhat_t_ref):
    rows, cells, ch = lat_ref.shape
    lat_b = lat_ref[...]
    lat = lat_b.astype(f32)
    xhat, _ = normalized(lat, left_ref[...], right_ref[...])
    xhat = xhat.reshape(rows * cells, ch)
    pre = dot((xhat * gain_ref[...]).astype(bf16), w_in_ref[...])
    sig = jax.nn.sigmoid(pre)
    act = pre * sig
    act_b = act.astype(bf16)
    slope_ref[...] = (sig * (1.0 + pre * (1.0 - sig))).astype(bf16)
    new = lat.reshape(rows * cells, ch) + dot(act_b, w_out_ref[...])
    stk_ref[:, 0:cells, :] = lat_b
    stk_ref[:, cells : 2 * cells, :] = new.astype(bf16).reshape(rows, cells, ch)
    act_t_ref[...] = act_b.T
    xhat_t_ref[...] = xhat.astype(bf16).T


def forward(latent, left, right, gain, w_in, w_out):
    rows, cells, ch = latent.shape
    hid = w_in.shape[1]
    n = rows * cells
    step = ROWS_STEP * cells
    return pl.pallas_call(
        forward_kernel,
        grid=(rows // ROWS_STEP,),
        out_shape=(
            pltpu.HBM((rows, 2 * cells, ch), bf16),
            pltpu.HBM((n, hid), bf16),
            pltpu.HBM((hid, n), bf16),
            pltpu.HBM((ch, n), bf16),
        ),
        in_specs=[
            pl.BlockSpec((ROWS_STEP, cells, ch), lambda i: (i, 0, 0)),
            pl.BlockSpec((ROWS_STEP, 1, ch), lambda i: (i, 0, 0)),
            pl.BlockSpec((ROWS_STEP, 1, ch), lambda i: (i, 0, 0)),
            pl.BlockSpec((1, ch), lambda i: (0, 0)),
            pl.BlockSpec((ch, hid), lambda i: (0, 0)),
            pl.BlockSpec((hid, ch), lambda i: (0, 0)),
        ],
        out_specs=(
            pl.BlockSpec((ROWS_STEP, 2 * cells, ch), lambda i: (i, 0, 0)),
            pl.BlockSpec((step, hid), lambda i: (i, 0)),
            pl.BlockSpec((hid, step), lambda i: (0, i)),
            pl.BlockSpec((ch, step), lambda i: (0, i)),
        ),
        compiler_params=params(),
        cost_estimate=cost(4 * n * ch * hid, 16 * 2**20, 2 * n * hid),
        name="forward",
    )(latent, left, right, gain, w_in, w_out)


def decode_kernel(
    rows_ref, got_hbm, stk_hbm, head_ref, head_t_ref, w_out_t_ref, slope_hbm, act_t_hbm, xhat_t_hbm,
    pre_grad_hbm, both_hbm, sums_ref,
    got, stk, slope, act_t, xhat_t, pre_grad_all, acc_both, acc_new, acc_head, acc_in, acc_out,
    got_sems, stk_sems, in_sems, out_sems,
):
    nb, nr = BLOCKS_STEP, PULL_ROWS
    blocks = got.shape[0]
    ch, nv = head_ref.shape
    obs = (got.shape[1] - META) // 2
    rows, cells, _ = acc_both.shape
    scale = 1.0 / math.sqrt(obs)
    step = nr * cells

    def got_copy(i):
        here = pl.ds(i * nb, nb)
        return pltpu.make_async_copy(got_hbm.at[here], got.at[here], got_sems.at[i])

    def stk_copy(b):
        return pltpu.make_async_copy(stk_hbm.at[rows_ref[0, 0, b]], stk.at[b], stk_sems.at[b])

    def pre_grad_copy(k):
        flat = pl.ds(pl.multiple_of(k * step, step), step)
        return pltpu.make_async_copy(pre_grad_all.at[flat], pre_grad_hbm.at[flat], out_sems.at[k])

    for i in range(blocks // nb):
        got_copy(i).start()
        for j in range(nb):
            stk_copy(i * nb + j).start()
    later = [
        pltpu.make_async_copy(src, dst, in_sems.at[i])
        for i, (src, dst) in enumerate(((slope_hbm, slope), (xhat_t_hbm, xhat_t), (act_t_hbm, act_t)))
    ]
    for c in later:
        c.start()
    for acc in (acc_both, acc_new, acc_head, acc_in, acc_out):
        acc[...] = jnp.zeros_like(acc)

    def observe(i, carry):
        first = i * nb
        got_copy(i).wait()
        for j in range(nb):
            stk_copy(first + j).wait()
        places = [rows_ref[0, 0, first + j] for j in range(nb)]
        latents, coefs, lives = [], [], []
        for j in range(nb):
            meta = got[first + j, 2 * obs : 2 * obs + META, :].astype(f32).T
            t, live = meta[:, 0:1], meta[:, 1:2]
            w = got[first + j, 0:obs, :].astype(f32)
            pair = jnp.concatenate([(w * (1.0 - t)).astype(bf16), (w * t).astype(bf16)], axis=1)
            latents.append(dot(pair, stk[first + j]).astype(bf16))
            coefs.append(t)
            lives.append(live)
        obs_latent = jnp.concatenate(latents, axis=0)
        pred = dot(obs_latent, head_ref[...])
        goals = jnp.concatenate([got[first + j, obs : 2 * obs, :] for j in range(nb)], axis=0)
        live = jnp.concatenate(lives, axis=0)
        residual = jnp.where(live > 0.5, pred - goals.astype(f32), 0.0)
        pred_grad = (residual * scale).astype(bf16)
        acc_head[...] += dot_t(pred_grad, obs_latent)
        grad = dot(pred_grad, head_t_ref[...])
        for j in range(nb):
            g = grad[j * obs : (j + 1) * obs, :]
            w = got[first + j, 0:obs, :]
            pulled = dot_t(w, jnp.concatenate([g.astype(bf16), (g * coefs[j]).astype(bf16)], axis=1))
            acc_both[places[j]] += pulled[:, :ch]
            acc_new[places[j]] += pulled[:, ch:]
        return carry

    lax.fori_loop(0, blocks // nb, observe, 0)
    both_copy = pltpu.make_async_copy(acc_both, both_hbm, out_sems.at[rows // nr])
    both_copy.start()
    for c in later:
        c.wait()

    def pull(k, carry):
        flat = pl.ds(pl.multiple_of(k * step, step), step)
        adv = acc_new[pl.ds(k * nr, nr)].reshape(step, ch).astype(bf16)
        pre_grad = (dot(adv, w_out_t_ref[...]) * slope[flat, :].astype(f32)).astype(bf16)
        pre_grad_all[flat, :] = pre_grad
        pre_grad_copy(k).start()
        acc_in[...] += dot(xhat_t[:, flat], pre_grad)
        acc_out[...] += dot(act_t[:, flat], adv)
        return carry

    lax.fori_loop(0, rows // nr, pull, 0)
    put_chunks(sums_ref, 0, acc_in)
    put_chunks(sums_ref, 1, acc_out)
    put_chunks(sums_ref, 2, acc_head)
    left = acc_head.shape[0] * acc_head.shape[1] // (8 * 128)
    sums_ref[left:, 16:24, :] = jnp.zeros((sums_ref.shape[0] - left, 8, 128), bf16)
    both_copy.wait()
    for k in range(rows // nr):
        pre_grad_copy(k).wait()


def put_chunks(sums_ref, part, acc):
    down = acc.shape[0] // 8
    for j in range(acc.shape[1] // 128):
        tiles = acc[:, 128 * j : 128 * (j + 1)].reshape(down, 8, 128)
        sums_ref[down * j : down * (j + 1), 8 * part : 8 * part + 8, :] = tiles.astype(bf16)


def take_chunks(got_ref, part, shape):
    down = shape[0] // 8
    return jnp.concatenate(
        [
            got_ref[down * j : down * (j + 1), 8 * part : 8 * part + 8, :].astype(f32).reshape(shape[0], 128)
            for j in range(shape[1] // 128)
        ],
        axis=1,
    )


def decode(rows, got, stk, head, head_t, w_out_t, slope, act_t, xhat_t, chunks):
    nrow, two_cells, ch = stk.shape
    cells = two_cells // 2
    nv = head.shape[1]
    hid = w_out_t.shape[1]
    n = nrow * cells
    blocks = got.shape[0]
    dma = pltpu.SemaphoreType.DMA
    return pl.pallas_call(
        decode_kernel,
        out_shape=(
            pltpu.HBM((n, hid), bf16),
            pltpu.HBM((nrow, cells, ch), f32),
            pltpu.HBM((chunks, 24, 128), bf16),
        ),
        in_specs=[pl.BlockSpec(memory_space=pltpu.SMEM)] + [OUTSIDE] * 2 + [INSIDE] * 3 + [OUTSIDE] * 3,
        out_specs=(OUTSIDE, OUTSIDE, INSIDE),
        scratch_shapes=[pltpu.VMEM(x.shape, bf16) for x in (got, stk, slope, act_t, xhat_t, slope)]
        + [
            pltpu.VMEM((nrow, cells, ch), f32),
            pltpu.VMEM((nrow, cells, ch), f32),
            pltpu.VMEM((nv, ch), f32),
            pltpu.VMEM((ch, hid), f32),
            pltpu.VMEM((hid, ch), f32),
            dma((blocks // BLOCKS_STEP,)),
            dma((blocks,)),
            dma((3,)),
            dma((nrow // PULL_ROWS + 1,)),
        ],
        compiler_params=params(),
        cost_estimate=cost(10 * n * ch * hid, 24 * 2**20),
        name="decode",
    )(rows, *in_hbm(got, stk), head, head_t, w_out_t, *in_hbm(slope, act_t, xhat_t))


def backward_kernel(lat_ref, left_ref, right_ref, gain_ref, w_in_t_ref, pre_grad_ref, both_ref, out_ref, first_ref, last_ref):
    rows, cells, ch = lat_ref.shape
    xhat, inv = normalized(lat_ref[...].astype(f32), left_ref[...], right_ref[...])
    gained = dot(pre_grad_ref[...], w_in_t_ref[...]) * gain_ref[...]
    gained = gained.reshape(rows, cells, ch)
    summed_grad = inv * (gained - xhat * jnp.mean(gained * xhat, axis=-1, keepdims=True))
    out_ref[...] = both_ref[...] + mixed(summed_grad, jnp.zeros((), f32), jnp.zeros((), f32))
    first_ref[...] = summed_grad[:, 0:1, :]
    last_ref[...] = summed_grad[:, cells - 1 : cells, :]


def backward(latent, left, right, gain, w_in_t, pre_grad, both):
    rows, cells, ch = latent.shape
    hid = w_in_t.shape[0]
    step = ROWS_STEP * cells
    edge = pl.BlockSpec((ROWS_STEP, 1, ch), lambda i: (i, 0, 0))
    whole = pl.BlockSpec((ROWS_STEP, cells, ch), lambda i: (i, 0, 0))
    return pl.pallas_call(
        backward_kernel,
        grid=(rows // ROWS_STEP,),
        out_shape=(
            jax.ShapeDtypeStruct((rows, cells, ch), f32),
            jax.ShapeDtypeStruct((rows, 1, ch), f32),
            jax.ShapeDtypeStruct((rows, 1, ch), f32),
        ),
        in_specs=[
            whole,
            edge,
            edge,
            pl.BlockSpec((1, ch), lambda i: (0, 0)),
            pl.BlockSpec((hid, ch), lambda i: (0, 0)),
            pl.BlockSpec((step, hid), lambda i: (i, 0)),
            whole,
        ],
        out_specs=(whole, edge, edge),
        compiler_params=params(),
        cost_estimate=cost(2 * rows * cells * ch * hid, 16 * 2**20),
        name="backward",
    )(latent, left, right, gain, w_in_t, pre_grad, both)


def edges_kernel(left_ref, right_ref, grad_ref, out_ref):
    block = grad_ref[...]
    place = lax.broadcasted_iota(jnp.int32, block.shape, 1)
    at_start = pl.program_id(0) == 0
    add = 0.5 * jnp.where(at_start, left_ref[...], right_ref[...])
    hit = place == jnp.where(at_start, 0, block.shape[1] - 1)
    out_ref[...] = block + jnp.where(hit, add, 0.0)


def add_edges(grad, left, right):
    rows, cells, ch = grad.shape
    ends = pl.BlockSpec((rows, 8, ch), lambda i: (0, i * (cells // 8 - 1), 0))
    edge = pl.BlockSpec((rows, 1, ch), lambda i: (0, 0, 0))
    return pl.pallas_call(
        edges_kernel,
        grid=(2,),
        out_shape=jax.ShapeDtypeStruct(grad.shape, f32),
        in_specs=[edge, edge, ends],
        out_specs=ends,
        input_output_aliases={2: 0},
        compiler_params=params(),
        cost_estimate=cost(rows * 16 * ch, 2**20),
        name="edges",
    )(left, right, grad)


def total_kernel(got_ref, out_ref):
    total = jnp.sum(got_ref[...].astype(f32), axis=0, keepdims=True).astype(bf16)
    out_ref[...] = jnp.broadcast_to(total, out_ref.shape)


def total(got):
    return pl.pallas_call(
        total_kernel,
        out_shape=jax.ShapeDtypeStruct(got.shape, bf16),
        compiler_params=params(),
        cost_estimate=cost(got.size, 2 * got.size * 2),
        name="total",
    )(got)


def finish_kernel(got_ref, gain_ref, w_in_ref, in_ref, out_ref, gain_grad_ref, head_ref, *, devices):
    share = 1.0 / devices
    x = take_chunks(got_ref, 0, in_ref.shape) * share
    in_ref[...] = x * gain_ref[...]
    per_channel = jnp.sum(x * w_in_ref[...].astype(f32), axis=1, keepdims=True)
    gain_grad_ref[...] = jnp.broadcast_to(per_channel, (x.shape[0], 128)).T[0:1, :]
    out_ref[...] = take_chunks(got_ref, 1, out_ref.shape) * share
    head_ref[...] = (take_chunks(got_ref, 2, head_ref.shape[::-1]) * share).T


def finish(got, gain, w_in, head, devices):
    ch, hid = w_in.shape
    return pl.pallas_call(
        functools.partial(finish_kernel, devices=devices),
        out_shape=(
            jax.ShapeDtypeStruct((ch, hid), f32),
            jax.ShapeDtypeStruct((hid, ch), f32),
            jax.ShapeDtypeStruct((1, ch), f32),
            jax.ShapeDtypeStruct(head.shape, f32),
        ),
        compiler_params=params(),
        cost_estimate=cost(4 * ch * hid, 3 * 2**20),
        name="finish",
    )(got, gain.reshape(ch, 1), w_in)


def from_sides(first, last):
    count = lax.axis_size("lon")
    left = lax.ppermute(last, "lon", [(i, (i + 1) % count) for i in range(count)])
    right = lax.ppermute(first, "lon", [((i + 1) % count, i) for i in range(count)])
    return left, right


def body(latent, row_index, weights, slots, counts, targets, gain, w_in, w_out, head):
    both_axes = ("band", "lon")
    devices = lax.axis_size("band") * lax.axis_size("lon")
    cells = latent.shape[1]
    packed = pack(weights, targets, slots, counts)
    left, right = from_sides(latent[:, 0:1, :], latent[:, cells - 1 : cells, :])
    packed, left, right = lax.optimization_barrier((packed, left, right))
    got = lax.all_to_all(packed, "lon", 0, 0, tiled=True)
    left, right = left.astype(f32), right.astype(f32)
    gain_row = gain.reshape(1, -1)
    stk, slope, act_t, xhat_t = forward(latent, left, right, gain_row, w_in, w_out)
    pre_grad, both, sums = decode(row_index, got, stk, head, head.T, w_out.T, slope, act_t, xhat_t, devices)
    parts = lax.all_to_all(sums, both_axes, 0, 0, tiled=True)
    grad, first, last = backward(latent, left, right, gain_row, w_in.T, pre_grad, both)
    parts, first, last = lax.optimization_barrier((parts, first, last))
    grad_left, grad_right = from_sides(first.astype(bf16), last.astype(bf16))
    grad = add_edges(grad, grad_left.astype(f32), grad_right.astype(f32))
    chunks = lax.all_to_all(total(parts), both_axes, 0, 0, tiled=True)
    grad_in, grad_out, grad_gain, grad_head = finish(chunks, gain, w_in, head, devices)
    return grad, grad_in, grad_out, grad_gain.reshape(-1), grad_head


def solution(mesh):
    return jax.shard_map(
        body,
        mesh=mesh,
        in_specs=(
            P("band", "lon", None),
            P("band", "lon", None),
            P(("band", "lon"), None, None),
            P(("band", "lon"), None),
            P(("band", "lon")),
            P(("band", "lon"), None, None),
            P(),
            P(),
            P(),
            P(),
        ),
        out_specs=(P("band", "lon", None), P(), P(), P(), P()),
        check_vma=False,
    )
```

```python
import functools
import math

import jax
import jax.numpy as jnp
from jax import lax
from jax.experimental import pallas as pl
from jax.experimental.pallas import tpu as pltpu
from jax.sharding import PartitionSpec as P

WINDOW_SLOTS = 7
NORM_EPS = 1e-05
ROWS_STEP = 4
BLOCKS_STEP = 8
PULL_ROWS = 16
PACK_CHUNKS = 4
META = 8

f32 = jnp.float32
bf16 = jnp.bfloat16
INSIDE = pl.BlockSpec(memory_space=pltpu.VMEM)
OUTSIDE = pl.BlockSpec(memory_space=pltpu.HBM)


def dot(a, b):
    return jnp.dot(a, b, preferred_element_type=f32)


def dot_t(a, b):
    return lax.dot_general(a, b, (((0,), (0,)), ((), ())), preferred_element_type=f32)


def params(mib=48):
    return pltpu.CompilerParams(vmem_limit_bytes=mib * 2**20)


def in_hbm(*arrays):
    return [pltpu.with_memory_space_constraint(x, pltpu.HBM) for x in arrays]


def cost(flops, nbytes, trans=0):
    return pl.CostEstimate(flops=flops, bytes_accessed=nbytes, transcendentals=trans)


def pack_kernel(w_hbm, t_hbm, slot_hbm, count_hbm, out_hbm, buf, slots, counts, small_sems, in_sems, out_sems):
    blocks, obs = slots.shape
    nv = t_hbm.shape[1]
    n = blocks // PACK_CHUNKS
    small = [
        pltpu.make_async_copy(slot_hbm, slots, small_sems.at[0]),
        pltpu.make_async_copy(count_hbm, counts, small_sems.at[1]),
    ]
    arrive, leave = [], []
    for c in range(PACK_CHUNKS):
        here = pl.ds(c * n, n)
        arrive.append(
            (
                pltpu.make_async_copy(w_hbm.at[here], buf.at[here, pl.ds(0, obs), :], in_sems.at[2 * c]),
                pltpu.make_async_copy(t_hbm.at[here], buf.at[here, pl.ds(obs, nv), :], in_sems.at[2 * c + 1]),
            )
        )
        leave.append(pltpu.make_async_copy(buf.at[here], out_hbm.at[here], out_sems.at[c]))
    for c in small:
        c.start()
    for pair in arrive:
        for c in pair:
            c.start()
    for c in small:
        c.wait()
    coef = slots[...].astype(f32) / (WINDOW_SLOTS - 1)
    lane = lax.broadcasted_iota(jnp.int32, (META, obs), 1)
    row = lax.broadcasted_iota(jnp.int32, (META, obs), 0)
    for b in range(blocks):
        live = jnp.where(lane < counts[b], 1.0, 0.0)
        buf[b, obs + nv : obs + nv + META, :] = jnp.where(row == 0, coef[b : b + 1, :], live).astype(bf16)
    for pair, out in zip(arrive, leave):
        for c in pair:
            c.wait()
        out.start()
    for c in leave:
        c.wait()


def pack(weights, targets, slots, counts):
    blocks, obs, cells = weights.shape
    shape = (blocks, 2 * obs + META, cells)
    dma = pltpu.SemaphoreType.DMA
    return pl.pallas_call(
        pack_kernel,
        out_shape=pltpu.HBM(shape, bf16),
        in_specs=[OUTSIDE] * 4,
        out_specs=OUTSIDE,
        scratch_shapes=[
            pltpu.VMEM(shape, bf16),
            pltpu.VMEM(slots.shape, jnp.int32),
            pltpu.SMEM(counts.shape, jnp.int32),
            dma((2,)),
            dma((2 * PACK_CHUNKS,)),
            dma((PACK_CHUNKS,)),
        ],
        compiler_params=params(),
        cost_estimate=cost(1, 4 * 2**20),
        name="pack",
    )(*in_hbm(weights, targets, slots, counts))


def mixed(x, left, right):
    cells = x.shape[1]
    place = lax.broadcasted_iota(jnp.int32, x.shape, 1)
    from_left = jnp.where(place == 0, left, pltpu.roll(x, 1, 1))
    from_right = jnp.where(place == cells - 1, right, pltpu.roll(x, cells - 1, 1))
    return x + 0.5 * (from_left + from_right)


def normalized(lat, left, right):
    summed = mixed(lat, left, right)
    inv = lax.rsqrt(jnp.mean(summed * summed, axis=-1, keepdims=True) + NORM_EPS)
    return summed * inv, inv


def forward_kernel(lat_ref, left_ref, right_ref, gain_ref, w_in_ref, w_out_ref, stk_ref, slope_ref, act_t_ref, xhat_t_ref):
    rows, cells, ch = lat_ref.shape
    lat_b = lat_ref[...]
    lat = lat_b.astype(f32)
    xhat, _ = normalized(lat, left_ref[...], right_ref[...])
    xhat = xhat.reshape(rows * cells, ch)
    pre = dot((xhat * gain_ref[...]).astype(bf16), w_in_ref[...])
    sig = jax.nn.sigmoid(pre)
    act = pre * sig
    act_b = act.astype(bf16)
    slope_ref[...] = (sig * (1.0 + pre * (1.0 - sig))).astype(bf16)
    new = lat.reshape(rows * cells, ch) + dot(act_b, w_out_ref[...])
    stk_ref[:, 0:cells, :] = lat_b
    stk_ref[:, cells : 2 * cells, :] = new.astype(bf16).reshape(rows, cells, ch)
    act_t_ref[...] = act_b.T
    xhat_t_ref[...] = xhat.astype(bf16).T


def forward(latent, left, right, gain, w_in, w_out):
    rows, cells, ch = latent.shape
    hid = w_in.shape[1]
    n = rows * cells
    step = ROWS_STEP * cells
    return pl.pallas_call(
        forward_kernel,
        grid=(rows // ROWS_STEP,),
        out_shape=(
            pltpu.HBM((rows, 2 * cells, ch), bf16),
            pltpu.HBM((n, hid), bf16),
            pltpu.HBM((hid, n), bf16),
            pltpu.HBM((ch, n), bf16),
        ),
        in_specs=[
            pl.BlockSpec((ROWS_STEP, cells, ch), lambda i: (i, 0, 0)),
            pl.BlockSpec((ROWS_STEP, 1, ch), lambda i: (i, 0, 0)),
            pl.BlockSpec((ROWS_STEP, 1, ch), lambda i: (i, 0, 0)),
            pl.BlockSpec((1, ch), lambda i: (0, 0)),
            pl.BlockSpec((ch, hid), lambda i: (0, 0)),
            pl.BlockSpec((hid, ch), lambda i: (0, 0)),
        ],
        out_specs=(
            pl.BlockSpec((ROWS_STEP, 2 * cells, ch), lambda i: (i, 0, 0)),
            pl.BlockSpec((step, hid), lambda i: (i, 0)),
            pl.BlockSpec((hid, step), lambda i: (0, i)),
            pl.BlockSpec((ch, step), lambda i: (0, i)),
        ),
        compiler_params=params(),
        cost_estimate=cost(4 * n * ch * hid, 16 * 2**20, 2 * n * hid),
        name="forward",
    )(latent, left, right, gain, w_in, w_out)


def decode_kernel(
    rows_ref, got_hbm, stk_hbm, head_ref, head_t_ref, w_out_t_ref, slope_hbm, act_t_hbm, xhat_t_hbm,
    pre_grad_hbm, both_hbm, sums_ref,
    got, stk, slope, act_t, xhat_t, pre_grad_all, acc_both, acc_new, acc_head, acc_in, acc_out,
    got_sems, stk_sems, in_sems, out_sems,
):
    nb, nr = BLOCKS_STEP, PULL_ROWS
    blocks = got.shape[0]
    ch, nv = head_ref.shape
    obs = (got.shape[1] - META) // 2
    rows, cells, _ = acc_both.shape
    scale = 1.0 / math.sqrt(obs)
    step = nr * cells

    def got_copy(i):
        here = pl.ds(i * nb, nb)
        return pltpu.make_async_copy(got_hbm.at[here], got.at[here], got_sems.at[i])

    def stk_copy(b):
        return pltpu.make_async_copy(stk_hbm.at[rows_ref[0, 0, b]], stk.at[b], stk_sems.at[b])

    def pre_grad_copy(k):
        flat = pl.ds(pl.multiple_of(k * step, step), step)
        return pltpu.make_async_copy(pre_grad_all.at[flat], pre_grad_hbm.at[flat], out_sems.at[k])

    for i in range(blocks // nb):
        got_copy(i).start()
        for j in range(nb):
            stk_copy(i * nb + j).start()
    later = [
        pltpu.make_async_copy(src, dst, in_sems.at[i])
        for i, (src, dst) in enumerate(((slope_hbm, slope), (xhat_t_hbm, xhat_t), (act_t_hbm, act_t)))
    ]
    for c in later:
        c.start()
    for acc in (acc_both, acc_new, acc_head, acc_in, acc_out):
        acc[...] = jnp.zeros_like(acc)

    def observe(i, carry):
        first = i * nb
        got_copy(i).wait()
        for j in range(nb):
            stk_copy(first + j).wait()
        places = [rows_ref[0, 0, first + j] for j in range(nb)]
        latents, coefs, lives = [], [], []
        for j in range(nb):
            meta = got[first + j, 2 * obs : 2 * obs + META, :].astype(f32).T
            t, live = meta[:, 0:1], meta[:, 1:2]
            w = got[first + j, 0:obs, :].astype(f32)
            pair = jnp.concatenate([(w * (1.0 - t)).astype(bf16), (w * t).astype(bf16)], axis=1)
            latents.append(dot(pair, stk[first + j]).astype(bf16))
            coefs.append(t)
            lives.append(live)
        obs_latent = jnp.concatenate(latents, axis=0)
        pred = dot(obs_latent, head_ref[...])
        goals = jnp.concatenate([got[first + j, obs : 2 * obs, :] for j in range(nb)], axis=0)
        live = jnp.concatenate(lives, axis=0)
        residual = jnp.where(live > 0.5, pred - goals.astype(f32), 0.0)
        pred_grad = (residual * scale).astype(bf16)
        acc_head[...] += dot_t(pred_grad, obs_latent)
        grad = dot(pred_grad, head_t_ref[...])
        for j in range(nb):
            g = grad[j * obs : (j + 1) * obs, :]
            w = got[first + j, 0:obs, :]
            pulled = dot_t(w, jnp.concatenate([g.astype(bf16), (g * coefs[j]).astype(bf16)], axis=1))
            acc_both[places[j]] += pulled[:, :ch]
            acc_new[places[j]] += pulled[:, ch:]
        return carry

    lax.fori_loop(0, blocks // nb, observe, 0)
    both_copy = pltpu.make_async_copy(acc_both, both_hbm, out_sems.at[rows // nr])
    both_copy.start()
    for c in later:
        c.wait()

    def pull(k, carry):
        flat = pl.ds(pl.multiple_of(k * step, step), step)
        adv = acc_new[pl.ds(k * nr, nr)].reshape(step, ch).astype(bf16)
        pre_grad = (dot(adv, w_out_t_ref[...]) * slope[flat, :].astype(f32)).astype(bf16)
        pre_grad_all[flat, :] = pre_grad
        pre_grad_copy(k).start()
        acc_in[...] += dot(xhat_t[:, flat], pre_grad)
        acc_out[...] += dot(act_t[:, flat], adv)
        return carry

    lax.fori_loop(0, rows // nr, pull, 0)
    put_chunks(sums_ref, 0, acc_in)
    put_chunks(sums_ref, 1, acc_out)
    put_chunks(sums_ref, 2, acc_head)
    left = acc_head.shape[0] * acc_head.shape[1] // (8 * 128)
    sums_ref[left:, 16:24, :] = jnp.zeros((sums_ref.shape[0] - left, 8, 128), bf16)
    both_copy.wait()
    for k in range(rows // nr):
        pre_grad_copy(k).wait()


def put_chunks(sums_ref, part, acc):
    down = acc.shape[0] // 8
    for j in range(acc.shape[1] // 128):
        tiles = acc[:, 128 * j : 128 * (j + 1)].reshape(down, 8, 128)
        sums_ref[down * j : down * (j + 1), 8 * part : 8 * part + 8, :] = tiles.astype(bf16)


def take_chunks(got_ref, part, shape):
    down = shape[0] // 8
    return jnp.concatenate(
        [
            got_ref[down * j : down * (j + 1), 8 * part : 8 * part + 8, :].astype(f32).reshape(shape[0], 128)
            for j in range(shape[1] // 128)
        ],
        axis=1,
    )


def decode(rows, got, stk, head, head_t, w_out_t, slope, act_t, xhat_t, chunks):
    nrow, two_cells, ch = stk.shape
    cells = two_cells // 2
    nv = head.shape[1]
    hid = w_out_t.shape[1]
    n = nrow * cells
    blocks = got.shape[0]
    dma = pltpu.SemaphoreType.DMA
    return pl.pallas_call(
        decode_kernel,
        out_shape=(
            pltpu.HBM((n, hid), bf16),
            pltpu.HBM((nrow, cells, ch), f32),
            pltpu.HBM((chunks, 24, 128), bf16),
        ),
        in_specs=[pl.BlockSpec(memory_space=pltpu.SMEM)] + [OUTSIDE] * 2 + [INSIDE] * 3 + [OUTSIDE] * 3,
        out_specs=(OUTSIDE, OUTSIDE, INSIDE),
        scratch_shapes=[pltpu.VMEM(x.shape, bf16) for x in (got, stk, slope, act_t, xhat_t, slope)]
        + [
            pltpu.VMEM((nrow, cells, ch), f32),
            pltpu.VMEM((nrow, cells, ch), f32),
            pltpu.VMEM((nv, ch), f32),
            pltpu.VMEM((ch, hid), f32),
            pltpu.VMEM((hid, ch), f32),
            dma((blocks // BLOCKS_STEP,)),
            dma((blocks,)),
            dma((3,)),
            dma((nrow // PULL_ROWS + 1,)),
        ],
        compiler_params=params(),
        cost_estimate=cost(10 * n * ch * hid, 24 * 2**20),
        name="decode",
    )(rows, *in_hbm(got, stk), head, head_t, w_out_t, *in_hbm(slope, act_t, xhat_t))


def backward_kernel(lat_ref, left_ref, right_ref, gain_ref, w_in_t_ref, pre_grad_ref, both_ref, out_ref, first_ref, last_ref):
    rows, cells, ch = lat_ref.shape
    xhat, inv = normalized(lat_ref[...].astype(f32), left_ref[...], right_ref[...])
    gained = dot(pre_grad_ref[...], w_in_t_ref[...]) * gain_ref[...]
    gained = gained.reshape(rows, cells, ch)
    summed_grad = inv * (gained - xhat * jnp.mean(gained * xhat, axis=-1, keepdims=True))
    out_ref[...] = both_ref[...] + mixed(summed_grad, jnp.zeros((), f32), jnp.zeros((), f32))
    first_ref[...] = summed_grad[:, 0:1, :]
    last_ref[...] = summed_grad[:, cells - 1 : cells, :]


def backward(latent, left, right, gain, w_in_t, pre_grad, both):
    rows, cells, ch = latent.shape
    hid = w_in_t.shape[0]
    step = ROWS_STEP * cells
    edge = pl.BlockSpec((ROWS_STEP, 1, ch), lambda i: (i, 0, 0))
    whole = pl.BlockSpec((ROWS_STEP, cells, ch), lambda i: (i, 0, 0))
    return pl.pallas_call(
        backward_kernel,
        grid=(rows // ROWS_STEP,),
        out_shape=(
            jax.ShapeDtypeStruct((rows, cells, ch), f32),
            jax.ShapeDtypeStruct((rows, 1, ch), f32),
            jax.ShapeDtypeStruct((rows, 1, ch), f32),
        ),
        in_specs=[
            whole,
            edge,
            edge,
            pl.BlockSpec((1, ch), lambda i: (0, 0)),
            pl.BlockSpec((hid, ch), lambda i: (0, 0)),
            pl.BlockSpec((step, hid), lambda i: (i, 0)),
            whole,
        ],
        out_specs=(whole, edge, edge),
        compiler_params=params(),
        cost_estimate=cost(2 * rows * cells * ch * hid, 16 * 2**20),
        name="backward",
    )(latent, left, right, gain, w_in_t, pre_grad, both)


def edges_kernel(left_ref, right_ref, grad_ref, out_ref):
    block = grad_ref[...]
    place = lax.broadcasted_iota(jnp.int32, block.shape, 1)
    at_start = pl.program_id(0) == 0
    add = 0.5 * jnp.where(at_start, left_ref[...], right_ref[...])
    hit = place == jnp.where(at_start, 0, block.shape[1] - 1)
    out_ref[...] = block + jnp.where(hit, add, 0.0)


def add_edges(grad, left, right):
    rows, cells, ch = grad.shape
    ends = pl.BlockSpec((rows, 8, ch), lambda i: (0, i * (cells // 8 - 1), 0))
    edge = pl.BlockSpec((rows, 1, ch), lambda i: (0, 0, 0))
    return pl.pallas_call(
        edges_kernel,
        grid=(2,),
        out_shape=jax.ShapeDtypeStruct(grad.shape, f32),
        in_specs=[edge, edge, ends],
        out_specs=ends,
        input_output_aliases={2: 0},
        compiler_params=params(),
        cost_estimate=cost(rows * 16 * ch, 2**20),
        name="edges",
    )(left, right, grad)


def total_kernel(got_ref, out_ref):
    total = jnp.sum(got_ref[...].astype(f32), axis=0, keepdims=True).astype(bf16)
    out_ref[...] = jnp.broadcast_to(total, out_ref.shape)


def total(got):
    return pl.pallas_call(
        total_kernel,
        out_shape=jax.ShapeDtypeStruct(got.shape, bf16),
        compiler_params=params(),
        cost_estimate=cost(got.size, 2 * got.size * 2),
        name="total",
    )(got)


def finish_kernel(got_ref, gain_ref, w_in_ref, in_ref, out_ref, gain_grad_ref, head_ref, *, devices):
    share = 1.0 / devices
    x = take_chunks(got_ref, 0, in_ref.shape) * share
    in_ref[...] = x * gain_ref[...]
    per_channel = jnp.sum(x * w_in_ref[...].astype(f32), axis=1, keepdims=True)
    gain_grad_ref[...] = jnp.broadcast_to(per_channel, (x.shape[0], 128)).T[0:1, :]
    out_ref[...] = take_chunks(got_ref, 1, out_ref.shape) * share
    head_ref[...] = (take_chunks(got_ref, 2, head_ref.shape[::-1]) * share).T


def finish(got, gain, w_in, head, devices):
    ch, hid = w_in.shape
    return pl.pallas_call(
        functools.partial(finish_kernel, devices=devices),
        out_shape=(
            jax.ShapeDtypeStruct((ch, hid), f32),
            jax.ShapeDtypeStruct((hid, ch), f32),
            jax.ShapeDtypeStruct((1, ch), f32),
            jax.ShapeDtypeStruct(head.shape, f32),
        ),
        compiler_params=params(),
        cost_estimate=cost(4 * ch * hid, 3 * 2**20),
        name="finish",
    )(got, gain.reshape(ch, 1), w_in)


def from_sides(first, last):
    count = lax.axis_size("lon")
    left = lax.ppermute(last, "lon", [(i, (i + 1) % count) for i in range(count)])
    right = lax.ppermute(first, "lon", [((i + 1) % count, i) for i in range(count)])
    return left, right


def body(latent, row_index, weights, slots, counts, targets, gain, w_in, w_out, head):
    both_axes = ("band", "lon")
    devices = lax.axis_size("band") * lax.axis_size("lon")
    cells = latent.shape[1]
    packed = pack(weights, targets, slots, counts)
    left, right = from_sides(latent[:, 0:1, :], latent[:, cells - 1 : cells, :])
    packed, left, right = lax.optimization_barrier((packed, left, right))
    got = lax.all_to_all(packed, "lon", 0, 0, tiled=True)
    left, right = left.astype(f32), right.astype(f32)
    gain_row = gain.reshape(1, -1)
    stk, slope, act_t, xhat_t = forward(latent, left, right, gain_row, w_in, w_out)
    pre_grad, both, sums = decode(row_index, got, stk, head, head.T, w_out.T, slope, act_t, xhat_t, devices)
    parts = lax.all_to_all(sums, both_axes, 0, 0, tiled=True)
    grad, first, last = backward(latent, left, right, gain_row, w_in.T, pre_grad, both)
    parts, first, last = lax.optimization_barrier((parts, first, last))
    grad_left, grad_right = from_sides(first.astype(bf16), last.astype(bf16))
    grad = add_edges(grad, grad_left.astype(f32), grad_right.astype(f32))
    chunks = lax.all_to_all(total(parts), both_axes, 0, 0, tiled=True)
    grad_in, grad_out, grad_gain, grad_head = finish(chunks, gain, w_in, head, devices)
    return grad, grad_in, grad_out, grad_gain.reshape(-1), grad_head


def solution(mesh):
    return jax.shard_map(
        body,
        mesh=mesh,
        in_specs=(
            P("band", "lon", None),
            P("band", "lon", None),
            P(("band", "lon"), None, None),
            P(("band", "lon"), None),
            P(("band", "lon")),
            P(("band", "lon"), None, None),
            P(),
            P(),
            P(),
            P(),
        ),
        out_specs=(P("band", "lon", None), P(), P(), P(), P()),
        check_vma=False,
    )
```

```python
import functools
import math

import jax
import jax.numpy as jnp
from jax import lax
from jax.experimental import pallas as pl
from jax.experimental.pallas import tpu as pltpu
from jax.sharding import PartitionSpec as P

WINDOW_SLOTS = 7
NORM_EPS = 1e-05
ROWS_STEP = 4
BLOCKS_STEP = 8
PULL_ROWS = 16
PACK_CHUNKS = 4
META = 8

f32 = jnp.float32
bf16 = jnp.bfloat16
INSIDE = pl.BlockSpec(memory_space=pltpu.VMEM)
OUTSIDE = pl.BlockSpec(memory_space=pltpu.HBM)


def dot(a, b):
    return jnp.dot(a, b, preferred_element_type=f32)


def dot_t(a, b):
    return lax.dot_general(a, b, (((0,), (0,)), ((), ())), preferred_element_type=f32)


def params(mib=48):
    return pltpu.CompilerParams(vmem_limit_bytes=mib * 2**20)


def in_hbm(*arrays):
    return [pltpu.with_memory_space_constraint(x, pltpu.HBM) for x in arrays]


def cost(flops, nbytes, trans=0):
    return pl.CostEstimate(flops=flops, bytes_accessed=nbytes, transcendentals=trans)


def pack_kernel(w_hbm, t_hbm, slot_hbm, count_hbm, out_hbm, buf, slots, counts, small_sems, in_sems, out_sems):
    blocks, obs = slots.shape
    nv = t_hbm.shape[1]
    n = blocks // PACK_CHUNKS
    small = [
        pltpu.make_async_copy(slot_hbm, slots, small_sems.at[0]),
        pltpu.make_async_copy(count_hbm, counts, small_sems.at[1]),
    ]
    arrive, leave = [], []
    for c in range(PACK_CHUNKS):
        here = pl.ds(c * n, n)
        arrive.append(
            (
                pltpu.make_async_copy(w_hbm.at[here], buf.at[here, pl.ds(0, obs), :], in_sems.at[2 * c]),
                pltpu.make_async_copy(t_hbm.at[here], buf.at[here, pl.ds(obs, nv), :], in_sems.at[2 * c + 1]),
            )
        )
        leave.append(pltpu.make_async_copy(buf.at[here], out_hbm.at[here], out_sems.at[c]))
    for c in small:
        c.start()
    for pair in arrive:
        for c in pair:
            c.start()
    for c in small:
        c.wait()
    coef = slots[...].astype(f32) / (WINDOW_SLOTS - 1)
    lane = lax.broadcasted_iota(jnp.int32, (META, obs), 1)
    row = lax.broadcasted_iota(jnp.int32, (META, obs), 0)
    for b in range(blocks):
        live = jnp.where(lane < counts[b], 1.0, 0.0)
        buf[b, obs + nv : obs + nv + META, :] = jnp.where(row == 0, coef[b : b + 1, :], live).astype(bf16)
    for pair, out in zip(arrive, leave):
        for c in pair:
            c.wait()
        out.start()
    for c in leave:
        c.wait()


def pack(weights, targets, slots, counts):
    blocks, obs, cells = weights.shape
    shape = (blocks, 2 * obs + META, cells)
    dma = pltpu.SemaphoreType.DMA
    return pl.pallas_call(
        pack_kernel,
        out_shape=pltpu.HBM(shape, bf16),
        in_specs=[OUTSIDE] * 4,
        out_specs=OUTSIDE,
        scratch_shapes=[
            pltpu.VMEM(shape, bf16),
            pltpu.VMEM(slots.shape, jnp.int32),
            pltpu.SMEM(counts.shape, jnp.int32),
            dma((2,)),
            dma((2 * PACK_CHUNKS,)),
            dma((PACK_CHUNKS,)),
        ],
        compiler_params=params(),
        cost_estimate=cost(1, 4 * 2**20),
        name="pack",
    )(*in_hbm(weights, targets, slots, counts))


def mixed(x, left, right):
    cells = x.shape[1]
    place = lax.broadcasted_iota(jnp.int32, x.shape, 1)
    from_left = jnp.where(place == 0, left, pltpu.roll(x, 1, 1))
    from_right = jnp.where(place == cells - 1, right, pltpu.roll(x, cells - 1, 1))
    return x + 0.5 * (from_left + from_right)


def normalized(lat, left, right):
    summed = mixed(lat, left, right)
    inv = lax.rsqrt(jnp.mean(summed * summed, axis=-1, keepdims=True) + NORM_EPS)
    return summed * inv, inv


def forward_kernel(lat_ref, left_ref, right_ref, gain_ref, w_in_ref, w_out_ref, stk_ref, slope_ref, act_t_ref, xhat_t_ref):
    rows, cells, ch = lat_ref.shape
    lat_b = lat_ref[...]
    lat = lat_b.astype(f32)
    xhat, _ = normalized(lat, left_ref[...], right_ref[...])
    xhat = xhat.reshape(rows * cells, ch)
    pre = dot((xhat * gain_ref[...]).astype(bf16), w_in_ref[...])
    sig = jax.nn.sigmoid(pre)
    act = pre * sig
    act_b = act.astype(bf16)
    slope_ref[...] = (sig * (1.0 + pre * (1.0 - sig))).astype(bf16)
    new = lat.reshape(rows * cells, ch) + dot(act_b, w_out_ref[...])
    stk_ref[:, 0:cells, :] = lat_b
    stk_ref[:, cells : 2 * cells, :] = new.astype(bf16).reshape(rows, cells, ch)
    act_t_ref[...] = act_b.T
    xhat_t_ref[...] = xhat.astype(bf16).T


def forward(latent, left, right, gain, w_in, w_out):
    rows, cells, ch = latent.shape
    hid = w_in.shape[1]
    n = rows * cells
    step = ROWS_STEP * cells
    return pl.pallas_call(
        forward_kernel,
        grid=(rows // ROWS_STEP,),
        out_shape=(
            pltpu.HBM((rows, 2 * cells, ch), bf16),
            pltpu.HBM((n, hid), bf16),
            pltpu.HBM((hid, n), bf16),
            pltpu.HBM((ch, n), bf16),
        ),
        in_specs=[
            pl.BlockSpec((ROWS_STEP, cells, ch), lambda i: (i, 0, 0)),
            pl.BlockSpec((ROWS_STEP, 1, ch), lambda i: (i, 0, 0)),
            pl.BlockSpec((ROWS_STEP, 1, ch), lambda i: (i, 0, 0)),
            pl.BlockSpec((1, ch), lambda i: (0, 0)),
            pl.BlockSpec((ch, hid), lambda i: (0, 0)),
            pl.BlockSpec((hid, ch), lambda i: (0, 0)),
        ],
        out_specs=(
            pl.BlockSpec((ROWS_STEP, 2 * cells, ch), lambda i: (i, 0, 0)),
            pl.BlockSpec((step, hid), lambda i: (i, 0)),
            pl.BlockSpec((hid, step), lambda i: (0, i)),
            pl.BlockSpec((ch, step), lambda i: (0, i)),
        ),
        compiler_params=params(),
        cost_estimate=cost(4 * n * ch * hid, 16 * 2**20, 2 * n * hid),
        name="forward",
    )(latent, left, right, gain, w_in, w_out)


def decode_kernel(
    core_ref, rows_ref, got_hbm, stk_hbm, head_ref, head_t_ref, w_out_t_ref, slope_hbm, act_t_hbm, xhat_t_hbm,
    adv_hbm, both_hbm, keep_ref, send_ref,
    got, stk, slope, act_t, xhat_t, adv_all, acc_both, acc_new, acc_head, acc_in, acc_out,
    got_sems, stk_sems, in_sems, out_sems,
):
    nb, nr = BLOCKS_STEP, PULL_ROWS
    blocks = got.shape[0]
    ch, nv = head_ref.shape
    obs = (got.shape[1] - META) // 2
    rows, cells, _ = acc_both.shape
    scale = 1.0 / math.sqrt(obs)
    step = nr * cells

    def got_copy(i):
        here = pl.ds(i * nb, nb)
        return pltpu.make_async_copy(got_hbm.at[here], got.at[here], got_sems.at[i])

    def stk_copy(b):
        return pltpu.make_async_copy(stk_hbm.at[rows_ref[0, 0, b]], stk.at[b], stk_sems.at[b])

    def adv_copy(k):
        flat = pl.ds(pl.multiple_of(k * step, step), step)
        return pltpu.make_async_copy(adv_all.at[flat], adv_hbm.at[flat], out_sems.at[k])

    later = [
        pltpu.make_async_copy(src, dst, in_sems.at[i])
        for i, (src, dst) in enumerate(((slope_hbm, slope), (xhat_t_hbm, xhat_t), (act_t_hbm, act_t)))
    ]
    for i in range(blocks // nb):
        got_copy(i).start()
        for j in range(nb):
            stk_copy(i * nb + j).start()
    for acc in (acc_both, acc_new, acc_head, acc_in, acc_out):
        acc[...] = jnp.zeros_like(acc)

    def observe(i, carry):
        first = i * nb
        got_copy(i).wait()
        for j in range(nb):
            stk_copy(first + j).wait()

        @pl.when(i == 0)
        def _():
            for c in later:
                c.start()

        places = [rows_ref[0, 0, first + j] for j in range(nb)]
        meta = jnp.concatenate([got[first + j, 2 * obs : 2 * obs + META, :].astype(f32) for j in range(nb)], axis=0).T
        latents, coefs, lives = [], [], []
        for j in range(nb):
            t, live = meta[:, META * j : META * j + 1], meta[:, META * j + 1 : META * j + 2]
            w = got[first + j, 0:obs, :]
            w_new = w * jnp.broadcast_to(t, w.shape).astype(bf16)
            latents.append(dot(jnp.concatenate([w - w_new, w_new], axis=1), stk[first + j]).astype(bf16))
            coefs.append(t)
            lives.append(live)
        obs_latent = jnp.concatenate(latents, axis=0)
        pred = dot(obs_latent, head_ref[...])
        goals = jnp.concatenate([got[first + j, obs : 2 * obs, :] for j in range(nb)], axis=0)
        live = jnp.concatenate(lives, axis=0)
        residual = jnp.where(live > 0.5, pred - goals.astype(f32), 0.0)
        pred_grad = (residual * scale).astype(bf16)
        acc_head[...] += dot_t(pred_grad, obs_latent)
        grad = dot(pred_grad, head_t_ref[...])
        for j in range(nb):
            g = grad[j * obs : (j + 1) * obs, :]
            w = got[first + j, 0:obs, :]
            pulled = dot_t(w, jnp.concatenate([g.astype(bf16), (g * coefs[j]).astype(bf16)], axis=1))
            acc_both[places[j]] += pulled[:, :ch]
            acc_new[places[j]] += pulled[:, ch:]
        return carry

    lax.fori_loop(0, blocks // nb, observe, 0)
    both_copy = pltpu.make_async_copy(acc_both, both_hbm, out_sems.at[rows // nr])
    both_copy.start()
    for c in later:
        c.wait()

    def pull(k, carry):
        flat = pl.ds(pl.multiple_of(k * step, step), step)
        adv = acc_new[pl.ds(k * nr, nr)].reshape(step, ch).astype(bf16)
        adv_all[flat, :] = adv
        adv_copy(k).start()
        pre_grad = (dot(adv, w_out_t_ref[...]) * slope[flat, :].astype(f32)).astype(bf16)
        acc_in[...] += dot(xhat_t[:, flat], pre_grad)
        acc_out[...] += dot(act_t[:, flat], adv)
        return carry

    lax.fori_loop(0, rows // nr, pull, 0)
    for core in range(2):

        @pl.when(core_ref[0] == core)
        def _(core=core):
            put_chunks(keep_ref, core, acc_in, acc_out, acc_head)
            put_chunks(send_ref, 1 - core, acc_in, acc_out, acc_head)

    both_copy.wait()
    for k in range(rows // nr):
        adv_copy(k).wait()


def put_chunks(ref, half, *accs):
    for p, acc in enumerate(accs):
        down = acc.shape[0] // 8
        across = acc.shape[1] // 256
        for j in range(across):
            at = 128 * (half * across + j)
            tiles = acc[:, at : at + 128].reshape(down, 8, 128)
            ref[down * j : down * (j + 1), 8 * p : 8 * p + 8, :] = tiles.astype(ref.dtype)
        if down * across < ref.shape[0]:
            rest = ref.shape[0] - down * across
            ref[down * across :, 8 * p : 8 * p + 8, :] = jnp.zeros((rest, 8, 128), ref.dtype)


def take_chunks(halves, part, shape):
    down = shape[0] // 8
    across = shape[1] // 256
    return jnp.concatenate(
        [
            half[down * j : down * (j + 1), 8 * part : 8 * part + 8, :].reshape(shape[0], 128)
            for half in halves
            for j in range(across)
        ],
        axis=1,
    )


def decode(core, rows, got, stk, head, head_t, w_out_t, slope, act_t, xhat_t, chunks):
    nrow, two_cells, ch = stk.shape
    cells = two_cells // 2
    nv = head.shape[1]
    hid = w_out_t.shape[1]
    n = nrow * cells
    blocks = got.shape[0]
    dma = pltpu.SemaphoreType.DMA
    scalars = pl.BlockSpec(memory_space=pltpu.SMEM)
    return pl.pallas_call(
        decode_kernel,
        out_shape=(
            pltpu.HBM((n, ch), bf16),
            pltpu.HBM((nrow, cells, ch), f32),
            jax.ShapeDtypeStruct((chunks, 24, 128), f32),
            jax.ShapeDtypeStruct((chunks, 24, 128), bf16),
        ),
        in_specs=[scalars] * 2 + [OUTSIDE] * 2 + [INSIDE] * 3 + [OUTSIDE] * 3,
        out_specs=(OUTSIDE, OUTSIDE, INSIDE, INSIDE),
        scratch_shapes=[pltpu.VMEM(x.shape, bf16) for x in (got, stk, slope, act_t, xhat_t)]
        + [
            pltpu.VMEM((n, ch), bf16),
            pltpu.VMEM((nrow, cells, ch), f32),
            pltpu.VMEM((nrow, cells, ch), f32),
            pltpu.VMEM((nv, ch), f32),
            pltpu.VMEM((ch, hid), f32),
            pltpu.VMEM((hid, ch), f32),
            dma((blocks // BLOCKS_STEP,)),
            dma((blocks,)),
            dma((3,)),
            dma((nrow // PULL_ROWS + 1,)),
        ],
        compiler_params=params(),
        cost_estimate=cost(10 * n * ch * hid, 24 * 2**20),
        name="decode",
    )(core, rows, *in_hbm(got, stk), head, head_t, w_out_t, *in_hbm(slope, act_t, xhat_t))


def backward_kernel(
    lat_ref, left_ref, right_ref, gain_ref, w_in_t_ref, w_out_t_ref, adv_ref, slope_ref, both_ref, out_ref, first_ref, last_ref
):
    rows, cells, ch = lat_ref.shape
    xhat, inv = normalized(lat_ref[...].astype(f32), left_ref[...], right_ref[...])
    pre_grad = (dot(adv_ref[...], w_out_t_ref[...]) * slope_ref[...].astype(f32)).astype(bf16)
    gained = dot(pre_grad, w_in_t_ref[...]) * gain_ref[...]
    gained = gained.reshape(rows, cells, ch)
    summed_grad = inv * (gained - xhat * jnp.mean(gained * xhat, axis=-1, keepdims=True))
    out_ref[...] = both_ref[...] + mixed(summed_grad, jnp.zeros((), f32), jnp.zeros((), f32))
    first_ref[...] = summed_grad[:, 0:1, :]
    last_ref[...] = summed_grad[:, cells - 1 : cells, :]


def backward(latent, left, right, gain, w_in_t, w_out_t, adv, slope, both):
    rows, cells, ch = latent.shape
    hid = w_in_t.shape[0]
    step = ROWS_STEP * cells
    edge = pl.BlockSpec((ROWS_STEP, 1, ch), lambda i: (i, 0, 0))
    whole = pl.BlockSpec((ROWS_STEP, cells, ch), lambda i: (i, 0, 0))
    return pl.pallas_call(
        backward_kernel,
        grid=(rows // ROWS_STEP,),
        out_shape=(
            jax.ShapeDtypeStruct((rows, cells, ch), f32),
            jax.ShapeDtypeStruct((rows, 1, ch), f32),
            jax.ShapeDtypeStruct((rows, 1, ch), f32),
        ),
        in_specs=[
            whole,
            edge,
            edge,
            pl.BlockSpec((1, ch), lambda i: (0, 0)),
            pl.BlockSpec((hid, ch), lambda i: (0, 0)),
            pl.BlockSpec((ch, hid), lambda i: (0, 0)),
            pl.BlockSpec((step, ch), lambda i: (i, 0)),
            pl.BlockSpec((step, hid), lambda i: (i, 0)),
            whole,
        ],
        out_specs=(whole, edge, edge),
        compiler_params=params(),
        cost_estimate=cost(4 * rows * cells * ch * hid, 16 * 2**20),
        name="backward",
    )(latent, left, right, gain, w_in_t, w_out_t, *in_hbm(adv, slope, both))


def edges_kernel(left_ref, right_ref, grad_ref, out_ref):
    block = grad_ref[...]
    place = lax.broadcasted_iota(jnp.int32, block.shape, 1)
    at_start = pl.program_id(0) == 0
    add = 0.5 * jnp.where(at_start, left_ref[...], right_ref[...])
    hit = place == jnp.where(at_start, 0, block.shape[1] - 1)
    out_ref[...] = block + jnp.where(hit, add, 0.0)


def add_edges(grad, left, right):
    rows, cells, ch = grad.shape
    ends = pl.BlockSpec((rows, 8, ch), lambda i: (0, i * (cells // 8 - 1), 0))
    edge = pl.BlockSpec((rows, 1, ch), lambda i: (0, 0, 0))
    return pl.pallas_call(
        edges_kernel,
        grid=(2,),
        out_shape=jax.ShapeDtypeStruct(grad.shape, f32),
        in_specs=[edge, edge, ends],
        out_specs=ends,
        input_output_aliases={2: 0},
        compiler_params=params(),
        cost_estimate=cost(rows * 16 * ch, 2**20),
        name="edges",
    )(left, right, grad)


def total_kernel(got_ref, out_ref):
    total = jnp.sum(got_ref[...].astype(f32), axis=0, keepdims=True).astype(bf16)
    out_ref[...] = jnp.broadcast_to(total, out_ref.shape)


def total(got):
    return pl.pallas_call(
        total_kernel,
        out_shape=jax.ShapeDtypeStruct(got.shape, bf16),
        compiler_params=params(),
        cost_estimate=cost(got.size, 2 * got.size * 2),
        name="total",
    )(got)


def pair_kernel(keep_ref, came_ref, out_ref):
    out_ref[...] = (keep_ref[...] + came_ref[...].astype(f32)).astype(bf16)


def pair(keep, came):
    return pl.pallas_call(
        pair_kernel,
        out_shape=jax.ShapeDtypeStruct(keep.shape, bf16),
        compiler_params=params(),
        cost_estimate=cost(keep.size, 8 * keep.size),
        name="pair",
    )(keep, came)


def finish_kernel(core_ref, mine_ref, other_ref, gain_ref, w_in_ref, in_ref, out_ref, gain_grad_ref, head_ref, *, devices):
    share = 1.0 / devices
    for core in range(2):

        @pl.when(core_ref[0] == core)
        def _(core=core):
            pair = (mine_ref, other_ref) if core == 0 else (other_ref, mine_ref)
            halves = [ref[...].astype(f32) * share for ref in pair]
            x = take_chunks(halves, 0, in_ref.shape)
            in_ref[...] = x * gain_ref[...]
            per_channel = jnp.sum(x * w_in_ref[...].astype(f32), axis=1, keepdims=True)
            gain_grad_ref[...] = jnp.broadcast_to(per_channel, (x.shape[0], 128)).T[0:1, :]
            out_ref[...] = take_chunks(halves, 1, out_ref.shape)
            head_ref[...] = take_chunks(halves, 2, head_ref.shape[::-1]).T


def finish(core, mine, other, gain, w_in, head, devices):
    ch, hid = w_in.shape
    return pl.pallas_call(
        functools.partial(finish_kernel, devices=devices),
        out_shape=(
            jax.ShapeDtypeStruct((ch, hid), f32),
            jax.ShapeDtypeStruct((hid, ch), f32),
            jax.ShapeDtypeStruct((1, ch), f32),
            jax.ShapeDtypeStruct(head.shape, f32),
        ),
        in_specs=[pl.BlockSpec(memory_space=pltpu.SMEM)] + [INSIDE] * 4,
        out_specs=(INSIDE,) * 4,
        compiler_params=params(),
        cost_estimate=cost(4 * ch * hid, 3 * 2**20),
        name="finish",
    )(core, mine, other, gain.reshape(ch, 1), w_in)


LON = ("chip", "core")


def from_sides(first, last):
    count = lax.axis_size("chip") * lax.axis_size("core")
    left = lax.ppermute(last, LON, [(i, (i + 1) % count) for i in range(count)])
    right = lax.ppermute(first, LON, [((i + 1) % count, i) for i in range(count)])
    return left, right


def body(latent, row_index, weights, slots, counts, targets, gain, w_in, w_out, head):
    chips = ("band", "chip")
    swap = [(0, 1), (1, 0)]
    groups = lax.axis_size("band") * lax.axis_size("chip")
    core = lax.axis_index("core").astype(jnp.int32).reshape(1)
    cells = latent.shape[1]
    packed = pack(weights, targets, slots, counts)
    left, right = from_sides(latent[:, 0:1, :], latent[:, cells - 1 : cells, :])
    packed, left, right = lax.optimization_barrier((packed, left, right))
    got = lax.all_to_all(packed, LON, 0, 0, tiled=True)
    left, right = left.astype(f32), right.astype(f32)
    gain_row = gain.reshape(1, -1)
    w_out_t = w_out.T
    stk, slope, act_t, xhat_t = forward(latent, left, right, gain_row, w_in, w_out)
    adv, both, keep, send = decode(core, row_index, got, stk, head, head.T, w_out_t, slope, act_t, xhat_t, groups)
    came = lax.ppermute(send, "core", swap)
    parts = lax.all_to_all(pair(keep, came), chips, 0, 0, tiled=True)
    grad, first, last = backward(latent, left, right, gain_row, w_in.T, w_out_t, adv, slope, both)
    parts, first, last = lax.optimization_barrier((parts, first, last))
    grad_left, grad_right = from_sides(first.astype(bf16), last.astype(bf16))
    grad = add_edges(grad, grad_left.astype(f32), grad_right.astype(f32))
    mine = lax.all_to_all(total(parts), chips, 0, 0, tiled=True)
    mine, grad = lax.optimization_barrier((mine, grad))
    other = lax.ppermute(mine, "core", swap)
    grad_in, grad_out, grad_gain, grad_head = finish(core, mine, other, gain, w_in, head, 2 * groups)
    return grad, grad_in, grad_out, grad_gain.reshape(-1), grad_head


def solution(mesh):
    bands, lons = mesh.devices.shape
    by_core = jax.sharding.Mesh(mesh.devices.reshape(bands, lons // 2, 2), ("band", "chip", "core"))
    every = ("band", "chip", "core")
    return jax.shard_map(
        body,
        mesh=by_core,
        in_specs=(
            P("band", LON, None),
            P("band", LON, None),
            P(every, None, None),
            P(every, None),
            P(every),
            P(every, None, None),
            P(),
            P(),
            P(),
            P(),
        ),
        out_specs=(P("band", LON, None), P(), P(), P(), P()),
        check_vma=False,
    )
```

```python
import functools
import math

import jax
import jax.numpy as jnp
from jax import lax
from jax.experimental import pallas as pl
from jax.experimental.pallas import tpu as pltpu
from jax.sharding import PartitionSpec as P

WINDOW_SLOTS = 7
NORM_EPS = 1e-05
ROWS_STEP = 8
BLOCKS_STEP = 8
PULL_ROWS = 16
PACK_CHUNKS = 4
META = 8

f32 = jnp.float32
bf16 = jnp.bfloat16
INSIDE = pl.BlockSpec(memory_space=pltpu.VMEM)
OUTSIDE = pl.BlockSpec(memory_space=pltpu.HBM)


def dot(a, b):
    return jnp.dot(a, b, preferred_element_type=f32)


def dot_t(a, b):
    return lax.dot_general(a, b, (((0,), (0,)), ((), ())), preferred_element_type=f32)


def params(mib=48):
    return pltpu.CompilerParams(vmem_limit_bytes=mib * 2**20)


def in_hbm(*arrays):
    return [pltpu.with_memory_space_constraint(x, pltpu.HBM) for x in arrays]


def cost(flops, nbytes, trans=0):
    return pl.CostEstimate(flops=flops, bytes_accessed=nbytes, transcendentals=trans)


def pack_kernel(w_hbm, t_hbm, slot_hbm, count_hbm, out_hbm, buf, slots, counts, small_sems, in_sems, out_sems):
    blocks, obs = slots.shape
    nv = t_hbm.shape[1]
    n = blocks // PACK_CHUNKS
    small = [
        pltpu.make_async_copy(slot_hbm, slots, small_sems.at[0]),
        pltpu.make_async_copy(count_hbm, counts, small_sems.at[1]),
    ]
    arrive, leave = [], []
    for c in range(PACK_CHUNKS):
        here = pl.ds(c * n, n)
        arrive.append(
            (
                pltpu.make_async_copy(w_hbm.at[here], buf.at[here, pl.ds(0, obs), :], in_sems.at[2 * c]),
                pltpu.make_async_copy(t_hbm.at[here], buf.at[here, pl.ds(obs, nv), :], in_sems.at[2 * c + 1]),
            )
        )
        leave.append(pltpu.make_async_copy(buf.at[here], out_hbm.at[here], out_sems.at[c]))
    for c in small:
        c.start()
    for pair in arrive:
        for c in pair:
            c.start()
    for c in small:
        c.wait()
    coef = slots[...].astype(f32) / (WINDOW_SLOTS - 1)
    lane = lax.broadcasted_iota(jnp.int32, (META, obs), 1)
    row = lax.broadcasted_iota(jnp.int32, (META, obs), 0)
    for b in range(blocks):
        live = jnp.where(lane < counts[b], 1.0, 0.0)
        buf[b, obs + nv : obs + nv + META, :] = jnp.where(row == 0, coef[b : b + 1, :], live).astype(bf16)
    for pair, out in zip(arrive, leave):
        for c in pair:
            c.wait()
        out.start()
    for c in leave:
        c.wait()


def pack(weights, targets, slots, counts):
    blocks, obs, cells = weights.shape
    shape = (blocks, 2 * obs + META, cells)
    dma = pltpu.SemaphoreType.DMA
    return pl.pallas_call(
        pack_kernel,
        out_shape=pltpu.HBM(shape, bf16),
        in_specs=[OUTSIDE] * 4,
        out_specs=OUTSIDE,
        scratch_shapes=[
            pltpu.VMEM(shape, bf16),
            pltpu.VMEM(slots.shape, jnp.int32),
            pltpu.SMEM(counts.shape, jnp.int32),
            dma((2,)),
            dma((2 * PACK_CHUNKS,)),
            dma((PACK_CHUNKS,)),
        ],
        compiler_params=params(),
        cost_estimate=cost(1, 4 * 2**20),
        name="pack",
    )(*in_hbm(weights, targets, slots, counts))


def mixed(x, left, right):
    cells = x.shape[1]
    place = lax.broadcasted_iota(jnp.int32, x.shape, 1)
    from_left = jnp.where(place == 0, left, pltpu.roll(x, 1, 1))
    from_right = jnp.where(place == cells - 1, right, pltpu.roll(x, cells - 1, 1))
    return x + 0.5 * (from_left + from_right)


def normalized(lat, left, right):
    summed = mixed(lat, left, right)
    inv = lax.rsqrt(jnp.mean(summed * summed, axis=-1, keepdims=True) + NORM_EPS)
    return summed * inv, inv


def forward_kernel(
    lat_ref, left_ref, right_ref, gain_ref, w_in_ref, w_out_ref,
    stk_ref, slope_ref, act_t_ref, xhat_t_ref, xhat_ref, inv_slope_ref, ends_ref,
):
    rows, cells, ch = lat_ref.shape
    lat_b = lat_ref[...]
    lat = lat_b.astype(f32)
    xhat3, inv3 = normalized(lat, left_ref[...], right_ref[...])
    for k, cell in enumerate((0, cells - 1)):
        ends_ref[2 * k] = xhat3[:, cell, :]
        ends_ref[2 * k + 1] = jnp.broadcast_to(inv3[:, cell, :], (rows, ch))
    xhat = xhat3.reshape(rows * cells, ch)
    pre = dot((xhat * gain_ref[...]).astype(bf16), w_in_ref[...])
    sig = jax.nn.sigmoid(pre)
    act = pre * sig
    act_b = act.astype(bf16)
    slope = sig * (1.0 + pre * (1.0 - sig))
    slope_ref[...] = slope.astype(bf16)
    inv_slope_ref[...] = (slope * inv3.reshape(rows * cells, 1)).astype(bf16)
    new = lat.reshape(rows * cells, ch) + dot(act_b, w_out_ref[...])
    stk_ref[:, 0:cells, :] = lat_b
    stk_ref[:, cells : 2 * cells, :] = new.astype(bf16).reshape(rows, cells, ch)
    xhat_b = xhat.astype(bf16)
    xhat_ref[...] = xhat_b
    act_t_ref[...] = act_b.T
    xhat_t_ref[...] = xhat_b.T


def forward(latent, left, right, gain, w_in, w_out):
    rows, cells, ch = latent.shape
    hid = w_in.shape[1]
    n = rows * cells
    step = ROWS_STEP * cells
    return pl.pallas_call(
        forward_kernel,
        grid=(rows // ROWS_STEP,),
        out_shape=(
            pltpu.HBM((rows, 2 * cells, ch), bf16),
            pltpu.HBM((n, hid), bf16),
            pltpu.HBM((hid, n), bf16),
            pltpu.HBM((ch, n), bf16),
            pltpu.HBM((n, ch), bf16),
            pltpu.HBM((n, hid), bf16),
            jax.ShapeDtypeStruct((4, rows, ch), f32),
        ),
        in_specs=[
            pl.BlockSpec((ROWS_STEP, cells, ch), lambda i: (i, 0, 0)),
            pl.BlockSpec((ROWS_STEP, 1, ch), lambda i: (i, 0, 0)),
            pl.BlockSpec((ROWS_STEP, 1, ch), lambda i: (i, 0, 0)),
            pl.BlockSpec((1, ch), lambda i: (0, 0)),
            pl.BlockSpec((ch, hid), lambda i: (0, 0)),
            pl.BlockSpec((hid, ch), lambda i: (0, 0)),
        ],
        out_specs=(
            pl.BlockSpec((ROWS_STEP, 2 * cells, ch), lambda i: (i, 0, 0)),
            pl.BlockSpec((step, hid), lambda i: (i, 0)),
            pl.BlockSpec((hid, step), lambda i: (0, i)),
            pl.BlockSpec((ch, step), lambda i: (0, i)),
            pl.BlockSpec((step, ch), lambda i: (i, 0)),
            pl.BlockSpec((step, hid), lambda i: (i, 0)),
            pl.BlockSpec((4, ROWS_STEP, ch), lambda i: (0, i, 0)),
        ),
        compiler_params=params(),
        cost_estimate=cost(4 * n * ch * hid, 16 * 2**20, 2 * n * hid),
        name="forward",
    )(latent, left, right, gain, w_in, w_out)


def decode_kernel(
    core_ref, rows_ref, got_hbm, stk_hbm, head_ref, head_t_ref, w_out_t_ref, w_in_t_ref, gain_ref, ends_ref,
    slope_hbm, act_t_hbm, xhat_t_hbm,
    adv_hbm, both_hbm, keep_ref, send_ref, first_ref, last_ref,
    got, stk, slope, act_t, xhat_t, adv_all, both_all, ends, acc_both, acc_new, acc_head, acc_in, acc_out,
    got_sems, stk_sems, in_sems, out_sems,
):
    nb, nr = BLOCKS_STEP, PULL_ROWS
    blocks = got.shape[0]
    ch, nv = head_ref.shape
    obs = (got.shape[1] - META) // 2
    rows, cells, _ = acc_both.shape
    scale = 1.0 / math.sqrt(obs)
    step = nr * cells

    def got_copy(i):
        here = pl.ds(i * nb, nb)
        return pltpu.make_async_copy(got_hbm.at[here], got.at[here], got_sems.at[i])

    def stk_copy(b):
        return pltpu.make_async_copy(stk_hbm.at[rows_ref[0, 0, b]], stk.at[b], stk_sems.at[b])

    def adv_copy(k):
        flat = pl.ds(pl.multiple_of(k * step, step), step)
        return pltpu.make_async_copy(adv_all.at[flat], adv_hbm.at[flat], out_sems.at[k])

    later = [
        pltpu.make_async_copy(src, dst, in_sems.at[i])
        for i, (src, dst) in enumerate(((slope_hbm, slope), (xhat_t_hbm, xhat_t), (act_t_hbm, act_t)))
    ]
    for i in range(blocks // nb):
        got_copy(i).start()
        for j in range(nb):
            stk_copy(i * nb + j).start()
    for acc in (acc_both, acc_new, acc_head, acc_in, acc_out):
        acc[...] = jnp.zeros_like(acc)

    def observe(i, carry):
        first = i * nb
        got_copy(i).wait()
        for j in range(nb):
            stk_copy(first + j).wait()

        @pl.when(i == 0)
        def _():
            for c in later:
                c.start()

        places = [rows_ref[0, 0, first + j] for j in range(nb)]
        meta = jnp.concatenate([got[first + j, 2 * obs : 2 * obs + META, :].astype(f32) for j in range(nb)], axis=0).T
        latents, coefs, lives = [], [], []
        for j in range(nb):
            t, live = meta[:, META * j : META * j + 1], meta[:, META * j + 1 : META * j + 2]
            w = got[first + j, 0:obs, :]
            w_new = w * jnp.broadcast_to(t, w.shape).astype(bf16)
            latents.append(dot(jnp.concatenate([w - w_new, w_new], axis=1), stk[first + j]).astype(bf16))
            coefs.append(t)
            lives.append(live)
        obs_latent = jnp.concatenate(latents, axis=0)
        pred = dot(obs_latent, head_ref[...])
        goals = jnp.concatenate([got[first + j, obs : 2 * obs, :] for j in range(nb)], axis=0)
        live = jnp.concatenate(lives, axis=0)
        residual = jnp.where(live > 0.5, pred - goals.astype(f32), 0.0)
        pred_grad = (residual * scale).astype(bf16)
        acc_head[...] += dot_t(pred_grad, obs_latent)
        grad = dot(pred_grad, head_t_ref[...])
        for j in range(nb):
            g = grad[j * obs : (j + 1) * obs, :]
            w = got[first + j, 0:obs, :]
            pulled = dot_t(w, jnp.concatenate([g.astype(bf16), (g * coefs[j]).astype(bf16)], axis=1))
            acc_both[places[j]] += pulled[:, :ch]
            acc_new[places[j]] += pulled[:, ch:]
        return carry

    lax.fori_loop(0, blocks // nb, observe, 0)
    both_all[...] = acc_both[...].astype(bf16)
    both_copy = pltpu.make_async_copy(both_all, both_hbm, out_sems.at[rows // nr])
    both_copy.start()
    for c in later:
        c.wait()

    def pull(k, carry):
        flat = pl.ds(pl.multiple_of(k * step, step), step)
        adv = acc_new[pl.ds(k * nr, nr)].reshape(step, ch).astype(bf16)
        adv_all[flat, :] = adv
        adv_copy(k).start()
        pre_grad = (dot(adv, w_out_t_ref[...]) * slope[flat, :].astype(f32)).astype(bf16)
        here = pl.ds(pl.multiple_of(k * nr, nr), nr)
        by_row = pre_grad.reshape(nr, cells, pre_grad.shape[1])
        ends[0, here, :] = by_row[:, 0, :].astype(f32)
        ends[1, here, :] = by_row[:, cells - 1, :].astype(f32)
        acc_in[...] += dot(xhat_t[:, flat], pre_grad)
        acc_out[...] += dot(act_t[:, flat], adv)
        return carry

    lax.fori_loop(0, rows // nr, pull, 0)
    for k, ref in enumerate((first_ref, last_ref)):
        gained = dot(ends[k].astype(bf16), w_in_t_ref[...]) * gain_ref[...]
        xhat, inv = ends_ref[2 * k], ends_ref[2 * k + 1]
        ref[...] = (inv * (gained - xhat * jnp.mean(gained * xhat, axis=-1, keepdims=True))).astype(bf16)
    for core in range(2):

        @pl.when(core_ref[0] == core)
        def _(core=core):
            put_chunks(keep_ref, core, acc_in, acc_out, acc_head)
            put_chunks(send_ref, 1 - core, acc_in, acc_out, acc_head)

    both_copy.wait()
    for k in range(rows // nr):
        adv_copy(k).wait()


def put_chunks(ref, half, *accs):
    for p, acc in enumerate(accs):
        down = acc.shape[0] // 8
        across = acc.shape[1] // 256
        for j in range(across):
            at = 128 * (half * across + j)
            tiles = acc[:, at : at + 128].reshape(down, 8, 128)
            ref[down * j : down * (j + 1), 8 * p : 8 * p + 8, :] = tiles.astype(ref.dtype)
        if down * across < ref.shape[0]:
            rest = ref.shape[0] - down * across
            ref[down * across :, 8 * p : 8 * p + 8, :] = jnp.zeros((rest, 8, 128), ref.dtype)


def take_chunks(halves, part, shape):
    down = shape[0] // 8
    across = shape[1] // 256
    return jnp.concatenate(
        [
            half[down * j : down * (j + 1), 8 * part : 8 * part + 8, :].reshape(shape[0], 128)
            for half in halves
            for j in range(across)
        ],
        axis=1,
    )


def decode(core, rows, got, stk, head, head_t, w_out_t, w_in_t, gain, ends, slope, act_t, xhat_t, chunks):
    nrow, two_cells, ch = stk.shape
    cells = two_cells // 2
    nv = head.shape[1]
    hid = w_out_t.shape[1]
    n = nrow * cells
    blocks = got.shape[0]
    dma = pltpu.SemaphoreType.DMA
    scalars = pl.BlockSpec(memory_space=pltpu.SMEM)
    return pl.pallas_call(
        decode_kernel,
        out_shape=(
            pltpu.HBM((n, ch), bf16),
            pltpu.HBM((nrow, cells, ch), bf16),
            jax.ShapeDtypeStruct((chunks, 24, 128), f32),
            jax.ShapeDtypeStruct((chunks, 24, 128), bf16),
            jax.ShapeDtypeStruct((nrow, ch), bf16),
            jax.ShapeDtypeStruct((nrow, ch), bf16),
        ),
        in_specs=[scalars] * 2 + [OUTSIDE] * 2 + [INSIDE] * 6 + [OUTSIDE] * 3,
        out_specs=(OUTSIDE, OUTSIDE) + (INSIDE,) * 4,
        scratch_shapes=[pltpu.VMEM(x.shape, bf16) for x in (got, stk, slope, act_t, xhat_t)]
        + [
            pltpu.VMEM((n, ch), bf16),
            pltpu.VMEM((nrow, cells, ch), bf16),
            pltpu.VMEM((2, nrow, hid), f32),
            pltpu.VMEM((nrow, cells, ch), f32),
            pltpu.VMEM((nrow, cells, ch), f32),
            pltpu.VMEM((nv, ch), f32),
            pltpu.VMEM((ch, hid), f32),
            pltpu.VMEM((hid, ch), f32),
            dma((blocks // BLOCKS_STEP,)),
            dma((blocks,)),
            dma((3,)),
            dma((nrow // PULL_ROWS + 1,)),
        ],
        compiler_params=params(),
        cost_estimate=cost(10 * n * ch * hid, 24 * 2**20),
        name="decode",
    )(core, rows, *in_hbm(got, stk), head, head_t, w_out_t, w_in_t, gain, ends, *in_hbm(slope, act_t, xhat_t))


def backward_kernel(left_ref, right_ref, gain_ref, w_in_t_ref, w_out_t_ref, adv_ref, slope_ref, xhat_ref, both_ref, out_ref):
    rows, cells, ch = out_ref.shape
    pre_grad = (dot(adv_ref[...], w_out_t_ref[...]) * slope_ref[...].astype(f32)).astype(bf16)
    gained = dot(pre_grad, w_in_t_ref[...]) * gain_ref[...]
    xhat = xhat_ref[...].astype(f32)
    summed_grad = gained - xhat * jnp.mean(gained * xhat, axis=-1, keepdims=True)
    out_ref[...] = both_ref[...].astype(f32) + mixed(summed_grad.reshape(rows, cells, ch), left_ref[...], right_ref[...])


def backward(left, right, gain, w_in_t, w_out_t, adv, inv_slope, xhat, both):
    rows, cells, ch = both.shape
    hid = w_in_t.shape[0]
    step = ROWS_STEP * cells
    edge = pl.BlockSpec((ROWS_STEP, 1, ch), lambda i: (i, 0, 0))
    whole = pl.BlockSpec((ROWS_STEP, cells, ch), lambda i: (i, 0, 0))
    return pl.pallas_call(
        backward_kernel,
        grid=(rows // ROWS_STEP,),
        out_shape=jax.ShapeDtypeStruct((rows, cells, ch), f32),
        in_specs=[
            edge,
            edge,
            pl.BlockSpec((1, ch), lambda i: (0, 0)),
            pl.BlockSpec((hid, ch), lambda i: (0, 0)),
            pl.BlockSpec((ch, hid), lambda i: (0, 0)),
            pl.BlockSpec((step, ch), lambda i: (i, 0)),
            pl.BlockSpec((step, hid), lambda i: (i, 0)),
            pl.BlockSpec((step, ch), lambda i: (i, 0)),
            whole,
        ],
        out_specs=whole,
        compiler_params=params(),
        cost_estimate=cost(4 * rows * cells * ch * hid, 16 * 2**20),
        name="backward",
    )(left, right, gain, w_in_t, w_out_t, *in_hbm(adv, inv_slope, xhat, both))


def total_kernel(got_ref, out_ref):
    total = jnp.sum(got_ref[...].astype(f32), axis=0, keepdims=True).astype(bf16)
    out_ref[...] = jnp.broadcast_to(total, out_ref.shape)


def total(got):
    return pl.pallas_call(
        total_kernel,
        out_shape=jax.ShapeDtypeStruct(got.shape, bf16),
        compiler_params=params(),
        cost_estimate=cost(got.size, 2 * got.size * 2),
        name="total",
    )(got)


def pair_kernel(keep_ref, came_ref, out_ref):
    out_ref[...] = (keep_ref[...] + came_ref[...].astype(f32)).astype(bf16)


def pair(keep, came):
    return pl.pallas_call(
        pair_kernel,
        out_shape=jax.ShapeDtypeStruct(keep.shape, bf16),
        compiler_params=params(),
        cost_estimate=cost(keep.size, 8 * keep.size),
        name="pair",
    )(keep, came)


def finish_kernel(core_ref, mine_ref, other_ref, gain_ref, w_in_ref, in_ref, out_ref, gain_grad_ref, head_ref, *, devices):
    share = 1.0 / devices
    for core in range(2):

        @pl.when(core_ref[0] == core)
        def _(core=core):
            pair = (mine_ref, other_ref) if core == 0 else (other_ref, mine_ref)
            halves = [ref[...].astype(f32) * share for ref in pair]
            x = take_chunks(halves, 0, in_ref.shape)
            in_ref[...] = x * gain_ref[...]
            per_channel = jnp.sum(x * w_in_ref[...].astype(f32), axis=1, keepdims=True)
            gain_grad_ref[...] = jnp.broadcast_to(per_channel, (x.shape[0], 128)).T[0:1, :]
            out_ref[...] = take_chunks(halves, 1, out_ref.shape)
            head_ref[...] = take_chunks(halves, 2, head_ref.shape[::-1]).T


def finish(core, mine, other, gain, w_in, head, devices):
    ch, hid = w_in.shape
    return pl.pallas_call(
        functools.partial(finish_kernel, devices=devices),
        out_shape=(
            jax.ShapeDtypeStruct((ch, hid), f32),
            jax.ShapeDtypeStruct((hid, ch), f32),
            jax.ShapeDtypeStruct((1, ch), f32),
            jax.ShapeDtypeStruct(head.shape, f32),
        ),
        in_specs=[pl.BlockSpec(memory_space=pltpu.SMEM)] + [INSIDE] * 4,
        out_specs=(INSIDE,) * 4,
        compiler_params=params(),
        cost_estimate=cost(4 * ch * hid, 3 * 2**20),
        name="finish",
    )(core, mine, other, gain.reshape(ch, 1), w_in)


LON = ("chip", "core")


def from_sides(first, last):
    count = lax.axis_size("chip") * lax.axis_size("core")
    left = lax.ppermute(last, LON, [(i, (i + 1) % count) for i in range(count)])
    right = lax.ppermute(first, LON, [((i + 1) % count, i) for i in range(count)])
    return left, right


def body(latent, row_index, weights, slots, counts, targets, gain, w_in, w_out, head):
    chips = ("band", "chip")
    swap = [(0, 1), (1, 0)]
    groups = lax.axis_size("band") * lax.axis_size("chip")
    core = lax.axis_index("core").astype(jnp.int32).reshape(1)
    cells = latent.shape[1]
    packed = pack(weights, targets, slots, counts)
    left, right = from_sides(latent[:, 0:1, :], latent[:, cells - 1 : cells, :])
    packed, left, right = lax.optimization_barrier((packed, left, right))
    got = lax.all_to_all(packed, LON, 0, 0, tiled=True)
    left, right = left.astype(f32), right.astype(f32)
    gain_row = gain.reshape(1, -1)
    w_out_t = w_out.T
    w_in_t = w_in.T
    stk, slope, act_t, xhat_t, xhat, inv_slope, ends = forward(latent, left, right, gain_row, w_in, w_out)
    adv, both, keep, send, first, last = decode(
        core, row_index, got, stk, head, head.T, w_out_t, w_in_t, gain_row, ends, slope, act_t, xhat_t, groups
    )
    grad_left, grad_right = from_sides(first, last)
    came = lax.ppermute(send, "core", swap)
    summed, grad_left, grad_right = lax.optimization_barrier((pair(keep, came), grad_left, grad_right))
    parts = lax.all_to_all(summed, chips, 0, 0, tiled=True)
    grad_left, grad_right = (x.astype(f32)[:, None, :] for x in (grad_left, grad_right))
    grad = backward(grad_left, grad_right, gain_row, w_in_t, w_out_t, adv, inv_slope, xhat, both)
    parts, grad = lax.optimization_barrier((parts, grad))
    mine = lax.all_to_all(total(parts), chips, 0, 0, tiled=True)
    other = lax.ppermute(mine, "core", swap)
    grad_in, grad_out, grad_gain, grad_head = finish(core, mine, other, gain, w_in, head, 2 * groups)
    return grad, grad_in, grad_out, grad_gain.reshape(-1), grad_head


def solution(mesh):
    bands, lons = mesh.devices.shape
    by_core = jax.sharding.Mesh(mesh.devices.reshape(bands, lons // 2, 2), ("band", "chip", "core"))
    every = ("band", "chip", "core")
    return jax.shard_map(
        body,
        mesh=by_core,
        in_specs=(
            P("band", LON, None),
            P("band", LON, None),
            P(every, None, None),
            P(every, None),
            P(every),
            P(every, None, None),
            P(),
            P(),
            P(),
            P(),
        ),
        out_specs=(P("band", LON, None), P(), P(), P(), P()),
        check_vma=False,
    )
```

```python
import functools
import math

import jax
import jax.numpy as jnp
from jax import lax
from jax.experimental import pallas as pl
from jax.experimental.pallas import tpu as pltpu
from jax.sharding import PartitionSpec as P

WINDOW_SLOTS = 7
NORM_EPS = 1e-05
ROWS_STEP = 8
BLOCKS_STEP = 8
PULL_ROWS = 16
PACK_CHUNKS = 4
BACK_ROWS = 8
META = 8

f32 = jnp.float32
bf16 = jnp.bfloat16
INSIDE = pl.BlockSpec(memory_space=pltpu.VMEM)
OUTSIDE = pl.BlockSpec(memory_space=pltpu.HBM)


def dot(a, b):
    return jnp.dot(a, b, preferred_element_type=f32)


def dot_t(a, b):
    return lax.dot_general(a, b, (((0,), (0,)), ((), ())), preferred_element_type=f32)


def params(mib=48):
    return pltpu.CompilerParams(vmem_limit_bytes=mib * 2**20)


def in_hbm(*arrays):
    return [pltpu.with_memory_space_constraint(x, pltpu.HBM) for x in arrays]


def cost(flops, nbytes, trans=0):
    return pl.CostEstimate(flops=flops, bytes_accessed=nbytes, transcendentals=trans)


def pack_kernel(w_hbm, t_hbm, slot_hbm, count_hbm, out_hbm, buf, slots, counts, small_sems, in_sems, out_sems):
    blocks, obs = slots.shape
    nv = t_hbm.shape[1]
    n = blocks // PACK_CHUNKS
    small = [
        pltpu.make_async_copy(slot_hbm, slots, small_sems.at[0]),
        pltpu.make_async_copy(count_hbm, counts, small_sems.at[1]),
    ]
    arrive, leave = [], []
    for c in range(PACK_CHUNKS):
        here = pl.ds(c * n, n)
        arrive.append(
            (
                pltpu.make_async_copy(w_hbm.at[here], buf.at[here, pl.ds(0, obs), :], in_sems.at[2 * c]),
                pltpu.make_async_copy(t_hbm.at[here], buf.at[here, pl.ds(obs, nv), :], in_sems.at[2 * c + 1]),
            )
        )
        leave.append(pltpu.make_async_copy(buf.at[here], out_hbm.at[here], out_sems.at[c]))
    for c in small:
        c.start()
    for pair in arrive:
        for c in pair:
            c.start()
    for c in small:
        c.wait()
    coef = slots[...].astype(f32) / (WINDOW_SLOTS - 1)
    lane = lax.broadcasted_iota(jnp.int32, (META, obs), 1)
    row = lax.broadcasted_iota(jnp.int32, (META, obs), 0)
    for b in range(blocks):
        live = jnp.where(lane < counts[b], 1.0, 0.0)
        buf[b, obs + nv : obs + nv + META, :] = jnp.where(row == 0, coef[b : b + 1, :], live).astype(bf16)
    for pair, out in zip(arrive, leave):
        for c in pair:
            c.wait()
        out.start()
    for c in leave:
        c.wait()


def pack(weights, targets, slots, counts):
    blocks, obs, cells = weights.shape
    shape = (blocks, 2 * obs + META, cells)
    dma = pltpu.SemaphoreType.DMA
    return pl.pallas_call(
        pack_kernel,
        out_shape=pltpu.HBM(shape, bf16),
        in_specs=[OUTSIDE] * 4,
        out_specs=OUTSIDE,
        scratch_shapes=[
            pltpu.VMEM(shape, bf16),
            pltpu.VMEM(slots.shape, jnp.int32),
            pltpu.SMEM(counts.shape, jnp.int32),
            dma((2,)),
            dma((2 * PACK_CHUNKS,)),
            dma((PACK_CHUNKS,)),
        ],
        compiler_params=params(),
        cost_estimate=cost(1, 4 * 2**20),
        name="pack",
    )(*in_hbm(weights, targets, slots, counts))


def mixed(x, left, right):
    cells = x.shape[1]
    place = lax.broadcasted_iota(jnp.int32, x.shape, 1)
    from_left = jnp.where(place == 0, left, pltpu.roll(x, 1, 1))
    from_right = jnp.where(place == cells - 1, right, pltpu.roll(x, cells - 1, 1))
    return x + 0.5 * (from_left + from_right)


def normalized(lat, left, right):
    summed = mixed(lat, left, right)
    inv = lax.rsqrt(jnp.mean(summed * summed, axis=-1, keepdims=True) + NORM_EPS)
    return summed * inv, inv


def forward_kernel(
    lat_ref, left_ref, right_ref, gain_ref, w_in_ref, w_out_ref,
    stk_ref, slope_ref, act_t_ref, xhat_t_ref, xhat_ref, inv_slope_ref, ends_ref,
):
    rows, cells, ch = lat_ref.shape
    lat_b = lat_ref[...]
    lat = lat_b.astype(f32)
    xhat3, inv3 = normalized(lat, left_ref[...], right_ref[...])
    for k, cell in enumerate((0, cells - 1)):
        ends_ref[2 * k] = xhat3[:, cell, :]
        ends_ref[2 * k + 1] = jnp.broadcast_to(inv3[:, cell, :], (rows, ch))
    xhat = xhat3.reshape(rows * cells, ch)
    pre = dot((xhat * gain_ref[...]).astype(bf16), w_in_ref[...])
    sig = jax.nn.sigmoid(pre)
    act = pre * sig
    act_b = act.astype(bf16)
    slope = sig * (1.0 + pre * (1.0 - sig))
    slope_ref[...] = slope.astype(bf16)
    inv_slope_ref[...] = (slope * inv3.reshape(rows * cells, 1)).astype(bf16)
    new = lat.reshape(rows * cells, ch) + dot(act_b, w_out_ref[...])
    stk_ref[:, 0:cells, :] = lat_b
    stk_ref[:, cells : 2 * cells, :] = new.astype(bf16).reshape(rows, cells, ch)
    xhat_b = xhat.astype(bf16)
    xhat_ref[...] = xhat_b
    act_t_ref[...] = act_b.T
    xhat_t_ref[...] = xhat_b.T


def forward(latent, left, right, gain, w_in, w_out):
    rows, cells, ch = latent.shape
    hid = w_in.shape[1]
    n = rows * cells
    step = ROWS_STEP * cells
    return pl.pallas_call(
        forward_kernel,
        grid=(rows // ROWS_STEP,),
        out_shape=(
            pltpu.HBM((rows, 2 * cells, ch), bf16),
            pltpu.HBM((n, hid), bf16),
            pltpu.HBM((hid, n), bf16),
            pltpu.HBM((ch, n), bf16),
            pltpu.HBM((n, ch), bf16),
            pltpu.HBM((n, hid), bf16),
            jax.ShapeDtypeStruct((4, rows, ch), f32),
        ),
        in_specs=[
            pl.BlockSpec((ROWS_STEP, cells, ch), lambda i: (i, 0, 0)),
            pl.BlockSpec((ROWS_STEP, 1, ch), lambda i: (i, 0, 0)),
            pl.BlockSpec((ROWS_STEP, 1, ch), lambda i: (i, 0, 0)),
            pl.BlockSpec((1, ch), lambda i: (0, 0)),
            pl.BlockSpec((ch, hid), lambda i: (0, 0)),
            pl.BlockSpec((hid, ch), lambda i: (0, 0)),
        ],
        out_specs=(
            pl.BlockSpec((ROWS_STEP, 2 * cells, ch), lambda i: (i, 0, 0)),
            pl.BlockSpec((step, hid), lambda i: (i, 0)),
            pl.BlockSpec((hid, step), lambda i: (0, i)),
            pl.BlockSpec((ch, step), lambda i: (0, i)),
            pl.BlockSpec((step, ch), lambda i: (i, 0)),
            pl.BlockSpec((step, hid), lambda i: (i, 0)),
            pl.BlockSpec((4, ROWS_STEP, ch), lambda i: (0, i, 0)),
        ),
        compiler_params=params(),
        cost_estimate=cost(4 * n * ch * hid, 16 * 2**20, 2 * n * hid),
        name="forward",
    )(latent, left, right, gain, w_in, w_out)


def decode_kernel(
    core_ref, rows_ref, got_hbm, stk_hbm, head_ref, head_t_ref, w_out_t_ref, w_in_t_ref, gain_ref, ends_ref,
    slope_hbm, act_t_hbm, xhat_t_hbm,
    adv_hbm, both_hbm, keep_ref, send_ref, outer_ref,
    got, stk, slope, act_t, xhat_t, adv_all, both_all, ends, acc_both, acc_new, acc_head, acc_in, acc_out,
    got_sems, stk_sems, in_sems, out_sems,
):
    nb, nr = BLOCKS_STEP, PULL_ROWS
    blocks = got.shape[0]
    ch, nv = head_ref.shape
    obs = (got.shape[1] - META) // 2
    rows, cells, _ = acc_both.shape
    scale = 1.0 / math.sqrt(obs)
    step = nr * cells

    def got_copy(i):
        here = pl.ds(i * nb, nb)
        return pltpu.make_async_copy(got_hbm.at[here], got.at[here], got_sems.at[i])

    def stk_copy(b):
        return pltpu.make_async_copy(stk_hbm.at[rows_ref[0, 0, b]], stk.at[b], stk_sems.at[b])

    def adv_copy(k):
        flat = pl.ds(pl.multiple_of(k * step, step), step)
        return pltpu.make_async_copy(adv_all.at[flat], adv_hbm.at[flat], out_sems.at[k])

    later = [
        pltpu.make_async_copy(src, dst, in_sems.at[i])
        for i, (src, dst) in enumerate(((slope_hbm, slope), (xhat_t_hbm, xhat_t), (act_t_hbm, act_t)))
    ]
    for i in range(blocks // nb):
        got_copy(i).start()
        for j in range(nb):
            stk_copy(i * nb + j).start()
    for acc in (acc_both, acc_new, acc_head, acc_in, acc_out):
        acc[...] = jnp.zeros_like(acc)

    def observe(i, carry):
        first = i * nb
        got_copy(i).wait()
        for j in range(nb):
            stk_copy(first + j).wait()

        @pl.when(i == 0)
        def _():
            for c in later:
                c.start()

        places = [rows_ref[0, 0, first + j] for j in range(nb)]
        meta = jnp.concatenate([got[first + j, 2 * obs : 2 * obs + META, :].astype(f32) for j in range(nb)], axis=0).T
        latents, coefs, lives = [], [], []
        for j in range(nb):
            t, live = meta[:, META * j : META * j + 1], meta[:, META * j + 1 : META * j + 2]
            w = got[first + j, 0:obs, :]
            w_new = w * jnp.broadcast_to(t, w.shape).astype(bf16)
            latents.append(dot(jnp.concatenate([w - w_new, w_new], axis=1), stk[first + j]).astype(bf16))
            coefs.append(t)
            lives.append(live)
        obs_latent = jnp.concatenate(latents, axis=0)
        pred = dot(obs_latent, head_ref[...])
        goals = jnp.concatenate([got[first + j, obs : 2 * obs, :] for j in range(nb)], axis=0)
        live = jnp.concatenate(lives, axis=0)
        residual = jnp.where(live > 0.5, pred - goals.astype(f32), 0.0)
        pred_grad = (residual * scale).astype(bf16)
        acc_head[...] += dot_t(pred_grad, obs_latent)
        grad = dot(pred_grad, head_t_ref[...])
        for j in range(nb):
            g = grad[j * obs : (j + 1) * obs, :]
            w = got[first + j, 0:obs, :]
            pulled = dot_t(w, jnp.concatenate([g.astype(bf16), (g * coefs[j]).astype(bf16)], axis=1))
            acc_both[places[j]] += pulled[:, :ch]
            acc_new[places[j]] += pulled[:, ch:]
        return carry

    lax.fori_loop(0, blocks // nb, observe, 0)
    both_all[...] = acc_both[...].astype(bf16)
    both_copy = pltpu.make_async_copy(both_all, both_hbm, out_sems.at[rows // nr])
    both_copy.start()
    for c in later:
        c.wait()

    def pull(k, carry):
        flat = pl.ds(pl.multiple_of(k * step, step), step)
        adv = acc_new[pl.ds(k * nr, nr)].reshape(step, ch).astype(bf16)
        adv_all[flat, :] = adv
        adv_copy(k).start()
        pre_grad = (dot(adv, w_out_t_ref[...]) * slope[flat, :].astype(f32)).astype(bf16)
        here = pl.ds(pl.multiple_of(k * nr, nr), nr)
        by_row = pre_grad.reshape(nr, cells, pre_grad.shape[1])
        ends[0, here, :] = by_row[:, 0, :].astype(f32)
        ends[1, here, :] = by_row[:, cells - 1, :].astype(f32)
        acc_in[...] += dot(xhat_t[:, flat], pre_grad)
        acc_out[...] += dot(act_t[:, flat], adv)
        return carry

    lax.fori_loop(0, rows // nr, pull, 0)
    edges = []
    for k in range(2):
        gained = dot(ends[k].astype(bf16), w_in_t_ref[...]) * gain_ref[...]
        xhat, inv = ends_ref[2 * k], ends_ref[2 * k + 1]
        edges.append(inv * (gained - xhat * jnp.mean(gained * xhat, axis=-1, keepdims=True)))
    for core in range(2):

        @pl.when(core_ref[0] == core)
        def _(core=core):
            put_chunks(keep_ref, core, acc_in, acc_out, acc_head)
            put_chunks(send_ref, 1 - core, acc_in, acc_out, acc_head)
            outer_ref[...] = edges[core].astype(bf16)
            put_edge(send_ref, edges[1 - core])

    both_copy.wait()
    for k in range(rows // nr):
        adv_copy(k).wait()


def put_chunks(ref, half, *accs):
    for p, acc in enumerate(accs):
        down = acc.shape[0] // 8
        across = acc.shape[1] // 256
        for j in range(across):
            at = 128 * (half * across + j)
            tiles = acc[:, at : at + 128].reshape(down, 8, 128)
            ref[down * j : down * (j + 1), 8 * p : 8 * p + 8, :] = tiles.astype(ref.dtype)
        if down * across < ref.shape[0]:
            rest = ref.shape[0] - down * across
            ref[down * across :, 8 * p : 8 * p + 8, :] = jnp.zeros((rest, 8, 128), ref.dtype)


def edge_tiles(shape):
    first = 16
    return [(first + k, 8 * (k % (shape[0] // 8)), 128 * (k // (shape[0] // 8))) for k in range(shape[0] * shape[1] // 1024)]


def put_edge(ref, edge):
    for chunk, row, lane in edge_tiles(edge.shape):
        ref[chunk, 16:24, :] = edge[row : row + 8, lane : lane + 128].astype(ref.dtype)


def take_chunks(halves, part, shape):
    down = shape[0] // 8
    across = shape[1] // 256
    return jnp.concatenate(
        [
            half[down * j : down * (j + 1), 8 * part : 8 * part + 8, :].reshape(shape[0], 128)
            for half in halves
            for j in range(across)
        ],
        axis=1,
    )


def decode(core, rows, got, stk, head, head_t, w_out_t, w_in_t, gain, ends, slope, act_t, xhat_t, chunks):
    nrow, two_cells, ch = stk.shape
    cells = two_cells // 2
    nv = head.shape[1]
    hid = w_out_t.shape[1]
    n = nrow * cells
    blocks = got.shape[0]
    dma = pltpu.SemaphoreType.DMA
    scalars = pl.BlockSpec(memory_space=pltpu.SMEM)
    return pl.pallas_call(
        decode_kernel,
        out_shape=(
            pltpu.HBM((n, ch), bf16),
            pltpu.HBM((nrow, cells, ch), bf16),
            jax.ShapeDtypeStruct((chunks, 24, 128), f32),
            jax.ShapeDtypeStruct((chunks, 24, 128), bf16),
            jax.ShapeDtypeStruct((nrow, ch), bf16),
        ),
        in_specs=[scalars] * 2 + [OUTSIDE] * 2 + [INSIDE] * 6 + [OUTSIDE] * 3,
        out_specs=(OUTSIDE, OUTSIDE) + (INSIDE,) * 3,
        scratch_shapes=[pltpu.VMEM(x.shape, bf16) for x in (got, stk, slope, act_t, xhat_t)]
        + [
            pltpu.VMEM((n, ch), bf16),
            pltpu.VMEM((nrow, cells, ch), bf16),
            pltpu.VMEM((2, nrow, hid), f32),
            pltpu.VMEM((nrow, cells, ch), f32),
            pltpu.VMEM((nrow, cells, ch), f32),
            pltpu.VMEM((nv, ch), f32),
            pltpu.VMEM((ch, hid), f32),
            pltpu.VMEM((hid, ch), f32),
            dma((blocks // BLOCKS_STEP,)),
            dma((blocks,)),
            dma((3,)),
            dma((nrow // PULL_ROWS + 1,)),
        ],
        compiler_params=params(),
        cost_estimate=cost(10 * n * ch * hid, 24 * 2**20),
        name="decode",
    )(core, rows, *in_hbm(got, stk), head, head_t, w_out_t, w_in_t, gain, ends, *in_hbm(slope, act_t, xhat_t))


def backward_kernel(
    left_ref, right_ref, gain_ref, w_in_t_ref, w_out_t_ref, adv_ref, slope_ref, xhat_ref, both_ref, *rest
):
    out_ref = rest[-1]
    rows, cells, ch = out_ref.shape
    pre_grad = (dot(adv_ref[...], w_out_t_ref[...]) * slope_ref[...].astype(f32)).astype(bf16)
    gained = dot(pre_grad, w_in_t_ref[...]) * gain_ref[...]
    xhat = xhat_ref[...].astype(f32)
    summed_grad = gained - xhat * jnp.mean(gained * xhat, axis=-1, keepdims=True)
    out_ref[...] = both_ref[...].astype(f32) + mixed(summed_grad.reshape(rows, cells, ch), left_ref[...], right_ref[...])


def backward(left, right, gain, w_in_t, w_out_t, adv, inv_slope, xhat, both, begin, end, *before):
    rows, cells, ch = both.shape
    hid = w_in_t.shape[0]
    nr = BACK_ROWS
    step = nr * cells
    base = begin // nr
    edge = pl.BlockSpec((nr, 1, ch), lambda i: (i + base, 0, 0))
    whole = pl.BlockSpec((nr, cells, ch), lambda i: (i + base, 0, 0))
    share = (end - begin) * cells
    return pl.pallas_call(
        backward_kernel,
        grid=((end - begin) // nr,),
        out_shape=pltpu.HBM((rows, cells, ch), f32),
        in_specs=[
            edge,
            edge,
            pl.BlockSpec((1, ch), lambda i: (0, 0)),
            pl.BlockSpec((hid, ch), lambda i: (0, 0)),
            pl.BlockSpec((ch, hid), lambda i: (0, 0)),
            pl.BlockSpec((step, ch), lambda i: (i + base, 0)),
            pl.BlockSpec((step, hid), lambda i: (i + base, 0)),
            pl.BlockSpec((step, ch), lambda i: (i + base, 0)),
            whole,
        ]
        + [OUTSIDE] * len(before),
        out_specs=whole,
        input_output_aliases={9: 0} if before else {},
        compiler_params=params(),
        cost_estimate=cost(4 * share * ch * hid, 3584 * share),
        name="backward",
    )(left, right, gain, w_in_t, w_out_t, *in_hbm(adv, inv_slope, xhat, both, *before))


def total_kernel(got_ref, out_ref):
    total = jnp.sum(got_ref[...].astype(f32), axis=0, keepdims=True).astype(bf16)
    out_ref[...] = jnp.broadcast_to(total, out_ref.shape)


def total(got):
    return pl.pallas_call(
        total_kernel,
        out_shape=jax.ShapeDtypeStruct(got.shape, bf16),
        compiler_params=params(),
        cost_estimate=cost(got.size, 2 * got.size * 2),
        name="total",
    )(got)


def pair_kernel(keep_ref, came_ref, out_ref, edge_ref):
    out_ref[...] = (keep_ref[...] + came_ref[...].astype(f32)).astype(bf16)
    for chunk, row, lane in edge_tiles(edge_ref.shape):
        edge_ref[row : row + 8, lane : lane + 128] = came_ref[chunk, 16:24, :].astype(f32)


def pair(keep, came, edge):
    return pl.pallas_call(
        pair_kernel,
        out_shape=(jax.ShapeDtypeStruct(keep.shape, bf16), jax.ShapeDtypeStruct(edge.shape, f32)),
        compiler_params=params(),
        cost_estimate=cost(keep.size, 8 * keep.size),
        name="pair",
    )(keep, came)


def finish_kernel(core_ref, mine_ref, other_ref, gain_ref, w_in_ref, in_ref, out_ref, gain_grad_ref, head_ref, *, devices):
    share = 1.0 / devices
    for core in range(2):

        @pl.when(core_ref[0] == core)
        def _(core=core):
            pair = (mine_ref, other_ref) if core == 0 else (other_ref, mine_ref)
            halves = [ref[...].astype(f32) * share for ref in pair]
            x = take_chunks(halves, 0, in_ref.shape)
            in_ref[...] = x * gain_ref[...]
            per_channel = jnp.sum(x * w_in_ref[...].astype(f32), axis=1, keepdims=True)
            gain_grad_ref[...] = jnp.broadcast_to(per_channel, (x.shape[0], 128)).T[0:1, :]
            out_ref[...] = take_chunks(halves, 1, out_ref.shape)
            head_ref[...] = take_chunks(halves, 2, head_ref.shape[::-1]).T


def finish(core, mine, other, gain, w_in, head, devices):
    ch, hid = w_in.shape
    return pl.pallas_call(
        functools.partial(finish_kernel, devices=devices),
        out_shape=(
            jax.ShapeDtypeStruct((ch, hid), f32),
            jax.ShapeDtypeStruct((hid, ch), f32),
            jax.ShapeDtypeStruct((1, ch), f32),
            jax.ShapeDtypeStruct(head.shape, f32),
        ),
        in_specs=[pl.BlockSpec(memory_space=pltpu.SMEM)] + [INSIDE] * 4,
        out_specs=(INSIDE,) * 4,
        compiler_params=params(),
        cost_estimate=cost(4 * ch * hid, 3 * 2**20),
        name="finish",
    )(core, mine, other, gain.reshape(ch, 1), w_in)


LON = ("chip", "core")


def from_sides(first, last):
    count = lax.axis_size("chip") * lax.axis_size("core")
    left = lax.ppermute(last, LON, [(i, (i + 1) % count) for i in range(count)])
    right = lax.ppermute(first, LON, [((i + 1) % count, i) for i in range(count)])
    return left, right


def body(latent, row_index, weights, slots, counts, targets, gain, w_in, w_out, head):
    chips = ("band", "chip")
    swap = [(0, 1), (1, 0)]
    groups = lax.axis_size("band") * lax.axis_size("chip")
    core = lax.axis_index("core").astype(jnp.int32).reshape(1)
    cells = latent.shape[1]
    packed = pack(weights, targets, slots, counts)
    left, right = from_sides(latent[:, 0:1, :], latent[:, cells - 1 : cells, :])
    packed, left, right = lax.optimization_barrier((packed, left, right))
    got = lax.all_to_all(packed, LON, 0, 0, tiled=True)
    left, right = left.astype(f32), right.astype(f32)
    gain_row = gain.reshape(1, -1)
    w_out_t = w_out.T
    w_in_t = w_in.T
    stk, slope, act_t, xhat_t, xhat, inv_slope, ends = forward(latent, left, right, gain_row, w_in, w_out)
    adv, both, keep, send, outer = decode(
        core, row_index, got, stk, head, head.T, w_out_t, w_in_t, gain_row, ends, slope, act_t, xhat_t, groups
    )
    lons = 2 * lax.axis_size("chip")
    outer = lax.ppermute(outer, LON, [(i, (i + (1 if i % 2 else -1)) % lons) for i in range(lons)])
    summed, inner = pair(keep, lax.ppermute(send, "core", swap), outer)
    summed, outer, inner = lax.optimization_barrier((summed, outer, inner))
    parts = lax.all_to_all(summed, chips, 0, 0, tiled=True)
    outer = outer.astype(f32)
    grad_left = jnp.where(core == 0, outer, inner)[:, None, :]
    grad_right = jnp.where(core == 0, inner, outer)[:, None, :]
    rest = (grad_left, grad_right, gain_row, w_in_t, w_out_t, adv, inv_slope, xhat, both)
    rows = latent.shape[0]
    grad = backward(*rest, 0, rows // 2)
    parts, grad = lax.optimization_barrier((parts, grad))
    mine = lax.all_to_all(total(parts), chips, 0, 0, tiled=True)
    grad = backward(*rest, rows // 2, rows, grad)
    mine, grad = lax.optimization_barrier((mine, grad))
    other = lax.ppermute(mine, "core", swap)
    grad_in, grad_out, grad_gain, grad_head = finish(core, mine, other, gain, w_in, head, 2 * groups)
    return grad, grad_in, grad_out, grad_gain.reshape(-1), grad_head


def solution(mesh):
    bands, lons = mesh.devices.shape
    by_core = jax.sharding.Mesh(mesh.devices.reshape(bands, lons // 2, 2), ("band", "chip", "core"))
    every = ("band", "chip", "core")
    return jax.shard_map(
        body,
        mesh=by_core,
        in_specs=(
            P("band", LON, None),
            P("band", LON, None),
            P(every, None, None),
            P(every, None),
            P(every),
            P(every, None, None),
            P(),
            P(),
            P(),
            P(),
        ),
        out_specs=(P("band", LON, None), P(), P(), P(), P()),
        check_vma=False,
    )
```

```python
import functools
import math

import jax
import jax.numpy as jnp
from jax import lax
from jax.experimental import pallas as pl
from jax.experimental.pallas import tpu as pltpu
from jax.sharding import PartitionSpec as P

WINDOW_SLOTS = 7
NORM_EPS = 1e-05
ROWS_STEP = 8
BLOCKS_STEP = 8
PULL_ROWS = 16
PACK_CHUNKS = 4
BACK_ROWS = 8
AHEAD = 2
META = 8

f32 = jnp.float32
bf16 = jnp.bfloat16
INSIDE = pl.BlockSpec(memory_space=pltpu.VMEM)
OUTSIDE = pl.BlockSpec(memory_space=pltpu.HBM)


def dot(a, b):
    return jnp.dot(a, b, preferred_element_type=f32)


def dot_t(a, b):
    return lax.dot_general(a, b, (((0,), (0,)), ((), ())), preferred_element_type=f32)


def params(mib=48):
    return pltpu.CompilerParams(vmem_limit_bytes=mib * 2**20)


def in_hbm(*arrays):
    return [pltpu.with_memory_space_constraint(x, pltpu.HBM) for x in arrays]


def cost(flops, nbytes, trans=0):
    return pl.CostEstimate(flops=flops, bytes_accessed=nbytes, transcendentals=trans)


def pack_kernel(w_hbm, t_hbm, slot_hbm, count_hbm, out_hbm, buf, slots, counts, small_sems, in_sems, out_sems):
    blocks, obs = slots.shape
    nv = t_hbm.shape[1]
    n = blocks // PACK_CHUNKS
    small = [
        pltpu.make_async_copy(slot_hbm, slots, small_sems.at[0]),
        pltpu.make_async_copy(count_hbm, counts, small_sems.at[1]),
    ]
    arrive, leave = [], []
    for c in range(PACK_CHUNKS):
        here = pl.ds(c * n, n)
        arrive.append(
            (
                pltpu.make_async_copy(w_hbm.at[here], buf.at[here, pl.ds(0, obs), :], in_sems.at[2 * c]),
                pltpu.make_async_copy(t_hbm.at[here], buf.at[here, pl.ds(obs, nv), :], in_sems.at[2 * c + 1]),
            )
        )
        leave.append(pltpu.make_async_copy(buf.at[here], out_hbm.at[here], out_sems.at[c]))
    for c in small:
        c.start()
    for pair in arrive:
        for c in pair:
            c.start()
    for c in small:
        c.wait()
    coef = slots[...].astype(f32) / (WINDOW_SLOTS - 1)
    lane = lax.broadcasted_iota(jnp.int32, (META, obs), 1)
    row = lax.broadcasted_iota(jnp.int32, (META, obs), 0)
    for b in range(blocks):
        live = jnp.where(lane < counts[b], 1.0, 0.0)
        buf[b, obs + nv : obs + nv + META, :] = jnp.where(row == 0, coef[b : b + 1, :], live).astype(bf16)
    for pair, out in zip(arrive, leave):
        for c in pair:
            c.wait()
        out.start()
    for c in leave:
        c.wait()


def pack(weights, targets, slots, counts):
    blocks, obs, cells = weights.shape
    shape = (blocks, 2 * obs + META, cells)
    dma = pltpu.SemaphoreType.DMA
    return pl.pallas_call(
        pack_kernel,
        out_shape=pltpu.HBM(shape, bf16),
        in_specs=[OUTSIDE] * 4,
        out_specs=OUTSIDE,
        scratch_shapes=[
            pltpu.VMEM(shape, bf16),
            pltpu.VMEM(slots.shape, jnp.int32),
            pltpu.SMEM(counts.shape, jnp.int32),
            dma((2,)),
            dma((2 * PACK_CHUNKS,)),
            dma((PACK_CHUNKS,)),
        ],
        compiler_params=params(),
        cost_estimate=cost(1, 4 * 2**20),
        name="pack",
    )(*in_hbm(weights, targets, slots, counts))


def mixed(x, left, right):
    cells = x.shape[1]
    place = lax.broadcasted_iota(jnp.int32, x.shape, 1)
    from_left = jnp.where(place == 0, left, pltpu.roll(x, 1, 1))
    from_right = jnp.where(place == cells - 1, right, pltpu.roll(x, cells - 1, 1))
    return x + 0.5 * (from_left + from_right)


def normalized(lat, left, right):
    summed = mixed(lat, left, right)
    inv = lax.rsqrt(jnp.mean(summed * summed, axis=-1, keepdims=True) + NORM_EPS)
    return summed * inv, inv


def forward_kernel(
    lat_ref, left_ref, right_ref, gain_ref, w_in_ref, w_out_ref,
    stk_ref, slope_ref, act_t_ref, xhat_t_ref, xhat_ref, inv_slope_ref, ends_ref,
):
    rows, cells, ch = lat_ref.shape
    lat_b = lat_ref[...]
    lat = lat_b.astype(f32)
    xhat3, inv3 = normalized(lat, left_ref[...], right_ref[...])
    for k, cell in enumerate((0, cells - 1)):
        ends_ref[2 * k] = xhat3[:, cell, :]
        ends_ref[2 * k + 1] = jnp.broadcast_to(inv3[:, cell, :], (rows, ch))
    xhat = xhat3.reshape(rows * cells, ch)
    pre = dot((xhat * gain_ref[...]).astype(bf16), w_in_ref[...])
    sig = jax.nn.sigmoid(pre)
    act = pre * sig
    act_b = act.astype(bf16)
    slope = sig * (1.0 + pre * (1.0 - sig))
    slope_ref[...] = slope.astype(bf16)
    inv_slope_ref[...] = (slope * inv3.reshape(rows * cells, 1)).astype(bf16)
    new = lat.reshape(rows * cells, ch) + dot(act_b, w_out_ref[...])
    stk_ref[:, 0:cells, :] = lat_b
    stk_ref[:, cells : 2 * cells, :] = new.astype(bf16).reshape(rows, cells, ch)
    xhat_b = xhat.astype(bf16)
    xhat_ref[...] = xhat_b
    act_t_ref[...] = act_b.T
    xhat_t_ref[...] = xhat_b.T


def forward(latent, left, right, gain, w_in, w_out):
    rows, cells, ch = latent.shape
    hid = w_in.shape[1]
    n = rows * cells
    step = ROWS_STEP * cells
    return pl.pallas_call(
        forward_kernel,
        grid=(rows // ROWS_STEP,),
        out_shape=(
            pltpu.HBM((rows, 2 * cells, ch), bf16),
            pltpu.HBM((n, hid), bf16),
            pltpu.HBM((hid, n), bf16),
            pltpu.HBM((ch, n), bf16),
            pltpu.HBM((n, ch), bf16),
            pltpu.HBM((n, hid), bf16),
            jax.ShapeDtypeStruct((4, rows, ch), f32),
        ),
        in_specs=[
            pl.BlockSpec((ROWS_STEP, cells, ch), lambda i: (i, 0, 0)),
            pl.BlockSpec((ROWS_STEP, 1, ch), lambda i: (i, 0, 0)),
            pl.BlockSpec((ROWS_STEP, 1, ch), lambda i: (i, 0, 0)),
            pl.BlockSpec((1, ch), lambda i: (0, 0)),
            pl.BlockSpec((ch, hid), lambda i: (0, 0)),
            pl.BlockSpec((hid, ch), lambda i: (0, 0)),
        ],
        out_specs=(
            pl.BlockSpec((ROWS_STEP, 2 * cells, ch), lambda i: (i, 0, 0)),
            pl.BlockSpec((step, hid), lambda i: (i, 0)),
            pl.BlockSpec((hid, step), lambda i: (0, i)),
            pl.BlockSpec((ch, step), lambda i: (0, i)),
            pl.BlockSpec((step, ch), lambda i: (i, 0)),
            pl.BlockSpec((step, hid), lambda i: (i, 0)),
            pl.BlockSpec((4, ROWS_STEP, ch), lambda i: (0, i, 0)),
        ),
        compiler_params=params(),
        cost_estimate=cost(4 * n * ch * hid, 16 * 2**20, 2 * n * hid),
        name="forward",
    )(latent, left, right, gain, w_in, w_out)


def decode_kernel(
    core_ref, rows_ref, got_hbm, stk_hbm, head_ref, head_t_ref, w_out_t_ref, w_in_t_ref, gain_ref, ends_ref,
    slope_hbm, act_t_hbm, xhat_t_hbm,
    adv_hbm, both_hbm, keep_ref, send_ref, outer_ref,
    got, stk, slope, act_t, xhat_t, adv_all, both_all, ends, acc_both, acc_new, acc_head, acc_in, acc_out,
    got_sems, stk_sems, in_sems, out_sems,
):
    nb, nr = BLOCKS_STEP, PULL_ROWS
    blocks = got.shape[0]
    ch, nv = head_ref.shape
    obs = (got.shape[1] - META) // 2
    rows, cells, _ = acc_both.shape
    scale = 1.0 / math.sqrt(obs)
    step = nr * cells

    def got_copy(i):
        here = pl.ds(i * nb, nb)
        return pltpu.make_async_copy(got_hbm.at[here], got.at[here], got_sems.at[i])

    def stk_copy(b):
        return pltpu.make_async_copy(stk_hbm.at[rows_ref[0, 0, b]], stk.at[b], stk_sems.at[b])

    def adv_copy(k):
        flat = pl.ds(pl.multiple_of(k * step, step), step)
        return pltpu.make_async_copy(adv_all.at[flat], adv_hbm.at[flat], out_sems.at[k])

    later = [
        pltpu.make_async_copy(src, dst, in_sems.at[i])
        for i, (src, dst) in enumerate(((slope_hbm, slope), (xhat_t_hbm, xhat_t), (act_t_hbm, act_t)))
    ]
    def start(i):
        got_copy(i).start()
        for j in range(nb):
            stk_copy(i * nb + j).start()

    for i in range(AHEAD):
        start(i)
    for acc in (acc_both, acc_new, acc_head, acc_in, acc_out):
        acc[...] = jnp.zeros_like(acc)

    def observe(i, carry):
        first = i * nb
        got_copy(i).wait()
        for j in range(nb):
            stk_copy(first + j).wait()

        @pl.when(i + AHEAD < blocks // nb)
        def _():
            start(i + AHEAD)

        @pl.when(i == blocks // nb - 1 - AHEAD)
        def _():
            for c in later:
                c.start()

        places = [rows_ref[0, 0, first + j] for j in range(nb)]
        meta = jnp.concatenate([got[first + j, 2 * obs : 2 * obs + META, :].astype(f32) for j in range(nb)], axis=0).T
        latents, coefs, lives = [], [], []
        for j in range(nb):
            t, live = meta[:, META * j : META * j + 1], meta[:, META * j + 1 : META * j + 2]
            w = got[first + j, 0:obs, :]
            w_new = w * jnp.broadcast_to(t, w.shape).astype(bf16)
            latents.append(dot(jnp.concatenate([w - w_new, w_new], axis=1), stk[first + j]).astype(bf16))
            coefs.append(t)
            lives.append(live)
        obs_latent = jnp.concatenate(latents, axis=0)
        pred = dot(obs_latent, head_ref[...])
        goals = jnp.concatenate([got[first + j, obs : 2 * obs, :] for j in range(nb)], axis=0)
        live = jnp.concatenate(lives, axis=0)
        residual = jnp.where(live > 0.5, pred - goals.astype(f32), 0.0)
        pred_grad = (residual * scale).astype(bf16)
        acc_head[...] += dot_t(pred_grad, obs_latent)
        grad = dot(pred_grad, head_t_ref[...])
        for j in range(nb):
            g = grad[j * obs : (j + 1) * obs, :]
            w = got[first + j, 0:obs, :]
            pulled = dot_t(w, jnp.concatenate([g.astype(bf16), (g * coefs[j]).astype(bf16)], axis=1))
            acc_both[places[j]] += pulled[:, :ch]
            acc_new[places[j]] += pulled[:, ch:]
        return carry

    lax.fori_loop(0, blocks // nb, observe, 0)
    both_all[...] = acc_both[...].astype(bf16)
    both_copy = pltpu.make_async_copy(both_all, both_hbm, out_sems.at[rows // nr])
    both_copy.start()
    for c in later:
        c.wait()

    def pull(k, carry):
        flat = pl.ds(pl.multiple_of(k * step, step), step)
        adv = acc_new[pl.ds(k * nr, nr)].reshape(step, ch).astype(bf16)
        adv_all[flat, :] = adv
        adv_copy(k).start()
        pre_grad = (dot(adv, w_out_t_ref[...]) * slope[flat, :].astype(f32)).astype(bf16)
        here = pl.ds(pl.multiple_of(k * nr, nr), nr)
        by_row = pre_grad.reshape(nr, cells, pre_grad.shape[1])
        ends[0, here, :] = by_row[:, 0, :].astype(f32)
        ends[1, here, :] = by_row[:, cells - 1, :].astype(f32)
        acc_in[...] += dot(xhat_t[:, flat], pre_grad)
        acc_out[...] += dot(act_t[:, flat], adv)
        return carry

    lax.fori_loop(0, rows // nr, pull, 0)
    edges = []
    for k in range(2):
        gained = dot(ends[k].astype(bf16), w_in_t_ref[...]) * gain_ref[...]
        xhat, inv = ends_ref[2 * k], ends_ref[2 * k + 1]
        edges.append(inv * (gained - xhat * jnp.mean(gained * xhat, axis=-1, keepdims=True)))
    for core in range(2):

        @pl.when(core_ref[0] == core)
        def _(core=core):
            put_chunks(keep_ref, core, acc_in, acc_out, acc_head)
            put_chunks(send_ref, 1 - core, acc_in, acc_out, acc_head)
            outer_ref[...] = edges[core].astype(bf16)
            put_edge(send_ref, edges[1 - core])

    both_copy.wait()
    for k in range(rows // nr):
        adv_copy(k).wait()


def put_chunks(ref, half, *accs):
    for p, acc in enumerate(accs):
        down = acc.shape[0] // 8
        across = acc.shape[1] // 256
        for j in range(across):
            at = 128 * (half * across + j)
            tiles = acc[:, at : at + 128].reshape(down, 8, 128)
            ref[down * j : down * (j + 1), 8 * p : 8 * p + 8, :] = tiles.astype(ref.dtype)
        if down * across < ref.shape[0]:
            rest = ref.shape[0] - down * across
            ref[down * across :, 8 * p : 8 * p + 8, :] = jnp.zeros((rest, 8, 128), ref.dtype)


def edge_tiles(shape):
    first = 16
    return [(first + k, 8 * (k % (shape[0] // 8)), 128 * (k // (shape[0] // 8))) for k in range(shape[0] * shape[1] // 1024)]


def put_edge(ref, edge):
    for chunk, row, lane in edge_tiles(edge.shape):
        ref[chunk, 16:24, :] = edge[row : row + 8, lane : lane + 128].astype(ref.dtype)


def take_chunks(halves, part, shape):
    down = shape[0] // 8
    across = shape[1] // 256
    return jnp.concatenate(
        [
            half[down * j : down * (j + 1), 8 * part : 8 * part + 8, :].reshape(shape[0], 128)
            for half in halves
            for j in range(across)
        ],
        axis=1,
    )


def decode(core, rows, got, stk, head, head_t, w_out_t, w_in_t, gain, ends, slope, act_t, xhat_t, chunks):
    nrow, two_cells, ch = stk.shape
    cells = two_cells // 2
    nv = head.shape[1]
    hid = w_out_t.shape[1]
    n = nrow * cells
    blocks = got.shape[0]
    dma = pltpu.SemaphoreType.DMA
    scalars = pl.BlockSpec(memory_space=pltpu.SMEM)
    return pl.pallas_call(
        decode_kernel,
        out_shape=(
            pltpu.HBM((n, ch), bf16),
            pltpu.HBM((nrow, cells, ch), bf16),
            jax.ShapeDtypeStruct((chunks, 24, 128), f32),
            jax.ShapeDtypeStruct((chunks, 24, 128), bf16),
            jax.ShapeDtypeStruct((nrow, ch), bf16),
        ),
        in_specs=[scalars] * 2 + [OUTSIDE] * 2 + [INSIDE] * 6 + [OUTSIDE] * 3,
        out_specs=(OUTSIDE, OUTSIDE) + (INSIDE,) * 3,
        scratch_shapes=[pltpu.VMEM(x.shape, bf16) for x in (got, stk, slope, act_t, xhat_t)]
        + [
            pltpu.VMEM((n, ch), bf16),
            pltpu.VMEM((nrow, cells, ch), bf16),
            pltpu.VMEM((2, nrow, hid), f32),
            pltpu.VMEM((nrow, cells, ch), f32),
            pltpu.VMEM((nrow, cells, ch), f32),
            pltpu.VMEM((nv, ch), f32),
            pltpu.VMEM((ch, hid), f32),
            pltpu.VMEM((hid, ch), f32),
            dma((blocks // BLOCKS_STEP,)),
            dma((blocks,)),
            dma((3,)),
            dma((nrow // PULL_ROWS + 1,)),
        ],
        compiler_params=params(),
        cost_estimate=cost(10 * n * ch * hid, 24 * 2**20),
        name="decode",
    )(core, rows, *in_hbm(got, stk), head, head_t, w_out_t, w_in_t, gain, ends, *in_hbm(slope, act_t, xhat_t))


def backward_kernel(
    left_ref, right_ref, gain_ref, w_in_t_ref, w_out_t_ref, adv_ref, slope_ref, xhat_ref, both_ref, *rest
):
    out_ref = rest[-1]
    rows, cells, ch = out_ref.shape
    pre_grad = (dot(adv_ref[...], w_out_t_ref[...]) * slope_ref[...].astype(f32)).astype(bf16)
    gained = dot(pre_grad, w_in_t_ref[...]) * gain_ref[...]
    xhat = xhat_ref[...].astype(f32)
    summed_grad = gained - xhat * jnp.mean(gained * xhat, axis=-1, keepdims=True)
    out_ref[...] = both_ref[...].astype(f32) + mixed(summed_grad.reshape(rows, cells, ch), left_ref[...], right_ref[...])


def backward(left, right, gain, w_in_t, w_out_t, adv, inv_slope, xhat, both, begin, end, *before):
    rows, cells, ch = both.shape
    hid = w_in_t.shape[0]
    nr = BACK_ROWS
    step = nr * cells
    base = begin // nr
    edge = pl.BlockSpec((nr, 1, ch), lambda i: (i + base, 0, 0))
    whole = pl.BlockSpec((nr, cells, ch), lambda i: (i + base, 0, 0))
    share = (end - begin) * cells
    return pl.pallas_call(
        backward_kernel,
        grid=((end - begin) // nr,),
        out_shape=pltpu.HBM((rows, cells, ch), f32),
        in_specs=[
            edge,
            edge,
            pl.BlockSpec((1, ch), lambda i: (0, 0)),
            pl.BlockSpec((hid, ch), lambda i: (0, 0)),
            pl.BlockSpec((ch, hid), lambda i: (0, 0)),
            pl.BlockSpec((step, ch), lambda i: (i + base, 0)),
            pl.BlockSpec((step, hid), lambda i: (i + base, 0)),
            pl.BlockSpec((step, ch), lambda i: (i + base, 0)),
            whole,
        ]
        + [OUTSIDE] * len(before),
        out_specs=whole,
        input_output_aliases={9: 0} if before else {},
        compiler_params=params(),
        cost_estimate=cost(4 * share * ch * hid, 3584 * share),
        name="backward",
    )(left, right, gain, w_in_t, w_out_t, *in_hbm(adv, inv_slope, xhat, both, *before))


def edge_kernel(core_ref, outer_ref, grad_ref, out_ref):
    block = grad_ref[...]
    place = lax.broadcasted_iota(jnp.int32, block.shape, 1)
    out_ref[...] = block + jnp.where(place == core_ref[0] * (block.shape[1] - 1), 0.5 * outer_ref[...].astype(f32), 0.0)


def add_outer(core, outer, grad):
    rows, cells, ch = grad.shape
    ends = pl.BlockSpec((rows, 8, ch), lambda i, core: (0, core[0] * (cells // 8 - 1), 0))
    return pl.pallas_call(
        edge_kernel,
        grid_spec=pltpu.PrefetchScalarGridSpec(
            num_scalar_prefetch=1,
            grid=(1,),
            in_specs=[pl.BlockSpec((rows, 1, ch), lambda i, core: (0, 0, 0)), ends],
            out_specs=ends,
        ),
        out_shape=pltpu.HBM(grad.shape, f32),
        input_output_aliases={2: 0},
        compiler_params=params(),
        cost_estimate=cost(rows * 8 * ch, 2**19),
        name="edge",
    )(core, outer, *in_hbm(grad))


def total_kernel(got_ref, out_ref):
    total = jnp.sum(got_ref[...].astype(f32), axis=0, keepdims=True).astype(bf16)
    out_ref[...] = jnp.broadcast_to(total, out_ref.shape)


def total(got):
    return pl.pallas_call(
        total_kernel,
        out_shape=jax.ShapeDtypeStruct(got.shape, bf16),
        compiler_params=params(),
        cost_estimate=cost(got.size, 2 * got.size * 2),
        name="total",
    )(got)


def pair_kernel(keep_ref, came_ref, out_ref, edge_ref):
    out_ref[...] = (keep_ref[...] + came_ref[...].astype(f32)).astype(bf16)
    for chunk, row, lane in edge_tiles(edge_ref.shape):
        edge_ref[row : row + 8, lane : lane + 128] = came_ref[chunk, 16:24, :].astype(f32)


def pair(keep, came, edge):
    return pl.pallas_call(
        pair_kernel,
        out_shape=(jax.ShapeDtypeStruct(keep.shape, bf16), jax.ShapeDtypeStruct(edge.shape, f32)),
        compiler_params=params(),
        cost_estimate=cost(keep.size, 8 * keep.size),
        name="pair",
    )(keep, came)


def finish_kernel(core_ref, mine_ref, other_ref, gain_ref, w_in_ref, in_ref, out_ref, gain_grad_ref, head_ref, *, devices):
    share = 1.0 / devices
    for core in range(2):

        @pl.when(core_ref[0] == core)
        def _(core=core):
            pair = (mine_ref, other_ref) if core == 0 else (other_ref, mine_ref)
            halves = [ref[...].astype(f32) * share for ref in pair]
            x = take_chunks(halves, 0, in_ref.shape)
            in_ref[...] = x * gain_ref[...]
            per_channel = jnp.sum(x * w_in_ref[...].astype(f32), axis=1, keepdims=True)
            gain_grad_ref[...] = jnp.broadcast_to(per_channel, (x.shape[0], 128)).T[0:1, :]
            out_ref[...] = take_chunks(halves, 1, out_ref.shape)
            head_ref[...] = take_chunks(halves, 2, head_ref.shape[::-1]).T


def finish(core, mine, other, gain, w_in, head, devices):
    ch, hid = w_in.shape
    return pl.pallas_call(
        functools.partial(finish_kernel, devices=devices),
        out_shape=(
            jax.ShapeDtypeStruct((ch, hid), f32),
            jax.ShapeDtypeStruct((hid, ch), f32),
            jax.ShapeDtypeStruct((1, ch), f32),
            jax.ShapeDtypeStruct(head.shape, f32),
        ),
        in_specs=[pl.BlockSpec(memory_space=pltpu.SMEM)] + [INSIDE] * 4,
        out_specs=(INSIDE,) * 4,
        compiler_params=params(),
        cost_estimate=cost(4 * ch * hid, 3 * 2**20),
        name="finish",
    )(core, mine, other, gain.reshape(ch, 1), w_in)


LON = ("chip", "core")


def from_sides(first, last):
    count = lax.axis_size("chip") * lax.axis_size("core")
    left = lax.ppermute(last, LON, [(i, (i + 1) % count) for i in range(count)])
    right = lax.ppermute(first, LON, [((i + 1) % count, i) for i in range(count)])
    return left, right


def body(latent, row_index, weights, slots, counts, targets, gain, w_in, w_out, head):
    chips = ("band", "chip")
    swap = [(0, 1), (1, 0)]
    groups = lax.axis_size("band") * lax.axis_size("chip")
    core = lax.axis_index("core").astype(jnp.int32).reshape(1)
    cells = latent.shape[1]
    packed = pack(weights, targets, slots, counts)
    left, right = from_sides(latent[:, 0:1, :], latent[:, cells - 1 : cells, :])
    packed, left, right = lax.optimization_barrier((packed, left, right))
    got = lax.all_to_all(packed, LON, 0, 0, tiled=True)
    left, right = left.astype(f32), right.astype(f32)
    gain_row = gain.reshape(1, -1)
    w_out_t = w_out.T
    w_in_t = w_in.T
    stk, slope, act_t, xhat_t, xhat, inv_slope, ends = forward(latent, left, right, gain_row, w_in, w_out)
    adv, both, keep, send, outer = decode(
        core, row_index, got, stk, head, head.T, w_out_t, w_in_t, gain_row, ends, slope, act_t, xhat_t, groups
    )
    lons = 2 * lax.axis_size("chip")
    outer = lax.ppermute(outer, LON, [(i, (i + (1 if i % 2 else -1)) % lons) for i in range(lons)])
    summed, inner = pair(keep, lax.ppermute(send, "core", swap), outer)
    parts = lax.all_to_all(summed, chips, 0, 0, tiled=True)
    grad_left = jnp.where(core == 1, inner, 0.0)[:, None, :]
    grad_right = jnp.where(core == 0, inner, 0.0)[:, None, :]
    rest = (grad_left, grad_right, gain_row, w_in_t, w_out_t, adv, inv_slope, xhat, both)
    rows = latent.shape[0]
    grad = backward(*rest, 0, rows // 2)
    parts, grad, outer = lax.optimization_barrier((parts, grad, outer))
    outer = outer.astype(f32)[:, None, :]
    mine = lax.all_to_all(total(parts), chips, 0, 0, tiled=True)
    grad = add_outer(core, outer, backward(*rest, rows // 2, rows, grad))
    mine, grad = lax.optimization_barrier((mine, grad))
    other = lax.ppermute(mine, "core", swap)
    grad_in, grad_out, grad_gain, grad_head = finish(core, mine, other, gain, w_in, head, 2 * groups)
    return grad, grad_in, grad_out, grad_gain.reshape(-1), grad_head


def solution(mesh):
    bands, lons = mesh.devices.shape
    by_core = jax.sharding.Mesh(mesh.devices.reshape(bands, lons // 2, 2), ("band", "chip", "core"))
    every = ("band", "chip", "core")
    return jax.shard_map(
        body,
        mesh=by_core,
        in_specs=(
            P("band", LON, None),
            P("band", LON, None),
            P(every, None, None),
            P(every, None),
            P(every),
            P(every, None, None),
            P(),
            P(),
            P(),
            P(),
        ),
        out_specs=(P("band", LON, None), P(), P(), P(), P()),
        check_vma=False,
    )
```

```python
import functools
import math

import jax
import jax.numpy as jnp
from jax import lax
from jax.experimental import pallas as pl
from jax.experimental.pallas import tpu as pltpu
from jax.sharding import PartitionSpec as P

WINDOW_SLOTS = 7
NORM_EPS = 1e-05
ROWS_STEP = 8
BLOCKS_STEP = 8
PULL_ROWS = 8
PACK_CHUNKS = 4
BACK_ROWS = 8
AHEAD = 3
LATER_AT = 0
META = 8

f32 = jnp.float32
bf16 = jnp.bfloat16
INSIDE = pl.BlockSpec(memory_space=pltpu.VMEM)
OUTSIDE = pl.BlockSpec(memory_space=pltpu.HBM)


def dot(a, b):
    return jnp.dot(a, b, preferred_element_type=f32)


def dot_t(a, b):
    return lax.dot_general(a, b, (((0,), (0,)), ((), ())), preferred_element_type=f32)


def params(mib=48):
    return pltpu.CompilerParams(vmem_limit_bytes=mib * 2**20)


def in_hbm(*arrays):
    return [pltpu.with_memory_space_constraint(x, pltpu.HBM) for x in arrays]


def cost(flops, nbytes, trans=0):
    return pl.CostEstimate(flops=flops, bytes_accessed=nbytes, transcendentals=trans)


def pack_kernel(w_hbm, t_hbm, slot_hbm, count_hbm, out_hbm, buf, slots, counts, small_sems, in_sems, out_sems):
    blocks, obs = slots.shape
    nv = t_hbm.shape[1]
    n = blocks // PACK_CHUNKS
    small = [
        pltpu.make_async_copy(slot_hbm, slots, small_sems.at[0]),
        pltpu.make_async_copy(count_hbm, counts, small_sems.at[1]),
    ]
    arrive, leave = [], []
    for c in range(PACK_CHUNKS):
        here = pl.ds(c * n, n)
        arrive.append(
            (
                pltpu.make_async_copy(w_hbm.at[here], buf.at[here, pl.ds(0, obs), :], in_sems.at[2 * c]),
                pltpu.make_async_copy(t_hbm.at[here], buf.at[here, pl.ds(obs, nv), :], in_sems.at[2 * c + 1]),
            )
        )
        leave.append(pltpu.make_async_copy(buf.at[here], out_hbm.at[here], out_sems.at[c]))
    for c in small:
        c.start()
    for pair in arrive:
        for c in pair:
            c.start()
    for c in small:
        c.wait()
    coef = slots[...].astype(f32) / (WINDOW_SLOTS - 1)
    lane = lax.broadcasted_iota(jnp.int32, (META, obs), 1)
    row = lax.broadcasted_iota(jnp.int32, (META, obs), 0)
    for b in range(blocks):
        live = jnp.where(lane < counts[b], 1.0, 0.0)
        buf[b, obs + nv : obs + nv + META, :] = jnp.where(row == 0, coef[b : b + 1, :], live).astype(bf16)
    for pair, out in zip(arrive, leave):
        for c in pair:
            c.wait()
        out.start()
    for c in leave:
        c.wait()


def pack(weights, targets, slots, counts):
    blocks, obs, cells = weights.shape
    shape = (blocks, 2 * obs + META, cells)
    dma = pltpu.SemaphoreType.DMA
    return pl.pallas_call(
        pack_kernel,
        out_shape=pltpu.HBM(shape, bf16),
        in_specs=[OUTSIDE] * 4,
        out_specs=OUTSIDE,
        scratch_shapes=[
            pltpu.VMEM(shape, bf16),
            pltpu.VMEM(slots.shape, jnp.int32),
            pltpu.SMEM(counts.shape, jnp.int32),
            dma((2,)),
            dma((2 * PACK_CHUNKS,)),
            dma((PACK_CHUNKS,)),
        ],
        compiler_params=params(),
        cost_estimate=cost(1, 4 * 2**20),
        name="pack",
    )(*in_hbm(weights, targets, slots, counts))


def mixed(x, left, right):
    cells = x.shape[1]
    place = lax.broadcasted_iota(jnp.int32, x.shape, 1)
    from_left = jnp.where(place == 0, left, pltpu.roll(x, 1, 1))
    from_right = jnp.where(place == cells - 1, right, pltpu.roll(x, cells - 1, 1))
    return x + 0.5 * (from_left + from_right)


def normalized(lat, left, right):
    summed = mixed(lat, left, right)
    inv = lax.rsqrt(jnp.mean(summed * summed, axis=-1, keepdims=True) + NORM_EPS)
    return summed * inv, inv


def forward_kernel(
    lat_ref, left_ref, right_ref, gain_ref, w_in_ref, w_out_ref, head_ref,
    shown_ref, lat_t_ref, slope_ref, act_t_ref, xhat_t_ref, xhat_ref, inv_slope_ref, ends_ref,
):
    rows, cells, ch = lat_ref.shape
    lat_b = lat_ref[...]
    lat = lat_b.astype(f32)
    xhat3, inv3 = normalized(lat, left_ref[...], right_ref[...])
    for k, cell in enumerate((0, cells - 1)):
        ends_ref[2 * k] = xhat3[:, cell, :]
        ends_ref[2 * k + 1] = jnp.broadcast_to(inv3[:, cell, :], (rows, ch))
    xhat = xhat3.reshape(rows * cells, ch)
    pre = dot((xhat * gain_ref[...]).astype(bf16), w_in_ref[...])
    sig = jax.nn.sigmoid(pre)
    act = pre * sig
    act_b = act.astype(bf16)
    slope = sig * (1.0 + pre * (1.0 - sig))
    slope_ref[...] = slope.astype(bf16)
    inv_slope_ref[...] = (slope * inv3.reshape(rows * cells, 1)).astype(bf16)
    new = (lat.reshape(rows * cells, ch) + dot(act_b, w_out_ref[...])).astype(bf16)
    old = lat_b.reshape(rows * cells, ch)
    for k, tile in enumerate((old, new)):
        shown = dot(tile, head_ref[...]).astype(bf16)
        shown_ref[:, k * cells : (k + 1) * cells, :] = shown.reshape(rows, cells, shown.shape[1])
    lat_t_ref[...] = old.T
    xhat_b = xhat.astype(bf16)
    xhat_ref[...] = xhat_b
    act_t_ref[...] = act_b.T
    xhat_t_ref[...] = xhat_b.T


def forward(latent, left, right, gain, w_in, w_out, head):
    rows, cells, ch = latent.shape
    hid = w_in.shape[1]
    nv = head.shape[1]
    n = rows * cells
    step = ROWS_STEP * cells
    return pl.pallas_call(
        forward_kernel,
        grid=(rows // ROWS_STEP,),
        out_shape=(
            pltpu.HBM((rows, 2 * cells, nv), bf16),
            pltpu.HBM((ch, n), bf16),
            pltpu.HBM((n, hid), bf16),
            pltpu.HBM((hid, n), bf16),
            pltpu.HBM((ch, n), bf16),
            pltpu.HBM((n, ch), bf16),
            pltpu.HBM((n, hid), bf16),
            jax.ShapeDtypeStruct((4, rows, ch), f32),
        ),
        in_specs=[
            pl.BlockSpec((ROWS_STEP, cells, ch), lambda i: (i, 0, 0)),
            pl.BlockSpec((ROWS_STEP, 1, ch), lambda i: (i, 0, 0)),
            pl.BlockSpec((ROWS_STEP, 1, ch), lambda i: (i, 0, 0)),
            pl.BlockSpec((1, ch), lambda i: (0, 0)),
            pl.BlockSpec((ch, hid), lambda i: (0, 0)),
            pl.BlockSpec((hid, ch), lambda i: (0, 0)),
            pl.BlockSpec((ch, nv), lambda i: (0, 0)),
        ],
        out_specs=(
            pl.BlockSpec((ROWS_STEP, 2 * cells, nv), lambda i: (i, 0, 0)),
            pl.BlockSpec((ch, step), lambda i: (0, i)),
            pl.BlockSpec((step, hid), lambda i: (i, 0)),
            pl.BlockSpec((hid, step), lambda i: (0, i)),
            pl.BlockSpec((ch, step), lambda i: (0, i)),
            pl.BlockSpec((step, ch), lambda i: (i, 0)),
            pl.BlockSpec((step, hid), lambda i: (i, 0)),
            pl.BlockSpec((4, ROWS_STEP, ch), lambda i: (0, i, 0)),
        ),
        compiler_params=params(),
        cost_estimate=cost(4 * n * ch * hid, 16 * 2**20, 2 * n * hid),
        name="forward",
    )(latent, left, right, gain, w_in, w_out, head)


def decode_kernel(
    core_ref, rows_ref, got_hbm, shown_hbm, head_t_ref, joint_ref, w_out_t_ref, w_in_t_ref, gain_ref, ends_ref,
    slope_hbm, act_t_hbm, xhat_t_hbm, lat_t_hbm,
    q_hbm, keep_ref, send_ref, outer_ref,
    got, shown, slope, act_t, xhat_t, lat_t, q_all, ends, acc_q, acc_head, acc_in, acc_act,
    got_sems, shown_sems, in_sems, q_sems,
):
    nb, nr = BLOCKS_STEP, PULL_ROWS
    blocks = got.shape[0]
    nv, ch = head_t_ref.shape
    obs = (got.shape[1] - META) // 2
    rows, cells, _ = acc_q.shape
    scale = 1.0 / math.sqrt(obs)
    step = nr * cells

    def got_copy(i):
        here = pl.ds(i * nb, nb)
        return pltpu.make_async_copy(got_hbm.at[here], got.at[here], got_sems.at[i])

    def shown_copy(b):
        return pltpu.make_async_copy(shown_hbm.at[rows_ref[0, 0, b]], shown.at[b], shown_sems.at[b])

    def q_copy(k):
        flat = pl.ds(pl.multiple_of(k * step, step), step)
        return pltpu.make_async_copy(q_all.at[flat], q_hbm.at[flat], q_sems.at[k])

    def chunk_copies(k):
        flat = pl.ds(pl.multiple_of(k * step, step), step)
        turned = ((lat_t_hbm, lat_t), (xhat_t_hbm, xhat_t), (act_t_hbm, act_t))
        return [pltpu.make_async_copy(slope_hbm.at[flat], slope.at[flat], in_sems.at[0, k])] + [
            pltpu.make_async_copy(src.at[:, flat], dst.at[:, flat], in_sems.at[1 + i, k]) for i, (src, dst) in enumerate(turned)
        ]

    def start(i):
        got_copy(i).start()
        for j in range(nb):
            shown_copy(i * nb + j).start()

    for i in range(AHEAD):
        start(i)
    for acc in (acc_q, acc_head, acc_in, acc_act):
        acc[...] = jnp.zeros_like(acc)

    def observe(i, carry):
        first = i * nb
        got_copy(i).wait()
        for j in range(nb):
            shown_copy(first + j).wait()

        @pl.when(i + AHEAD < blocks // nb)
        def _():
            start(i + AHEAD)

        @pl.when(i == LATER_AT)
        def _():
            for k in range(rows // nr):
                for c in chunk_copies(k):
                    c.start()

        places = [rows_ref[0, 0, first + j] for j in range(nb)]
        meta = jnp.concatenate([got[first + j, 2 * obs : 2 * obs + META, :].astype(f32) for j in range(nb)], axis=0).T
        preds = []
        for j in range(nb):
            t = meta[:, META * j : META * j + 1]
            w = got[first + j, 0:obs, :]
            w_new = w * jnp.broadcast_to(t, w.shape).astype(bf16)
            preds.append(dot(jnp.concatenate([w - w_new, w_new], axis=1), shown[first + j]))
        grads = []
        for j in range(nb):
            t, live = meta[:, META * j : META * j + 1], meta[:, META * j + 1 : META * j + 2]
            residual = jnp.where(live > 0.5, preds[j] - got[first + j, obs : 2 * obs, :].astype(f32), 0.0) * scale
            grads.append(jnp.concatenate([residual.astype(bf16), (residual * t).astype(bf16)], axis=1))
        pulled = [dot_t(got[first + j, 0:obs, :], grads[j]) for j in range(nb)]
        for j in range(nb):
            acc_q[places[j]] += pulled[j]
        return carry

    lax.fori_loop(0, blocks // nb, observe, 0)
    def pull(k, carry):
        flat = pl.ds(pl.multiple_of(k * step, step), step)
        for c in chunk_copies(k):
            c.wait()
        q = acc_q[pl.ds(k * nr, nr)].reshape(step, 2 * nv).astype(bf16)
        q_all[flat, :] = q
        q_copy(k).start()
        pre_grad = (dot(q[:, nv:], joint_ref[...]) * slope[flat, :].astype(f32)).astype(bf16)
        acc_act[...] += dot(act_t[:, flat], q[:, nv:])
        acc_head[...] += dot(lat_t[:, flat], q[:, :nv])
        here = pl.ds(pl.multiple_of(k * nr, nr), nr)
        by_row = pre_grad.reshape(nr, cells, pre_grad.shape[1])
        ends[0, here, :] = by_row[:, 0, :].astype(f32)
        ends[1, here, :] = by_row[:, cells - 1, :].astype(f32)
        acc_in[...] += dot(xhat_t[:, flat], pre_grad)
        return carry

    lax.fori_loop(0, rows // nr, pull, 0)
    by_hidden = acc_act[...].astype(bf16)
    out_sum = dot(by_hidden, head_t_ref[...])
    head_sum = (acc_head[...] + dot(w_out_t_ref[...], by_hidden)).T
    edges = []
    for k in range(2):
        gained = dot(ends[k].astype(bf16), w_in_t_ref[...]) * gain_ref[...]
        xhat, inv = ends_ref[2 * k], ends_ref[2 * k + 1]
        edges.append(inv * (gained - xhat * jnp.mean(gained * xhat, axis=-1, keepdims=True)))
    for core in range(2):

        @pl.when(core_ref[0] == core)
        def _(core=core):
            put_chunks(keep_ref, core, acc_in, out_sum, head_sum)
            put_chunks(send_ref, 1 - core, acc_in, out_sum, head_sum)
            outer_ref[...] = edges[core].astype(bf16)
            put_edge(send_ref, edges[1 - core])

    for k in range(rows // nr):
        q_copy(k).wait()


def put_chunks(ref, half, *accs):
    for p, acc in enumerate(accs):
        down = acc.shape[0] // 8
        across = acc.shape[1] // 256
        for j in range(across):
            at = 128 * (half * across + j)
            tiles = acc[:, at : at + 128].reshape(down, 8, 128)
            ref[down * j : down * (j + 1), 8 * p : 8 * p + 8, :] = tiles.astype(ref.dtype)
        if down * across < ref.shape[0]:
            rest = ref.shape[0] - down * across
            ref[down * across :, 8 * p : 8 * p + 8, :] = jnp.zeros((rest, 8, 128), ref.dtype)


def edge_tiles(shape):
    first = 16
    return [(first + k, 8 * (k % (shape[0] // 8)), 128 * (k // (shape[0] // 8))) for k in range(shape[0] * shape[1] // 1024)]


def put_edge(ref, edge):
    for chunk, row, lane in edge_tiles(edge.shape):
        ref[chunk, 16:24, :] = edge[row : row + 8, lane : lane + 128].astype(ref.dtype)


def take_chunks(halves, part, shape):
    down = shape[0] // 8
    across = shape[1] // 256
    return jnp.concatenate(
        [
            half[down * j : down * (j + 1), 8 * part : 8 * part + 8, :].reshape(shape[0], 128)
            for half in halves
            for j in range(across)
        ],
        axis=1,
    )


def decode(core, rows, got, shown, head_t, joint, w_out_t, w_in_t, gain, ends, slope, act_t, xhat_t, lat_t, chunks):
    nrow, two_cells, nv = shown.shape
    cells = two_cells // 2
    ch = head_t.shape[1]
    hid = w_out_t.shape[1]
    n = nrow * cells
    blocks = got.shape[0]
    dma = pltpu.SemaphoreType.DMA
    scalars = pl.BlockSpec(memory_space=pltpu.SMEM)
    return pl.pallas_call(
        decode_kernel,
        out_shape=(
            pltpu.HBM((n, 2 * nv), bf16),
            jax.ShapeDtypeStruct((chunks, 24, 128), f32),
            jax.ShapeDtypeStruct((chunks, 24, 128), bf16),
            jax.ShapeDtypeStruct((nrow, ch), bf16),
        ),
        in_specs=[scalars] * 2 + [OUTSIDE] * 2 + [INSIDE] * 6 + [OUTSIDE] * 4,
        out_specs=(OUTSIDE,) + (INSIDE,) * 3,
        scratch_shapes=[pltpu.VMEM(x.shape, bf16) for x in (got, shown, slope, act_t, xhat_t, lat_t)]
        + [
            pltpu.VMEM((n, 2 * nv), bf16),
            pltpu.VMEM((2, nrow, hid), f32),
            pltpu.VMEM((nrow, cells, 2 * nv), f32),
            pltpu.VMEM((ch, nv), f32),
            pltpu.VMEM((ch, hid), f32),
            pltpu.VMEM((hid, nv), f32),
            dma((blocks // BLOCKS_STEP,)),
            dma((blocks,)),
            dma((4, nrow // PULL_ROWS)),
            dma((nrow // PULL_ROWS,)),
        ],
        compiler_params=params(),
        cost_estimate=cost(10 * n * ch * hid, 24 * 2**20),
        name="decode",
    )(core, rows, *in_hbm(got, shown), head_t, joint, w_out_t, w_in_t, gain, ends, *in_hbm(slope, act_t, xhat_t, lat_t))


def backward_kernel(
    left_ref, right_ref, gain_ref, w_in_t_ref, joint_ref, head_t_ref, q_ref, slope_ref, xhat_ref, *rest
):
    out_ref = rest[-1]
    rows, cells, ch = out_ref.shape
    nv = head_t_ref.shape[0]
    pre_grad = (dot(q_ref[:, nv:], joint_ref[...]) * slope_ref[...].astype(f32)).astype(bf16)
    both = dot(q_ref[:, :nv], head_t_ref[...]).reshape(rows, cells, ch)
    gained = dot(pre_grad, w_in_t_ref[...]) * gain_ref[...]
    xhat = xhat_ref[...].astype(f32)
    summed_grad = gained - xhat * jnp.mean(gained * xhat, axis=-1, keepdims=True)
    out_ref[...] = both + mixed(summed_grad.reshape(rows, cells, ch), left_ref[...], right_ref[...])


def backward(left, right, gain, w_in_t, joint, head_t, q, inv_slope, xhat, begin, end, *before):
    rows, ch = left.shape[0], left.shape[2]
    cells = xhat.shape[0] // rows
    nv, hid = joint.shape
    nr = BACK_ROWS
    step = nr * cells
    base = begin // nr
    edge = pl.BlockSpec((nr, 1, ch), lambda i: (i + base, 0, 0))
    whole = pl.BlockSpec((nr, cells, ch), lambda i: (i + base, 0, 0))
    share = (end - begin) * cells
    return pl.pallas_call(
        backward_kernel,
        grid=((end - begin) // nr,),
        out_shape=pltpu.HBM((rows, cells, ch), f32),
        in_specs=[
            edge,
            edge,
            pl.BlockSpec((1, ch), lambda i: (0, 0)),
            pl.BlockSpec((hid, ch), lambda i: (0, 0)),
            pl.BlockSpec((nv, hid), lambda i: (0, 0)),
            pl.BlockSpec((nv, ch), lambda i: (0, 0)),
            pl.BlockSpec((step, 2 * nv), lambda i: (i + base, 0)),
            pl.BlockSpec((step, hid), lambda i: (i + base, 0)),
            pl.BlockSpec((step, ch), lambda i: (i + base, 0)),
        ]
        + [OUTSIDE] * len(before),
        out_specs=whole,
        input_output_aliases={9: 0} if before else {},
        compiler_params=params(),
        cost_estimate=cost(4 * share * ch * hid, 3584 * share),
        name="backward",
    )(left, right, gain, w_in_t, joint, head_t, *in_hbm(q, inv_slope, xhat, *before))


def edge_kernel(core_ref, outer_ref, grad_ref, out_ref):
    block = grad_ref[...]
    place = lax.broadcasted_iota(jnp.int32, block.shape, 1)
    out_ref[...] = block + jnp.where(place == core_ref[0] * (block.shape[1] - 1), 0.5 * outer_ref[...].astype(f32), 0.0)


def add_outer(core, outer, grad):
    rows, cells, ch = grad.shape
    ends = pl.BlockSpec((rows, 8, ch), lambda i, core: (0, core[0] * (cells // 8 - 1), 0))
    return pl.pallas_call(
        edge_kernel,
        grid_spec=pltpu.PrefetchScalarGridSpec(
            num_scalar_prefetch=1,
            grid=(1,),
            in_specs=[pl.BlockSpec((rows, 1, ch), lambda i, core: (0, 0, 0)), ends],
            out_specs=ends,
        ),
        out_shape=pltpu.HBM(grad.shape, f32),
        input_output_aliases={2: 0},
        compiler_params=params(),
        cost_estimate=cost(rows * 8 * ch, 2**19),
        name="edge",
    )(core, outer, *in_hbm(grad))


def total_kernel(got_ref, out_ref):
    total = jnp.sum(got_ref[...].astype(f32), axis=0, keepdims=True).astype(bf16)
    out_ref[...] = jnp.broadcast_to(total, out_ref.shape)


def total(got):
    return pl.pallas_call(
        total_kernel,
        out_shape=jax.ShapeDtypeStruct(got.shape, bf16),
        compiler_params=params(),
        cost_estimate=cost(got.size, 2 * got.size * 2),
        name="total",
    )(got)


def pair_kernel(keep_ref, came_ref, out_ref, edge_ref):
    out_ref[...] = (keep_ref[...] + came_ref[...].astype(f32)).astype(bf16)
    for chunk, row, lane in edge_tiles(edge_ref.shape):
        edge_ref[row : row + 8, lane : lane + 128] = came_ref[chunk, 16:24, :].astype(f32)


def pair(keep, came, edge):
    return pl.pallas_call(
        pair_kernel,
        out_shape=(jax.ShapeDtypeStruct(keep.shape, bf16), jax.ShapeDtypeStruct(edge.shape, f32)),
        compiler_params=params(),
        cost_estimate=cost(keep.size, 8 * keep.size),
        name="pair",
    )(keep, came)


def finish_kernel(core_ref, mine_ref, other_ref, gain_ref, w_in_ref, in_ref, out_ref, gain_grad_ref, head_ref, *, devices):
    share = 1.0 / devices
    for core in range(2):

        @pl.when(core_ref[0] == core)
        def _(core=core):
            pair = (mine_ref, other_ref) if core == 0 else (other_ref, mine_ref)
            halves = [ref[...].astype(f32) * share for ref in pair]
            x = take_chunks(halves, 0, in_ref.shape)
            in_ref[...] = x * gain_ref[...]
            per_channel = jnp.sum(x * w_in_ref[...].astype(f32), axis=1, keepdims=True)
            gain_grad_ref[...] = jnp.broadcast_to(per_channel, (x.shape[0], 128)).T[0:1, :]
            out_ref[...] = take_chunks(halves, 1, out_ref.shape)
            head_ref[...] = take_chunks(halves, 2, head_ref.shape[::-1]).T


def finish(core, mine, other, gain, w_in, head, devices):
    ch, hid = w_in.shape
    return pl.pallas_call(
        functools.partial(finish_kernel, devices=devices),
        out_shape=(
            jax.ShapeDtypeStruct((ch, hid), f32),
            jax.ShapeDtypeStruct((hid, ch), f32),
            jax.ShapeDtypeStruct((1, ch), f32),
            jax.ShapeDtypeStruct(head.shape, f32),
        ),
        in_specs=[pl.BlockSpec(memory_space=pltpu.SMEM)] + [INSIDE] * 4,
        out_specs=(INSIDE,) * 4,
        compiler_params=params(),
        cost_estimate=cost(4 * ch * hid, 3 * 2**20),
        name="finish",
    )(core, mine, other, gain.reshape(ch, 1), w_in)


LON = ("chip", "core")


def from_sides(first, last):
    count = lax.axis_size("chip") * lax.axis_size("core")
    left = lax.ppermute(last, LON, [(i, (i + 1) % count) for i in range(count)])
    right = lax.ppermute(first, LON, [((i + 1) % count, i) for i in range(count)])
    return left, right


def body(latent, row_index, weights, slots, counts, targets, gain, w_in, w_out, head):
    chips = ("band", "chip")
    swap = [(0, 1), (1, 0)]
    groups = lax.axis_size("band") * lax.axis_size("chip")
    core = lax.axis_index("core").astype(jnp.int32).reshape(1)
    cells = latent.shape[1]
    packed = pack(weights, targets, slots, counts)
    left, right = from_sides(latent[:, 0:1, :], latent[:, cells - 1 : cells, :])
    packed, left, right = lax.optimization_barrier((packed, left, right))
    got = lax.all_to_all(packed, LON, 0, 0, tiled=True)
    left, right = left.astype(f32), right.astype(f32)
    gain_row = gain.reshape(1, -1)
    w_out_t = w_out.T
    w_in_t = w_in.T
    shown, lat_t, slope, act_t, xhat_t, xhat, inv_slope, ends = forward(
        latent, left, right, gain_row, w_in, w_out, head
    )
    head_t = head.T
    joint = dot(head_t, w_out_t).astype(bf16)
    q, keep, send, outer = decode(
        core, row_index, got, shown, head_t, joint, w_out_t, w_in_t, gain_row, ends, slope, act_t, xhat_t, lat_t, groups
    )
    lons = 2 * lax.axis_size("chip")
    outer = lax.ppermute(outer, LON, [(i, (i + (1 if i % 2 else -1)) % lons) for i in range(lons)])
    summed, inner = pair(keep, lax.ppermute(send, "core", swap), outer)
    parts = lax.all_to_all(summed, chips, 0, 0, tiled=True)
    grad_left = jnp.where(core == 1, inner, 0.0)[:, None, :]
    grad_right = jnp.where(core == 0, inner, 0.0)[:, None, :]
    rest = (grad_left, grad_right, gain_row, w_in_t, joint, head_t, q, inv_slope, xhat)
    rows = latent.shape[0]
    grad = backward(*rest, 0, rows // 2)
    parts, grad, outer = lax.optimization_barrier((parts, grad, outer))
    outer = outer.astype(f32)[:, None, :]
    mine = lax.all_to_all(total(parts), chips, 0, 0, tiled=True)
    grad = add_outer(core, outer, backward(*rest, rows // 2, rows, grad))
    mine, grad = lax.optimization_barrier((mine, grad))
    other = lax.ppermute(mine, "core", swap)
    grad_in, grad_out, grad_gain, grad_head = finish(core, mine, other, gain, w_in, head, 2 * groups)
    return grad, grad_in, grad_out, grad_gain.reshape(-1), grad_head


def solution(mesh):
    bands, lons = mesh.devices.shape
    by_core = jax.sharding.Mesh(mesh.devices.reshape(bands, lons // 2, 2), ("band", "chip", "core"))
    every = ("band", "chip", "core")
    return jax.shard_map(
        body,
        mesh=by_core,
        in_specs=(
            P("band", LON, None),
            P("band", LON, None),
            P(every, None, None),
            P(every, None),
            P(every),
            P(every, None, None),
            P(),
            P(),
            P(),
            P(),
        ),
        out_specs=(P("band", LON, None), P(), P(), P(), P()),
        check_vma=False,
    )
```

```python
import functools
import math

import jax
import jax.numpy as jnp
from jax import lax
from jax.experimental import pallas as pl
from jax.experimental.pallas import tpu as pltpu
from jax.sharding import PartitionSpec as P

WINDOW_SLOTS = 7
NORM_EPS = 1e-05
ROWS_STEP = 8
BLOCKS_STEP = 8
PULL_ROWS = 8
PACK_CHUNKS = 4
BACK_ROWS = 8
AHEAD = 3
LATER_AT = 0
META = 8

f32 = jnp.float32
bf16 = jnp.bfloat16
INSIDE = pl.BlockSpec(memory_space=pltpu.VMEM)
OUTSIDE = pl.BlockSpec(memory_space=pltpu.HBM)


def dot(a, b):
    return jnp.dot(a, b, preferred_element_type=f32)


def dot_t(a, b):
    return lax.dot_general(a, b, (((0,), (0,)), ((), ())), preferred_element_type=f32)


def params(mib=48):
    return pltpu.CompilerParams(vmem_limit_bytes=mib * 2**20)


def in_hbm(*arrays):
    return [pltpu.with_memory_space_constraint(x, pltpu.HBM) for x in arrays]


def cost(flops, nbytes, trans=0):
    return pl.CostEstimate(flops=flops, bytes_accessed=nbytes, transcendentals=trans)


def pack_kernel(w_hbm, t_hbm, slot_hbm, count_hbm, out_hbm, buf, slots, counts, small_sems, in_sems, out_sems):
    blocks, obs = slots.shape
    nv = t_hbm.shape[1]
    n = blocks // PACK_CHUNKS
    small = [
        pltpu.make_async_copy(slot_hbm, slots, small_sems.at[0]),
        pltpu.make_async_copy(count_hbm, counts, small_sems.at[1]),
    ]
    arrive, leave = [], []
    for c in range(PACK_CHUNKS):
        here = pl.ds(c * n, n)
        arrive.append(
            (
                pltpu.make_async_copy(w_hbm.at[here], buf.at[here, pl.ds(0, obs), :], in_sems.at[2 * c]),
                pltpu.make_async_copy(t_hbm.at[here], buf.at[here, pl.ds(obs, nv), :], in_sems.at[2 * c + 1]),
            )
        )
        leave.append(pltpu.make_async_copy(buf.at[here], out_hbm.at[here], out_sems.at[c]))
    for c in small:
        c.start()
    for pair in arrive:
        for c in pair:
            c.start()
    for c in small:
        c.wait()
    coef = slots[...].astype(f32) / (WINDOW_SLOTS - 1)
    lane = lax.broadcasted_iota(jnp.int32, (META, obs), 1)
    row = lax.broadcasted_iota(jnp.int32, (META, obs), 0)
    for b in range(blocks):
        live = jnp.where(lane < counts[b], 1.0, 0.0)
        buf[b, obs + nv : obs + nv + META, :] = jnp.where(row == 0, coef[b : b + 1, :], live).astype(bf16)
    for pair, out in zip(arrive, leave):
        for c in pair:
            c.wait()
        out.start()
    for c in leave:
        c.wait()


def pack(weights, targets, slots, counts):
    blocks, obs, cells = weights.shape
    shape = (blocks, 2 * obs + META, cells)
    dma = pltpu.SemaphoreType.DMA
    return pl.pallas_call(
        pack_kernel,
        out_shape=pltpu.HBM(shape, bf16),
        in_specs=[OUTSIDE] * 4,
        out_specs=OUTSIDE,
        scratch_shapes=[
            pltpu.VMEM(shape, bf16),
            pltpu.VMEM(slots.shape, jnp.int32),
            pltpu.SMEM(counts.shape, jnp.int32),
            dma((2,)),
            dma((2 * PACK_CHUNKS,)),
            dma((PACK_CHUNKS,)),
        ],
        compiler_params=params(),
        cost_estimate=cost(1, 4 * 2**20),
        name="pack",
    )(*in_hbm(weights, targets, slots, counts))


def mixed(x, left, right):
    cells = x.shape[1]
    place = lax.broadcasted_iota(jnp.int32, x.shape, 1)
    from_left = jnp.where(place == 0, left, pltpu.roll(x, 1, 1))
    from_right = jnp.where(place == cells - 1, right, pltpu.roll(x, cells - 1, 1))
    return x + 0.5 * (from_left + from_right)


def normalized(lat, left, right):
    summed = mixed(lat, left, right)
    inv = lax.rsqrt(jnp.mean(summed * summed, axis=-1, keepdims=True) + NORM_EPS)
    return summed * inv, inv


def forward_kernel(
    lat_ref, left_ref, right_ref, gain_ref, w_in_ref, w_out_ref, head_ref,
    shown_ref, lat_t_ref, slope_ref, act_t_ref, xhat_t_ref, xhat_ref, inv_slope_ref, ends_ref,
):
    rows, cells, ch = lat_ref.shape
    lat_b = lat_ref[...]
    lat = lat_b.astype(f32)
    xhat3, inv3 = normalized(lat, left_ref[...], right_ref[...])
    for k, cell in enumerate((0, cells - 1)):
        ends_ref[2 * k] = xhat3[:, cell, :]
        ends_ref[2 * k + 1] = jnp.broadcast_to(inv3[:, cell, :], (rows, ch))
    xhat = xhat3.reshape(rows * cells, ch)
    pre = dot((xhat * gain_ref[...]).astype(bf16), w_in_ref[...])
    sig = jax.nn.sigmoid(pre)
    act = pre * sig
    act_b = act.astype(bf16)
    slope = sig * (1.0 + pre * (1.0 - sig))
    slope_ref[...] = slope.astype(bf16)
    inv_slope_ref[...] = (slope * inv3.reshape(rows * cells, 1)).astype(bf16)
    new = (lat.reshape(rows * cells, ch) + dot(act_b, w_out_ref[...])).astype(bf16)
    old = lat_b.reshape(rows * cells, ch)
    for k, tile in enumerate((old, new)):
        shown = dot(tile, head_ref[...]).astype(bf16)
        shown_ref[:, k * cells : (k + 1) * cells, :] = shown.reshape(rows, cells, shown.shape[1])
    lat_t_ref[...] = old.T
    xhat_b = xhat.astype(bf16)
    xhat_ref[...] = xhat_b
    act_t_ref[...] = act_b.T
    xhat_t_ref[...] = xhat_b.T


def forward(latent, left, right, gain, w_in, w_out, head):
    rows, cells, ch = latent.shape
    hid = w_in.shape[1]
    nv = head.shape[1]
    n = rows * cells
    step = ROWS_STEP * cells
    return pl.pallas_call(
        forward_kernel,
        grid=(rows // ROWS_STEP,),
        out_shape=(
            pltpu.HBM((rows, 2 * cells, nv), bf16),
            pltpu.HBM((ch, n), bf16),
            pltpu.HBM((n, hid), bf16),
            pltpu.HBM((hid, n), bf16),
            pltpu.HBM((ch, n), bf16),
            pltpu.HBM((n, ch), bf16),
            pltpu.HBM((n, hid), bf16),
            pltpu.HBM((4, rows, ch), f32),
        ),
        in_specs=[
            pl.BlockSpec((ROWS_STEP, cells, ch), lambda i: (i, 0, 0)),
            pl.BlockSpec((ROWS_STEP, 1, ch), lambda i: (i, 0, 0)),
            pl.BlockSpec((ROWS_STEP, 1, ch), lambda i: (i, 0, 0)),
            pl.BlockSpec((1, ch), lambda i: (0, 0)),
            pl.BlockSpec((ch, hid), lambda i: (0, 0)),
            pl.BlockSpec((hid, ch), lambda i: (0, 0)),
            pl.BlockSpec((ch, nv), lambda i: (0, 0)),
        ],
        out_specs=(
            pl.BlockSpec((ROWS_STEP, 2 * cells, nv), lambda i: (i, 0, 0)),
            pl.BlockSpec((ch, step), lambda i: (0, i)),
            pl.BlockSpec((step, hid), lambda i: (i, 0)),
            pl.BlockSpec((hid, step), lambda i: (0, i)),
            pl.BlockSpec((ch, step), lambda i: (0, i)),
            pl.BlockSpec((step, ch), lambda i: (i, 0)),
            pl.BlockSpec((step, hid), lambda i: (i, 0)),
            pl.BlockSpec((4, ROWS_STEP, ch), lambda i: (0, i, 0)),
        ),
        compiler_params=params(),
        cost_estimate=cost(4 * n * ch * hid, 16 * 2**20, 2 * n * hid),
        name="forward",
    )(latent, left, right, gain, w_in, w_out, head)


def decode_kernel(
    core_ref, rows_ref, got_hbm, shown_hbm, head_t_ref, joint_ref, w_out_t_ref, w_in_t_ref, gain_ref,
    ends_hbm, slope_hbm, act_t_hbm, xhat_t_hbm, lat_t_hbm,
    q_hbm, keep_ref, send_ref, outer_ref,
    got, shown, slope, act_t, xhat_t, lat_t, q_all, ends_ref, ends, acc_q, acc_head, acc_in, acc_act,
    got_sems, shown_sems, in_sems, q_sems, ends_sem,
):
    nb, nr = BLOCKS_STEP, PULL_ROWS
    blocks = got.shape[0]
    nv, ch = head_t_ref.shape
    obs = (got.shape[1] - META) // 2
    rows, cells, _ = acc_q.shape
    scale = 1.0 / math.sqrt(obs)
    step = nr * cells

    def got_copy(i):
        here = pl.ds(i * nb, nb)
        return pltpu.make_async_copy(got_hbm.at[here], got.at[here], got_sems.at[i])

    def shown_copy(b):
        return pltpu.make_async_copy(shown_hbm.at[rows_ref[0, 0, b]], shown.at[b], shown_sems.at[b])

    def q_copy(k):
        flat = pl.ds(pl.multiple_of(k * step, step), step)
        return pltpu.make_async_copy(q_all.at[flat], q_hbm.at[flat], q_sems.at[k])

    def chunk_copies(k):
        flat = pl.ds(pl.multiple_of(k * step, step), step)
        turned = ((lat_t_hbm, lat_t), (xhat_t_hbm, xhat_t), (act_t_hbm, act_t))
        return [pltpu.make_async_copy(slope_hbm.at[flat], slope.at[flat], in_sems.at[0, k])] + [
            pltpu.make_async_copy(src.at[:, flat], dst.at[:, flat], in_sems.at[1 + i, k]) for i, (src, dst) in enumerate(turned)
        ]

    def start(i):
        got_copy(i).start()
        for j in range(nb):
            shown_copy(i * nb + j).start()

    for i in range(AHEAD):
        start(i)
    ends_copy = pltpu.make_async_copy(ends_hbm, ends_ref, ends_sem.at[0])
    ends_copy.start()
    for acc in (acc_q, acc_head, acc_in, acc_act):
        acc[...] = jnp.zeros_like(acc)

    def observe(i, carry):
        first = i * nb
        got_copy(i).wait()
        for j in range(nb):
            shown_copy(first + j).wait()

        @pl.when(i + AHEAD < blocks // nb)
        def _():
            start(i + AHEAD)

        @pl.when(i == LATER_AT)
        def _():
            for k in range(rows // nr):
                for c in chunk_copies(k):
                    c.start()

        places = [rows_ref[0, 0, first + j] for j in range(nb)]
        meta = jnp.concatenate([got[first + j, 2 * obs : 2 * obs + META, :].astype(f32) for j in range(nb)], axis=0).T
        preds = []
        for j in range(nb):
            t = meta[:, META * j : META * j + 1]
            w = got[first + j, 0:obs, :]
            w_new = w * jnp.broadcast_to(t, w.shape).astype(bf16)
            preds.append(dot(jnp.concatenate([w - w_new, w_new], axis=1), shown[first + j]))
        grads = []
        for j in range(nb):
            t, live = meta[:, META * j : META * j + 1], meta[:, META * j + 1 : META * j + 2]
            residual = jnp.where(live > 0.5, preds[j] - got[first + j, obs : 2 * obs, :].astype(f32), 0.0) * scale
            grads.append(jnp.concatenate([residual.astype(bf16), (residual * t).astype(bf16)], axis=1))
        pulled = [dot_t(got[first + j, 0:obs, :], grads[j]) for j in range(nb)]
        for j in range(nb):
            acc_q[places[j]] += pulled[j]
        return carry

    lax.fori_loop(0, blocks // nb, observe, 0)
    def pull(k, carry):
        flat = pl.ds(pl.multiple_of(k * step, step), step)
        for c in chunk_copies(k):
            c.wait()
        q = acc_q[pl.ds(k * nr, nr)].reshape(step, 2 * nv).astype(bf16)
        q_all[flat, :] = q
        q_copy(k).start()
        pre_grad = (dot(q[:, nv:], joint_ref[...]) * slope[flat, :].astype(f32)).astype(bf16)
        acc_act[...] += dot(act_t[:, flat], q[:, nv:])
        acc_head[...] += dot(lat_t[:, flat], q[:, :nv])
        here = pl.ds(pl.multiple_of(k * nr, nr), nr)
        by_row = pre_grad.reshape(nr, cells, pre_grad.shape[1])
        ends[0, here, :] = by_row[:, 0, :].astype(f32)
        ends[1, here, :] = by_row[:, cells - 1, :].astype(f32)
        acc_in[...] += dot(xhat_t[:, flat], pre_grad)
        return carry

    lax.fori_loop(0, rows // nr, pull, 0)
    ends_copy.wait()
    by_hidden = acc_act[...].astype(bf16)
    out_sum = dot(by_hidden, head_t_ref[...])
    head_sum = (acc_head[...] + dot(w_out_t_ref[...], by_hidden)).T
    edges = []
    for k in range(2):
        gained = dot(ends[k].astype(bf16), w_in_t_ref[...]) * gain_ref[...]
        xhat, inv = ends_ref[2 * k], ends_ref[2 * k + 1]
        edges.append(inv * (gained - xhat * jnp.mean(gained * xhat, axis=-1, keepdims=True)))
    for core in range(2):

        @pl.when(core_ref[0] == core)
        def _(core=core):
            put_chunks(keep_ref, core, acc_in, out_sum, head_sum)
            put_chunks(send_ref, 1 - core, acc_in, out_sum, head_sum)
            outer_ref[...] = edges[core].astype(bf16)
            put_edge(send_ref, edges[1 - core])

    for k in range(rows // nr):
        q_copy(k).wait()


def put_chunks(ref, half, *accs):
    for p, acc in enumerate(accs):
        down = acc.shape[0] // 8
        across = acc.shape[1] // 256
        for j in range(across):
            at = 128 * (half * across + j)
            tiles = acc[:, at : at + 128].reshape(down, 8, 128)
            ref[down * j : down * (j + 1), 8 * p : 8 * p + 8, :] = tiles.astype(ref.dtype)
        if down * across < ref.shape[0]:
            rest = ref.shape[0] - down * across
            ref[down * across :, 8 * p : 8 * p + 8, :] = jnp.zeros((rest, 8, 128), ref.dtype)


def edge_tiles(shape):
    first = 16
    return [(first + k, 8 * (k % (shape[0] // 8)), 128 * (k // (shape[0] // 8))) for k in range(shape[0] * shape[1] // 1024)]


def put_edge(ref, edge):
    for chunk, row, lane in edge_tiles(edge.shape):
        ref[chunk, 16:24, :] = edge[row : row + 8, lane : lane + 128].astype(ref.dtype)


def take_chunks(halves, part, shape):
    down = shape[0] // 8
    across = shape[1] // 256
    return jnp.concatenate(
        [
            half[down * j : down * (j + 1), 8 * part : 8 * part + 8, :].reshape(shape[0], 128)
            for half in halves
            for j in range(across)
        ],
        axis=1,
    )


def decode(core, rows, got, shown, head_t, joint, w_out_t, w_in_t, gain, ends, slope, act_t, xhat_t, lat_t, chunks):
    nrow, two_cells, nv = shown.shape
    cells = two_cells // 2
    ch = head_t.shape[1]
    hid = w_out_t.shape[1]
    n = nrow * cells
    blocks = got.shape[0]
    dma = pltpu.SemaphoreType.DMA
    scalars = pl.BlockSpec(memory_space=pltpu.SMEM)
    return pl.pallas_call(
        decode_kernel,
        out_shape=(
            pltpu.HBM((n, 2 * nv), bf16),
            jax.ShapeDtypeStruct((chunks, 24, 128), f32),
            jax.ShapeDtypeStruct((chunks, 24, 128), bf16),
            jax.ShapeDtypeStruct((nrow, ch), bf16),
        ),
        in_specs=[scalars] * 2 + [OUTSIDE] * 2 + [INSIDE] * 5 + [OUTSIDE] * 5,
        out_specs=(OUTSIDE,) + (INSIDE,) * 3,
        scratch_shapes=[pltpu.VMEM(x.shape, bf16) for x in (got, shown, slope, act_t, xhat_t, lat_t)]
        + [
            pltpu.VMEM((n, 2 * nv), bf16),
            pltpu.VMEM(ends.shape, f32),
            pltpu.VMEM((2, nrow, hid), f32),
            pltpu.VMEM((nrow, cells, 2 * nv), f32),
            pltpu.VMEM((ch, nv), f32),
            pltpu.VMEM((ch, hid), f32),
            pltpu.VMEM((hid, nv), f32),
            dma((blocks // BLOCKS_STEP,)),
            dma((blocks,)),
            dma((4, nrow // PULL_ROWS)),
            dma((nrow // PULL_ROWS,)),
            dma((1,)),
        ],
        compiler_params=params(),
        cost_estimate=cost(10 * n * ch * hid, 24 * 2**20),
        name="decode",
    )(core, rows, *in_hbm(got, shown), head_t, joint, w_out_t, w_in_t, gain, *in_hbm(ends, slope, act_t, xhat_t, lat_t))


def backward_kernel(
    left_ref, right_ref, gain_ref, w_in_t_ref, joint_ref, head_t_ref, q_ref, slope_ref, xhat_ref, *rest
):
    out_ref = rest[-1]
    rows, cells, ch = out_ref.shape
    nv = head_t_ref.shape[0]
    pre_grad = (dot(q_ref[:, nv:], joint_ref[...]) * slope_ref[...].astype(f32)).astype(bf16)
    both = dot(q_ref[:, :nv], head_t_ref[...]).reshape(rows, cells, ch)
    gained = dot(pre_grad, w_in_t_ref[...]) * gain_ref[...]
    xhat = xhat_ref[...].astype(f32)
    summed_grad = gained - xhat * jnp.mean(gained * xhat, axis=-1, keepdims=True)
    out_ref[...] = both + mixed(summed_grad.reshape(rows, cells, ch), left_ref[...], right_ref[...])


def backward(left, right, gain, w_in_t, joint, head_t, q, inv_slope, xhat, begin, end, *before):
    rows, ch = left.shape[0], left.shape[2]
    cells = xhat.shape[0] // rows
    nv, hid = joint.shape
    nr = BACK_ROWS
    step = nr * cells
    base = begin // nr
    edge = pl.BlockSpec((nr, 1, ch), lambda i: (i + base, 0, 0))
    whole = pl.BlockSpec((nr, cells, ch), lambda i: (i + base, 0, 0))
    share = (end - begin) * cells
    return pl.pallas_call(
        backward_kernel,
        grid=((end - begin) // nr,),
        out_shape=pltpu.HBM((rows, cells, ch), f32),
        in_specs=[
            edge,
            edge,
            pl.BlockSpec((1, ch), lambda i: (0, 0)),
            pl.BlockSpec((hid, ch), lambda i: (0, 0)),
            pl.BlockSpec((nv, hid), lambda i: (0, 0)),
            pl.BlockSpec((nv, ch), lambda i: (0, 0)),
            pl.BlockSpec((step, 2 * nv), lambda i: (i + base, 0)),
            pl.BlockSpec((step, hid), lambda i: (i + base, 0)),
            pl.BlockSpec((step, ch), lambda i: (i + base, 0)),
        ]
        + [OUTSIDE] * len(before),
        out_specs=whole,
        input_output_aliases={9: 0} if before else {},
        compiler_params=params(),
        cost_estimate=cost(4 * share * ch * hid, 3584 * share),
        name="backward",
    )(left, right, gain, w_in_t, joint, head_t, *in_hbm(q, inv_slope, xhat, *before))


def edge_kernel(core_ref, outer_ref, grad_ref, out_ref):
    block = grad_ref[...]
    place = lax.broadcasted_iota(jnp.int32, block.shape, 1)
    out_ref[...] = block + jnp.where(place == core_ref[0] * (block.shape[1] - 1), 0.5 * outer_ref[...].astype(f32), 0.0)


def add_outer(core, outer, grad):
    rows, cells, ch = grad.shape
    ends = pl.BlockSpec((rows, 8, ch), lambda i, core: (0, core[0] * (cells // 8 - 1), 0))
    return pl.pallas_call(
        edge_kernel,
        grid_spec=pltpu.PrefetchScalarGridSpec(
            num_scalar_prefetch=1,
            grid=(1,),
            in_specs=[pl.BlockSpec((rows, 1, ch), lambda i, core: (0, 0, 0)), ends],
            out_specs=ends,
        ),
        out_shape=pltpu.HBM(grad.shape, f32),
        input_output_aliases={2: 0},
        compiler_params=params(),
        cost_estimate=cost(rows * 8 * ch, 2**19),
        name="edge",
    )(core, outer, *in_hbm(grad))


def total_kernel(got_ref, out_ref):
    total = jnp.sum(got_ref[...].astype(f32), axis=0, keepdims=True).astype(bf16)
    out_ref[...] = jnp.broadcast_to(total, out_ref.shape)


def total(got):
    return pl.pallas_call(
        total_kernel,
        out_shape=jax.ShapeDtypeStruct(got.shape, bf16),
        compiler_params=params(),
        cost_estimate=cost(got.size, 2 * got.size * 2),
        name="total",
    )(got)


def pair_kernel(keep_ref, came_ref, out_ref, edge_ref):
    out_ref[...] = (keep_ref[...] + came_ref[...].astype(f32)).astype(bf16)
    for chunk, row, lane in edge_tiles(edge_ref.shape):
        edge_ref[row : row + 8, lane : lane + 128] = came_ref[chunk, 16:24, :].astype(f32)


def pair(keep, came, edge):
    return pl.pallas_call(
        pair_kernel,
        out_shape=(jax.ShapeDtypeStruct(keep.shape, bf16), jax.ShapeDtypeStruct(edge.shape, f32)),
        compiler_params=params(),
        cost_estimate=cost(keep.size, 8 * keep.size),
        name="pair",
    )(keep, came)


def finish_kernel(core_ref, mine_ref, other_ref, gain_ref, w_in_ref, in_ref, out_ref, gain_grad_ref, head_ref, *, devices):
    share = 1.0 / devices
    for core in range(2):

        @pl.when(core_ref[0] == core)
        def _(core=core):
            pair = (mine_ref, other_ref) if core == 0 else (other_ref, mine_ref)
            halves = [ref[...].astype(f32) * share for ref in pair]
            x = take_chunks(halves, 0, in_ref.shape)
            in_ref[...] = x * gain_ref[...]
            per_channel = jnp.sum(x * w_in_ref[...].astype(f32), axis=1, keepdims=True)
            gain_grad_ref[...] = jnp.broadcast_to(per_channel, (x.shape[0], 128)).T[0:1, :]
            out_ref[...] = take_chunks(halves, 1, out_ref.shape)
            head_ref[...] = take_chunks(halves, 2, head_ref.shape[::-1]).T


def finish(core, mine, other, gain, w_in, head, devices):
    ch, hid = w_in.shape
    return pl.pallas_call(
        functools.partial(finish_kernel, devices=devices),
        out_shape=(
            jax.ShapeDtypeStruct((ch, hid), f32),
            jax.ShapeDtypeStruct((hid, ch), f32),
            jax.ShapeDtypeStruct((1, ch), f32),
            jax.ShapeDtypeStruct(head.shape, f32),
        ),
        in_specs=[pl.BlockSpec(memory_space=pltpu.SMEM)] + [INSIDE] * 4,
        out_specs=(INSIDE,) * 4,
        compiler_params=params(),
        cost_estimate=cost(4 * ch * hid, 3 * 2**20),
        name="finish",
    )(core, mine, other, gain.reshape(ch, 1), w_in)


LON = ("chip", "core")


def from_sides(first, last):
    count = lax.axis_size("chip") * lax.axis_size("core")
    left = lax.ppermute(last, LON, [(i, (i + 1) % count) for i in range(count)])
    right = lax.ppermute(first, LON, [((i + 1) % count, i) for i in range(count)])
    return left, right


def body(latent, row_index, weights, slots, counts, targets, gain, w_in, w_out, head):
    chips = ("band", "chip")
    swap = [(0, 1), (1, 0)]
    groups = lax.axis_size("band") * lax.axis_size("chip")
    core = lax.axis_index("core").astype(jnp.int32).reshape(1)
    cells = latent.shape[1]
    packed = pack(weights, targets, slots, counts)
    left, right = from_sides(latent[:, 0:1, :], latent[:, cells - 1 : cells, :])
    packed, left, right = lax.optimization_barrier((packed, left, right))
    got = lax.all_to_all(packed, LON, 0, 0, tiled=True)
    left, right = left.astype(f32), right.astype(f32)
    gain_row = gain.reshape(1, -1)
    w_out_t = w_out.T
    w_in_t = w_in.T
    shown, lat_t, slope, act_t, xhat_t, xhat, inv_slope, ends = forward(
        latent, left, right, gain_row, w_in, w_out, head
    )
    head_t = head.T
    joint = dot(head_t, w_out_t).astype(bf16)
    q, keep, send, outer = decode(
        core, row_index, got, shown, head_t, joint, w_out_t, w_in_t, gain_row, ends, slope, act_t, xhat_t, lat_t, groups
    )
    lons = 2 * lax.axis_size("chip")
    outer = lax.ppermute(outer, LON, [(i, (i + (1 if i % 2 else -1)) % lons) for i in range(lons)])
    summed, inner = pair(keep, lax.ppermute(send, "core", swap), outer)
    parts = lax.all_to_all(summed, chips, 0, 0, tiled=True)
    grad_left = jnp.where(core == 1, inner, 0.0)[:, None, :]
    grad_right = jnp.where(core == 0, inner, 0.0)[:, None, :]
    rest = (grad_left, grad_right, gain_row, w_in_t, joint, head_t, q, inv_slope, xhat)
    rows = latent.shape[0]
    grad = backward(*rest, 0, rows // 2)
    parts, grad, outer = lax.optimization_barrier((parts, grad, outer))
    outer = outer.astype(f32)[:, None, :]
    mine = lax.all_to_all(total(parts), chips, 0, 0, tiled=True)
    grad = add_outer(core, outer, backward(*rest, rows // 2, rows, grad))
    mine, grad = lax.optimization_barrier((mine, grad))
    other = lax.ppermute(mine, "core", swap)
    grad_in, grad_out, grad_gain, grad_head = finish(core, mine, other, gain, w_in, head, 2 * groups)
    return grad, grad_in, grad_out, grad_gain.reshape(-1), grad_head


def solution(mesh):
    bands, lons = mesh.devices.shape
    by_core = jax.sharding.Mesh(mesh.devices.reshape(bands, lons // 2, 2), ("band", "chip", "core"))
    every = ("band", "chip", "core")
    return jax.shard_map(
        body,
        mesh=by_core,
        in_specs=(
            P("band", LON, None),
            P("band", LON, None),
            P(every, None, None),
            P(every, None),
            P(every),
            P(every, None, None),
            P(),
            P(),
            P(),
            P(),
        ),
        out_specs=(P("band", LON, None), P(), P(), P(), P()),
        check_vma=False,
    )
```

```python
import functools
import math

import jax
import jax.numpy as jnp
from jax import lax
from jax.experimental import pallas as pl
from jax.experimental.pallas import tpu as pltpu
from jax.sharding import PartitionSpec as P

WINDOW_SLOTS = 7
NORM_EPS = 1e-05
ROWS_STEP = 8
BLOCKS_STEP = 8
PULL_ROWS = 8
PACK_CHUNKS = 4
BACK_ROWS = 8
AHEAD = 3
LATER_AT = 0
META = 8

f32 = jnp.float32
bf16 = jnp.bfloat16
INSIDE = pl.BlockSpec(memory_space=pltpu.VMEM)
OUTSIDE = pl.BlockSpec(memory_space=pltpu.HBM)


def dot(a, b):
    return jnp.dot(a, b, preferred_element_type=f32)


def dot_t(a, b):
    return lax.dot_general(a, b, (((0,), (0,)), ((), ())), preferred_element_type=f32)


def params(mib=48):
    return pltpu.CompilerParams(vmem_limit_bytes=mib * 2**20)


def in_hbm(*arrays):
    return [pltpu.with_memory_space_constraint(x, pltpu.HBM) for x in arrays]


def cost(flops, nbytes, trans=0):
    return pl.CostEstimate(flops=flops, bytes_accessed=nbytes, transcendentals=trans)


def pack_kernel(
    w_hbm, t_hbm, slot_hbm, count_hbm, lat_hbm, out_hbm, first_ref, last_ref,
    buf, slots, counts, ends, small_sems, in_sems, out_sems,
):
    blocks, obs = slots.shape
    nv = t_hbm.shape[1]
    n = blocks // PACK_CHUNKS
    small = [
        pltpu.make_async_copy(slot_hbm, slots, small_sems.at[0]),
        pltpu.make_async_copy(count_hbm, counts, small_sems.at[1]),
        pltpu.make_async_copy(lat_hbm.at[:, pl.ds(0, 8), :], ends.at[0], small_sems.at[2]),
        pltpu.make_async_copy(lat_hbm.at[:, pl.ds(lat_hbm.shape[1] - 8, 8), :], ends.at[1], small_sems.at[3]),
    ]
    arrive, leave = [], []
    for c in range(PACK_CHUNKS):
        here = pl.ds(c * n, n)
        arrive.append(
            (
                pltpu.make_async_copy(w_hbm.at[here], buf.at[here, pl.ds(0, obs), :], in_sems.at[2 * c]),
                pltpu.make_async_copy(t_hbm.at[here], buf.at[here, pl.ds(obs, nv), :], in_sems.at[2 * c + 1]),
            )
        )
        leave.append(pltpu.make_async_copy(buf.at[here], out_hbm.at[here], out_sems.at[c]))
    for c in small:
        c.start()
    for pair in arrive:
        for c in pair:
            c.start()
    for c in small:
        c.wait()
    coef = slots[...].astype(f32) / (WINDOW_SLOTS - 1)
    lane = lax.broadcasted_iota(jnp.int32, (META, obs), 1)
    row = lax.broadcasted_iota(jnp.int32, (META, obs), 0)
    for b in range(blocks):
        live = jnp.where(lane < counts[b], 1.0, 0.0)
        buf[b, obs + nv : obs + nv + META, :] = jnp.where(row == 0, coef[b : b + 1, :], live).astype(bf16)
    first_ref[...] = ends[0].astype(f32)[:, 0, :].astype(bf16)
    last_ref[...] = ends[1].astype(f32)[:, 7, :].astype(bf16)
    for pair, out in zip(arrive, leave):
        for c in pair:
            c.wait()
        out.start()
    for c in leave:
        c.wait()


def pack(weights, targets, slots, counts, latent):
    blocks, obs, cells = weights.shape
    shape = (blocks, 2 * obs + META, cells)
    rows, _, ch = latent.shape
    edge = jax.ShapeDtypeStruct((rows, ch), bf16)
    dma = pltpu.SemaphoreType.DMA
    return pl.pallas_call(
        pack_kernel,
        out_shape=(pltpu.HBM(shape, bf16), edge, edge),
        in_specs=[OUTSIDE] * 5,
        out_specs=(OUTSIDE, INSIDE, INSIDE),
        scratch_shapes=[
            pltpu.VMEM(shape, bf16),
            pltpu.VMEM(slots.shape, jnp.int32),
            pltpu.SMEM(counts.shape, jnp.int32),
            pltpu.VMEM((2, rows, 8, ch), bf16),
            dma((4,)),
            dma((2 * PACK_CHUNKS,)),
            dma((PACK_CHUNKS,)),
        ],
        compiler_params=params(),
        cost_estimate=cost(1, 4 * 2**20),
        name="pack",
    )(*in_hbm(weights, targets, slots, counts, latent))


def mixed(x, left, right):
    cells = x.shape[1]
    place = lax.broadcasted_iota(jnp.int32, x.shape, 1)
    from_left = jnp.where(place == 0, left, pltpu.roll(x, 1, 1))
    from_right = jnp.where(place == cells - 1, right, pltpu.roll(x, cells - 1, 1))
    return x + 0.5 * (from_left + from_right)


def normalized(lat, left, right):
    summed = mixed(lat, left, right)
    inv = lax.rsqrt(jnp.mean(summed * summed, axis=-1, keepdims=True) + NORM_EPS)
    return summed * inv, inv


def forward_kernel(
    lat_ref, left_ref, right_ref, gain_ref, w_in_ref, w_out_ref, head_ref,
    shown_ref, lat_t_ref, slope_ref, act_t_ref, xhat_t_ref, xhat_ref, inv_slope_ref, ends_ref,
):
    rows, cells, ch = lat_ref.shape
    lat_b = lat_ref[...]
    lat = lat_b.astype(f32)
    xhat3, inv3 = normalized(lat, left_ref[...], right_ref[...])
    for k, cell in enumerate((0, cells - 1)):
        ends_ref[2 * k] = xhat3[:, cell, :]
        ends_ref[2 * k + 1] = jnp.broadcast_to(inv3[:, cell, :], (rows, ch))
    xhat = xhat3.reshape(rows * cells, ch)
    pre = dot((xhat * gain_ref[...]).astype(bf16), w_in_ref[...])
    sig = jax.nn.sigmoid(pre)
    act = pre * sig
    act_b = act.astype(bf16)
    slope = sig * (1.0 + pre * (1.0 - sig))
    slope_ref[...] = slope.astype(bf16)
    inv_slope_ref[...] = (slope * inv3.reshape(rows * cells, 1)).astype(bf16)
    new = (lat.reshape(rows * cells, ch) + dot(act_b, w_out_ref[...])).astype(bf16)
    old = lat_b.reshape(rows * cells, ch)
    for k, tile in enumerate((old, new)):
        shown = dot(tile, head_ref[...]).astype(bf16)
        shown_ref[:, k * cells : (k + 1) * cells, :] = shown.reshape(rows, cells, shown.shape[1])
    lat_t_ref[...] = old.T
    xhat_b = xhat.astype(bf16)
    xhat_ref[...] = xhat_b
    act_t_ref[...] = act_b.T
    xhat_t_ref[...] = xhat_b.T


def forward(latent, left, right, gain, w_in, w_out, head):
    rows, cells, ch = latent.shape
    hid = w_in.shape[1]
    nv = head.shape[1]
    n = rows * cells
    step = ROWS_STEP * cells
    return pl.pallas_call(
        forward_kernel,
        grid=(rows // ROWS_STEP,),
        out_shape=(
            pltpu.HBM((rows, 2 * cells, nv), bf16),
            pltpu.HBM((ch, n), bf16),
            pltpu.HBM((n, hid), bf16),
            pltpu.HBM((hid, n), bf16),
            pltpu.HBM((ch, n), bf16),
            pltpu.HBM((n, ch), bf16),
            pltpu.HBM((n, hid), bf16),
            pltpu.HBM((4, rows, ch), f32),
        ),
        in_specs=[
            pl.BlockSpec((ROWS_STEP, cells, ch), lambda i: (i, 0, 0)),
            pl.BlockSpec((ROWS_STEP, 1, ch), lambda i: (i, 0, 0)),
            pl.BlockSpec((ROWS_STEP, 1, ch), lambda i: (i, 0, 0)),
            pl.BlockSpec((1, ch), lambda i: (0, 0)),
            pl.BlockSpec((ch, hid), lambda i: (0, 0)),
            pl.BlockSpec((hid, ch), lambda i: (0, 0)),
            pl.BlockSpec((ch, nv), lambda i: (0, 0)),
        ],
        out_specs=(
            pl.BlockSpec((ROWS_STEP, 2 * cells, nv), lambda i: (i, 0, 0)),
            pl.BlockSpec((ch, step), lambda i: (0, i)),
            pl.BlockSpec((step, hid), lambda i: (i, 0)),
            pl.BlockSpec((hid, step), lambda i: (0, i)),
            pl.BlockSpec((ch, step), lambda i: (0, i)),
            pl.BlockSpec((step, ch), lambda i: (i, 0)),
            pl.BlockSpec((step, hid), lambda i: (i, 0)),
            pl.BlockSpec((4, ROWS_STEP, ch), lambda i: (0, i, 0)),
        ),
        compiler_params=params(),
        cost_estimate=cost(4 * n * ch * hid, 16 * 2**20, 2 * n * hid),
        name="forward",
    )(latent, left, right, gain, w_in, w_out, head)


def decode_kernel(
    core_ref, rows_ref, got_hbm, shown_hbm, head_t_ref, joint_ref, w_out_t_ref, w_in_t_ref, gain_ref,
    ends_hbm, slope_hbm, act_t_hbm, xhat_t_hbm, lat_t_hbm,
    q_hbm, keep_ref, send_ref, outer_ref,
    got, shown, slope, act_t, xhat_t, lat_t, q_all, ends_ref, ends, acc_q, acc_head, acc_in, acc_act,
    got_sems, shown_sems, in_sems, q_sems, ends_sem,
):
    nb, nr = BLOCKS_STEP, PULL_ROWS
    blocks = got.shape[0]
    nv, ch = head_t_ref.shape
    obs = (got.shape[1] - META) // 2
    rows, cells, _ = acc_q.shape
    scale = 1.0 / math.sqrt(obs)
    step = nr * cells

    def got_copy(i):
        here = pl.ds(i * nb, nb)
        return pltpu.make_async_copy(got_hbm.at[here], got.at[here], got_sems.at[i])

    def shown_copy(b):
        return pltpu.make_async_copy(shown_hbm.at[rows_ref[0, 0, b]], shown.at[b], shown_sems.at[b])

    def q_copy(k):
        flat = pl.ds(pl.multiple_of(k * step, step), step)
        return pltpu.make_async_copy(q_all.at[flat], q_hbm.at[flat], q_sems.at[k])

    def chunk_copies(k):
        flat = pl.ds(pl.multiple_of(k * step, step), step)
        turned = ((lat_t_hbm, lat_t), (xhat_t_hbm, xhat_t), (act_t_hbm, act_t))
        return [pltpu.make_async_copy(slope_hbm.at[flat], slope.at[flat], in_sems.at[0, k])] + [
            pltpu.make_async_copy(src.at[:, flat], dst.at[:, flat], in_sems.at[1 + i, k]) for i, (src, dst) in enumerate(turned)
        ]

    def start(i):
        got_copy(i).start()
        for j in range(nb):
            shown_copy(i * nb + j).start()

    for i in range(AHEAD):
        start(i)
    ends_copy = pltpu.make_async_copy(ends_hbm, ends_ref, ends_sem.at[0])
    ends_copy.start()
    for acc in (acc_q, acc_head, acc_in, acc_act):
        acc[...] = jnp.zeros_like(acc)

    def observe(i, carry):
        first = i * nb
        got_copy(i).wait()
        for j in range(nb):
            shown_copy(first + j).wait()

        @pl.when(i + AHEAD < blocks // nb)
        def _():
            start(i + AHEAD)

        @pl.when(i == LATER_AT)
        def _():
            for k in range(rows // nr):
                for c in chunk_copies(k):
                    c.start()

        places = [rows_ref[0, 0, first + j] for j in range(nb)]
        meta = jnp.concatenate([got[first + j, 2 * obs : 2 * obs + META, :].astype(f32) for j in range(nb)], axis=0).T
        preds = []
        for j in range(nb):
            t = meta[:, META * j : META * j + 1]
            w = got[first + j, 0:obs, :]
            w_new = w * jnp.broadcast_to(t, w.shape).astype(bf16)
            preds.append(dot(jnp.concatenate([w - w_new, w_new], axis=1), shown[first + j]))
        grads = []
        for j in range(nb):
            t, live = meta[:, META * j : META * j + 1], meta[:, META * j + 1 : META * j + 2]
            residual = jnp.where(live > 0.5, preds[j] - got[first + j, obs : 2 * obs, :].astype(f32), 0.0) * scale
            grads.append(jnp.concatenate([residual.astype(bf16), (residual * t).astype(bf16)], axis=1))
        pulled = [dot_t(got[first + j, 0:obs, :], grads[j]) for j in range(nb)]
        for j in range(nb):
            acc_q[places[j]] += pulled[j]
        return carry

    lax.fori_loop(0, blocks // nb, observe, 0)
    def pull(k, carry):
        flat = pl.ds(pl.multiple_of(k * step, step), step)
        for c in chunk_copies(k):
            c.wait()
        q = acc_q[pl.ds(k * nr, nr)].reshape(step, 2 * nv).astype(bf16)
        q_all[flat, :] = q
        q_copy(k).start()
        pre_grad = (dot(q[:, nv:], joint_ref[...]) * slope[flat, :].astype(f32)).astype(bf16)
        acc_act[...] += dot(act_t[:, flat], q[:, nv:])
        acc_head[...] += dot(lat_t[:, flat], q[:, :nv])
        here = pl.ds(pl.multiple_of(k * nr, nr), nr)
        by_row = pre_grad.reshape(nr, cells, pre_grad.shape[1])
        ends[0, here, :] = by_row[:, 0, :].astype(f32)
        ends[1, here, :] = by_row[:, cells - 1, :].astype(f32)
        acc_in[...] += dot(xhat_t[:, flat], pre_grad)
        return carry

    lax.fori_loop(0, rows // nr, pull, 0)
    ends_copy.wait()
    by_hidden = acc_act[...].astype(bf16)
    out_sum = dot(by_hidden, head_t_ref[...])
    head_sum = (acc_head[...] + dot(w_out_t_ref[...], by_hidden)).T
    edges = []
    for k in range(2):
        gained = dot(ends[k].astype(bf16), w_in_t_ref[...]) * gain_ref[...]
        xhat, inv = ends_ref[2 * k], ends_ref[2 * k + 1]
        edges.append(inv * (gained - xhat * jnp.mean(gained * xhat, axis=-1, keepdims=True)))
    for core in range(2):

        @pl.when(core_ref[0] == core)
        def _(core=core):
            put_chunks(keep_ref, core, acc_in, out_sum, head_sum)
            put_chunks(send_ref, 1 - core, acc_in, out_sum, head_sum)
            outer_ref[...] = edges[core].astype(bf16)
            put_edge(send_ref, edges[1 - core])

    for k in range(rows // nr):
        q_copy(k).wait()


def put_chunks(ref, half, *accs):
    for p, acc in enumerate(accs):
        down = acc.shape[0] // 8
        across = acc.shape[1] // 256
        for j in range(across):
            at = 128 * (half * across + j)
            tiles = acc[:, at : at + 128].reshape(down, 8, 128)
            ref[down * j : down * (j + 1), 8 * p : 8 * p + 8, :] = tiles.astype(ref.dtype)
        if down * across < ref.shape[0]:
            rest = ref.shape[0] - down * across
            ref[down * across :, 8 * p : 8 * p + 8, :] = jnp.zeros((rest, 8, 128), ref.dtype)


def edge_tiles(shape):
    first = 16
    return [(first + k, 8 * (k % (shape[0] // 8)), 128 * (k // (shape[0] // 8))) for k in range(shape[0] * shape[1] // 1024)]


def put_edge(ref, edge):
    for chunk, row, lane in edge_tiles(edge.shape):
        ref[chunk, 16:24, :] = edge[row : row + 8, lane : lane + 128].astype(ref.dtype)


def take_chunks(halves, part, shape):
    down = shape[0] // 8
    across = shape[1] // 256
    return jnp.concatenate(
        [
            half[down * j : down * (j + 1), 8 * part : 8 * part + 8, :].reshape(shape[0], 128)
            for half in halves
            for j in range(across)
        ],
        axis=1,
    )


def decode(core, rows, got, shown, head_t, joint, w_out_t, w_in_t, gain, ends, slope, act_t, xhat_t, lat_t, chunks):
    nrow, two_cells, nv = shown.shape
    cells = two_cells // 2
    ch = head_t.shape[1]
    hid = w_out_t.shape[1]
    n = nrow * cells
    blocks = got.shape[0]
    dma = pltpu.SemaphoreType.DMA
    scalars = pl.BlockSpec(memory_space=pltpu.SMEM)
    return pl.pallas_call(
        decode_kernel,
        out_shape=(
            pltpu.HBM((n, 2 * nv), bf16),
            jax.ShapeDtypeStruct((chunks, 24, 128), f32),
            jax.ShapeDtypeStruct((chunks, 24, 128), bf16),
            jax.ShapeDtypeStruct((nrow, ch), bf16),
        ),
        in_specs=[scalars] * 2 + [OUTSIDE] * 2 + [INSIDE] * 5 + [OUTSIDE] * 5,
        out_specs=(OUTSIDE,) + (INSIDE,) * 3,
        scratch_shapes=[pltpu.VMEM(x.shape, bf16) for x in (got, shown, slope, act_t, xhat_t, lat_t)]
        + [
            pltpu.VMEM((n, 2 * nv), bf16),
            pltpu.VMEM(ends.shape, f32),
            pltpu.VMEM((2, nrow, hid), f32),
            pltpu.VMEM((nrow, cells, 2 * nv), f32),
            pltpu.VMEM((ch, nv), f32),
            pltpu.VMEM((ch, hid), f32),
            pltpu.VMEM((hid, nv), f32),
            dma((blocks // BLOCKS_STEP,)),
            dma((blocks,)),
            dma((4, nrow // PULL_ROWS)),
            dma((nrow // PULL_ROWS,)),
            dma((1,)),
        ],
        compiler_params=params(),
        cost_estimate=cost(10 * n * ch * hid, 24 * 2**20),
        name="decode",
    )(core, rows, *in_hbm(got, shown), head_t, joint, w_out_t, w_in_t, gain, *in_hbm(ends, slope, act_t, xhat_t, lat_t))


def backward_kernel(
    left_ref, right_ref, gain_ref, w_in_t_ref, joint_ref, head_t_ref, q_ref, slope_ref, xhat_ref, *rest
):
    out_ref = rest[-1]
    rows, cells, ch = out_ref.shape
    nv = head_t_ref.shape[0]
    pre_grad = (dot(q_ref[:, nv:], joint_ref[...]) * slope_ref[...].astype(f32)).astype(bf16)
    both = dot(q_ref[:, :nv], head_t_ref[...]).reshape(rows, cells, ch)
    gained = dot(pre_grad, w_in_t_ref[...]) * gain_ref[...]
    xhat = xhat_ref[...].astype(f32)
    summed_grad = gained - xhat * jnp.mean(gained * xhat, axis=-1, keepdims=True)
    out_ref[...] = both + mixed(summed_grad.reshape(rows, cells, ch), left_ref[...], right_ref[...])


def backward(left, right, gain, w_in_t, joint, head_t, q, inv_slope, xhat, begin, end, *before):
    rows, ch = left.shape[0], left.shape[2]
    cells = xhat.shape[0] // rows
    nv, hid = joint.shape
    nr = BACK_ROWS
    step = nr * cells
    base = begin // nr
    edge = pl.BlockSpec((nr, 1, ch), lambda i: (i + base, 0, 0))
    whole = pl.BlockSpec((nr, cells, ch), lambda i: (i + base, 0, 0))
    share = (end - begin) * cells
    return pl.pallas_call(
        backward_kernel,
        grid=((end - begin) // nr,),
        out_shape=pltpu.HBM((rows, cells, ch), f32),
        in_specs=[
            edge,
            edge,
            pl.BlockSpec((1, ch), lambda i: (0, 0)),
            pl.BlockSpec((hid, ch), lambda i: (0, 0)),
            pl.BlockSpec((nv, hid), lambda i: (0, 0)),
            pl.BlockSpec((nv, ch), lambda i: (0, 0)),
            pl.BlockSpec((step, 2 * nv), lambda i: (i + base, 0)),
            pl.BlockSpec((step, hid), lambda i: (i + base, 0)),
            pl.BlockSpec((step, ch), lambda i: (i + base, 0)),
        ]
        + [OUTSIDE] * len(before),
        out_specs=whole,
        input_output_aliases={9: 0} if before else {},
        compiler_params=params(),
        cost_estimate=cost(4 * share * ch * hid, 3584 * share),
        name="backward",
    )(left, right, gain, w_in_t, joint, head_t, *in_hbm(q, inv_slope, xhat, *before))


def edge_kernel(core_ref, outer_ref, grad_ref, out_ref):
    block = grad_ref[...]
    place = lax.broadcasted_iota(jnp.int32, block.shape, 1)
    out_ref[...] = block + jnp.where(place == core_ref[0] * (block.shape[1] - 1), 0.5 * outer_ref[...].astype(f32), 0.0)


def add_outer(core, outer, grad):
    rows, cells, ch = grad.shape
    ends = pl.BlockSpec((rows, 8, ch), lambda i, core: (0, core[0] * (cells // 8 - 1), 0))
    return pl.pallas_call(
        edge_kernel,
        grid_spec=pltpu.PrefetchScalarGridSpec(
            num_scalar_prefetch=1,
            grid=(1,),
            in_specs=[pl.BlockSpec((rows, 1, ch), lambda i, core: (0, 0, 0)), ends],
            out_specs=ends,
        ),
        out_shape=pltpu.HBM(grad.shape, f32),
        input_output_aliases={2: 0},
        compiler_params=params(),
        cost_estimate=cost(rows * 8 * ch, 2**19),
        name="edge",
    )(core, outer, *in_hbm(grad))


def total_kernel(got_ref, out_ref):
    total = jnp.sum(got_ref[...].astype(f32), axis=0, keepdims=True).astype(bf16)
    out_ref[...] = jnp.broadcast_to(total, out_ref.shape)


def total(got):
    return pl.pallas_call(
        total_kernel,
        out_shape=jax.ShapeDtypeStruct(got.shape, bf16),
        compiler_params=params(),
        cost_estimate=cost(got.size, 2 * got.size * 2),
        name="total",
    )(got)


def pair_kernel(keep_ref, came_ref, out_ref, edge_ref):
    out_ref[...] = (keep_ref[...] + came_ref[...].astype(f32)).astype(bf16)
    for chunk, row, lane in edge_tiles(edge_ref.shape):
        edge_ref[row : row + 8, lane : lane + 128] = came_ref[chunk, 16:24, :].astype(f32)


def pair(keep, came, edge):
    return pl.pallas_call(
        pair_kernel,
        out_shape=(jax.ShapeDtypeStruct(keep.shape, bf16), jax.ShapeDtypeStruct(edge.shape, f32)),
        compiler_params=params(),
        cost_estimate=cost(keep.size, 8 * keep.size),
        name="pair",
    )(keep, came)


def finish_kernel(core_ref, mine_ref, other_ref, gain_ref, w_in_ref, in_ref, out_ref, gain_grad_ref, head_ref, *, devices):
    share = 1.0 / devices
    for core in range(2):

        @pl.when(core_ref[0] == core)
        def _(core=core):
            pair = (mine_ref, other_ref) if core == 0 else (other_ref, mine_ref)
            halves = [ref[...].astype(f32) * share for ref in pair]
            x = take_chunks(halves, 0, in_ref.shape)
            in_ref[...] = x * gain_ref[...]
            per_channel = jnp.sum(x * w_in_ref[...].astype(f32), axis=1, keepdims=True)
            gain_grad_ref[...] = jnp.broadcast_to(per_channel, (x.shape[0], 128)).T[0:1, :]
            out_ref[...] = take_chunks(halves, 1, out_ref.shape)
            head_ref[...] = take_chunks(halves, 2, head_ref.shape[::-1]).T


def finish(core, mine, other, gain, w_in, head, devices):
    ch, hid = w_in.shape
    return pl.pallas_call(
        functools.partial(finish_kernel, devices=devices),
        out_shape=(
            jax.ShapeDtypeStruct((ch, hid), f32),
            jax.ShapeDtypeStruct((hid, ch), f32),
            jax.ShapeDtypeStruct((1, ch), f32),
            jax.ShapeDtypeStruct(head.shape, f32),
        ),
        in_specs=[pl.BlockSpec(memory_space=pltpu.SMEM)] + [INSIDE] * 4,
        out_specs=(INSIDE,) * 4,
        compiler_params=params(),
        cost_estimate=cost(4 * ch * hid, 3 * 2**20),
        name="finish",
    )(core, mine, other, gain.reshape(ch, 1), w_in)


LON = ("chip", "core")


def from_sides(first, last):
    count = lax.axis_size("chip") * lax.axis_size("core")
    left = lax.ppermute(last, LON, [(i, (i + 1) % count) for i in range(count)])
    right = lax.ppermute(first, LON, [((i + 1) % count, i) for i in range(count)])
    return left, right


def body(latent, row_index, weights, slots, counts, targets, gain, w_in, w_out, head):
    chips = ("band", "chip")
    swap = [(0, 1), (1, 0)]
    groups = lax.axis_size("band") * lax.axis_size("chip")
    core = lax.axis_index("core").astype(jnp.int32).reshape(1)
    packed, first, last = pack(weights, targets, slots, counts, latent)
    left, right = from_sides(first, last)
    packed, left, right = lax.optimization_barrier((packed, left, right))
    got = lax.all_to_all(packed, LON, 0, 0, tiled=True)
    left, right = left.astype(f32)[:, None, :], right.astype(f32)[:, None, :]
    gain_row = gain.reshape(1, -1)
    w_out_t = w_out.T
    w_in_t = w_in.T
    shown, lat_t, slope, act_t, xhat_t, xhat, inv_slope, ends = forward(
        latent, left, right, gain_row, w_in, w_out, head
    )
    head_t = head.T
    joint = dot(head_t, w_out_t).astype(bf16)
    q, keep, send, outer = decode(
        core, row_index, got, shown, head_t, joint, w_out_t, w_in_t, gain_row, ends, slope, act_t, xhat_t, lat_t, groups
    )
    lons = 2 * lax.axis_size("chip")
    outer = lax.ppermute(outer, LON, [(i, (i + (1 if i % 2 else -1)) % lons) for i in range(lons)])
    summed, inner = pair(keep, lax.ppermute(send, "core", swap), outer)
    parts = lax.all_to_all(summed, chips, 0, 0, tiled=True)
    grad_left = jnp.where(core == 1, inner, 0.0)[:, None, :]
    grad_right = jnp.where(core == 0, inner, 0.0)[:, None, :]
    rest = (grad_left, grad_right, gain_row, w_in_t, joint, head_t, q, inv_slope, xhat)
    rows = latent.shape[0]
    grad = backward(*rest, 0, rows // 2)
    parts, grad, outer = lax.optimization_barrier((parts, grad, outer))
    outer = outer.astype(f32)[:, None, :]
    mine = lax.all_to_all(total(parts), chips, 0, 0, tiled=True)
    grad = add_outer(core, outer, backward(*rest, rows // 2, rows, grad))
    mine, grad = lax.optimization_barrier((mine, grad))
    other = lax.ppermute(mine, "core", swap)
    grad_in, grad_out, grad_gain, grad_head = finish(core, mine, other, gain, w_in, head, 2 * groups)
    return grad, grad_in, grad_out, grad_gain.reshape(-1), grad_head


def solution(mesh):
    bands, lons = mesh.devices.shape
    by_core = jax.sharding.Mesh(mesh.devices.reshape(bands, lons // 2, 2), ("band", "chip", "core"))
    every = ("band", "chip", "core")
    return jax.shard_map(
        body,
        mesh=by_core,
        in_specs=(
            P("band", LON, None),
            P("band", LON, None),
            P(every, None, None),
            P(every, None),
            P(every),
            P(every, None, None),
            P(),
            P(),
            P(),
            P(),
        ),
        out_specs=(P("band", LON, None), P(), P(), P(), P()),
        check_vma=False,
    )
```
